32 devices in a mesh: ctx: 8 (over y, x, core), fsdp: 4 (over z).
Axes of the slice: x: 2, y: 2, z: 4, core: 2. Of those that a mesh axis runs over, the one named last changes fastest.
Arguments:
- tokens: bfloat16 [4, 4096, 768], P('fsdp', 'ctx'), may hold values from -6 to 6
- cotangent: bfloat16 [4, 4096, 768], P('fsdp', 'ctx'), may hold values from -6 to 6
- lengths: int32 [4, 4], P('fsdp'), may hold values from 1 to 2048, 4096 in all within a row
- dealing: int32 [4, 16], P('fsdp'), may hold values from 0 to 15, each once within a row
- qkv_weight: bfloat16 [768, 2304], P('fsdp'), may hold values from -0.21875 to 0.21875
- out_weight: bfloat16 [768, 768], P('fsdp'), may hold values from -0.21875 to 0.21875
- in_weight: bfloat16 [768, 3072], P('fsdp'), may hold values from -0.21875 to 0.21875
- back_weight: bfloat16 [3072, 768], P('fsdp'), may hold values from -0.109375 to 0.109375
- norm_gains: bfloat16 [3, 768], P(None, 'fsdp'), may hold values from 0.25 to 1.75
- shifts: bfloat16 [7, 768], P(None, 'fsdp'), may hold values from -1.796875 to 1.796875
- ffn_gain: bfloat16 [3072], P('fsdp'), may hold values from 0.25 to 1.75
- ffn_shifts: bfloat16 [2, 3072], P(None, 'fsdp'), may hold values from -1.796875 to 1.796875
Outputs:
- mixed_out: bfloat16 [4, 4096, 768], P('fsdp', 'ctx')
- input_grad: float32 [4, 4096, 768], P('fsdp', 'ctx')
- qkv_grad: float32 [768, 2304], P(('ctx', 'fsdp'))
- out_grad: float32 [768, 768], P(('ctx', 'fsdp'))
- in_grad: float32 [768, 3072], P(('ctx', 'fsdp'))
- back_grad: float32 [3072, 768], P(('ctx', 'fsdp'))
- gains_grad: float32 [3, 768], P(None, ('ctx', 'fsdp'))
- shifts_grad: float32 [7, 768], P(None, ('ctx', 'fsdp'))
- ffn_gain_grad: float32 [3072], P(('ctx', 'fsdp'))
- ffn_shifts_grad: float32 [2, 3072], P(None, ('ctx', 'fsdp'))
The draws below stay inside these ranges and needn't reach their ends.
Inputs may be any that keep to these rules, and one draw needn't show every extreme that they name: `lengths`: each row sums to 4096 and its largest entry is exactly 2048. `dealing`: each row is a permutation of the group numbers.
All inputs are finite; a program needn't handle non-finite values.
Results may differ from the reference program's by a relative error of at most 0.018.
Values may be sent and summed in bfloat16 or wider, within the bound.
No kernel may reach another device: no remote copies, remote signals or barrier semaphores. Data moves between devices by JAX's collectives and lax.ppermute only.
A program may use at most 256 MiB of HBM per device.

```python
import math
import jax
import jax.numpy as jnp
import numpy as np
from jax import lax

D = 768
H = 12
DH = 64
FF = 3072
NSEQ = 4
GROUP = 256
GROUPS = 16
STREAM = 4096
LONGEST = 2048
STREAMS = 4


def levels(stream_key, shape, cuts, least, largest):
    def one(axis_at, shards_of):
        draws = jax.random.uniform(jax.random.fold_in(jax.random.fold_in(stream_key, 6), axis_at), (shards_of,), jnp.float32, least / len(cuts), largest / len(cuts))
        return jnp.repeat(jnp.exp(draws), shape[axis_at] // shards_of).reshape((-1,) + (1,) * (len(shape) - axis_at - 1))

    level = one(*cuts[0])
    for cut in cuts[1:]:
        level = level * one(*cut)
    return level


def split_up(amount, total, bound, skew):
    loads = [(1 << 20) // math.isqrt(rank ** skew) + 1 for rank in range(2, amount + 1)]
    spare, counts = total - bound - (amount - 1), [1] * (amount - 1)
    while spare > 0:
        movable = [i for i in range(amount - 1) if counts[i] < bound]
        pool, budget = sum([loads[i] for i in movable]), spare
        for i in movable:
            addition = min(bound - counts[i], max(1, budget * loads[i] // pool), spare)
            counts[i] = counts[i] + addition
            spare = spare - addition
    return np.array([bound] + counts)


def ragged_sizes(stream_key, number_of, total, limit, slope):
    if number_of == 2:
        one = jax.random.randint(stream_key, (), max(1, total - limit), min(limit, total - 1) + 1)
        return jnp.stack([one, total - one])
    tallies = jnp.asarray(split_up(number_of, total, limit, slope), jnp.int32)
    couples = (number_of - 1) // 2
    giver, receiver = tallies[1:1 + 2 * couples:2], tallies[2:2 + 2 * couples:2]
    margin = jnp.minimum(giver - 1, limit - receiver)
    shifted = jax.random.randint(jax.random.fold_in(stream_key, 1), (couples,), 0, 1 << 20) % (margin + 1)
    tallies = tallies.at[1:1 + 2 * couples:2].set(giver - shifted).at[2:2 + 2 * couples:2].set(receiver + shifted)
    return tallies[jax.random.permutation(jax.random.fold_in(stream_key, 2), number_of)]


def gaussian(stream_key, dims, deviation, most, split=(), kind=jnp.bfloat16):
    values = deviation * jax.random.normal(stream_key, dims, jnp.float32)
    if split:
        values = values * levels(stream_key, dims, split, -0.22, 0.18)
    return jnp.clip(values, -most, most).astype(kind)


def setup_inputs(seed: int = 0) -> dict:
    streams_of = jax.random.split(jax.random.key(seed), 13)
    tokens = gaussian(streams_of[0], (STREAMS, STREAM, D), 1.0, 6.0, ((0, 4), (1, 8)))
    cotangent = gaussian(streams_of[1], (STREAMS, STREAM, D), 1.0, 6.0, ((0, 4), (1, 8)))
    lengths = jax.vmap(lambda own: ragged_sizes(own, NSEQ, STREAM, LONGEST, 2))(jax.random.split(streams_of[2], STREAMS)).reshape((STREAMS, NSEQ)).astype(jnp.int32)
    dealing = jax.vmap(lambda own: jax.random.permutation(own, GROUPS))(jax.random.split(streams_of[3], STREAMS)).reshape((STREAMS, GROUPS)).astype(jnp.int32)
    qkv_weight = gaussian(streams_of[4], (D, 3 * D), D ** -0.5, 0.21875, ((0, 4),))
    out_weight = gaussian(streams_of[5], (D, D), D ** -0.5, 0.21875, ((0, 4),))
    in_weight = gaussian(streams_of[6], (D, FF), D ** -0.5, 0.21875, ((0, 4),))
    back_weight = gaussian(streams_of[7], (FF, D), FF ** -0.5, 0.109375, ((0, 4),))
    norm_gains = jnp.clip(1.0 + 0.15 * jax.random.normal(streams_of[8], (3, D), jnp.float32), 0.25, 1.75).astype(jnp.bfloat16)
    shifts = gaussian(streams_of[9], (7, D), 0.3, 1.796875, ((1, 4),))
    ffn_gain = jnp.clip(1.0 + 0.15 * jax.random.normal(streams_of[10], (FF,), jnp.float32), 0.25, 1.75).astype(jnp.bfloat16)
    ffn_shifts = gaussian(streams_of[11], (2, FF), 0.3, 1.796875, ((1, 4),))
    return {"tokens": tokens, "cotangent": cotangent, "lengths": lengths, "dealing": dealing, "qkv_weight": qkv_weight, "out_weight": out_weight, "in_weight": in_weight, "back_weight": back_weight, "norm_gains": norm_gains, "shifts": shifts, "ffn_gain": ffn_gain, "ffn_shifts": ffn_shifts}


@jax.custom_vjp
def low(v):
    return lax.optimization_barrier(v.astype(jnp.bfloat16)).astype(jnp.float32)

@jax.custom_vjp
def low_back(v):
    return v

def low_keep(v):
    return (low(v), None)

def low_pass(kept, grad):
    return (grad,)

def back_keep(v):
    return (v, None)

def back_low(kept, grad):
    return (low(grad),)
low.defvjp(low_keep, low_pass)
low_back.defvjp(back_keep, back_low)

def layer_norm(values, gain, shift):
    average = lax.optimization_barrier(jnp.mean(values, axis=-1, keepdims=True))
    centred = values - average
    variance = lax.optimization_barrier(jnp.mean(centred * centred, axis=-1, keepdims=True))
    return centred * lax.rsqrt(variance + 1e-05) * gain + shift

def row_places(first_row, row_count, deal_row, bounds, group_rows):
    row_ids = first_row + jnp.arange(row_count, dtype=jnp.int32)
    group_ids = row_ids // group_rows
    onehot = (group_ids[:, None] == jnp.arange(deal_row.shape[0], dtype=jnp.int32)[None, :]).astype(jnp.int32)
    picked = lax.optimization_barrier(jnp.sum(onehot * deal_row[None, :].astype(jnp.int32), axis=1)).astype(jnp.int32)
    places = picked * group_rows + row_ids % group_rows
    segment = lax.optimization_barrier(jnp.sum((places[:, None] >= bounds[None, :]).astype(jnp.int32), axis=1)).astype(jnp.int32)
    return (places, segment)

def attend(query, keyed, valued, places, segment):
    block_rows = math.gcd(STREAM, 512)
    block_count = STREAM // block_rows
    key3 = keyed.reshape(STREAM, H, DH)
    value3 = valued.reshape(STREAM, H, DH)
    scaling = DH ** (-0.5)

    def one_block(pieces):
        query_block, query_places, query_segment = pieces
        scores = jnp.einsum('qhd,khd->hqk', query_block, key3, precision=lax.Precision.HIGHEST) * scaling
        scores = low_back(scores)
        allowed = ((segment[None, :] == query_segment[:, None]) & (places[None, :] <= query_places[:, None]))[None]
        masked = jnp.where(allowed, scores, -1e+30)
        highest = lax.optimization_barrier(jnp.max(masked, axis=-1, keepdims=True))
        expo = jnp.where(allowed, jnp.exp(masked - highest), 0.0)
        probabilities = low(expo / lax.optimization_barrier(jnp.sum(expo, axis=-1, keepdims=True)))
        return jnp.einsum('hqk,khd->qhd', probabilities, value3, precision=lax.Precision.HIGHEST)
    outputs = lax.map(jax.checkpoint(one_block), (query.reshape(block_count, block_rows, H, DH), places.reshape(block_count, block_rows), segment.reshape(block_count, block_rows)))
    return outputs.reshape(STREAM, D)

def layer(inputs, weights, places, segment):
    qkv_w, out_w, in_w, back_w, gains, shifts, ffn_gain, ffn_shifts = weights
    highest = lax.Precision.HIGHEST
    normed = low(layer_norm(inputs, gains[0], shifts[0]))
    projected = jnp.dot(normed, qkv_w, precision=highest)
    query = low(low_back(projected[:, :D] + shifts[1]))
    keyed = low(low_back(projected[:, D:2 * D]))
    valued = low(low_back(projected[:, 2 * D:] + shifts[2]))
    context = low_back(attend(query, keyed, valued, places, segment))
    inner = low(layer_norm(context, gains[1], shifts[3]))
    branch = low_back(jnp.dot(inner, out_w, precision=highest) + shifts[4])
    middle = inputs + branch
    normed_two = low(layer_norm(middle, gains[2], shifts[5]))
    hidden = low_back(jnp.dot(normed_two, in_w, precision=highest) + ffn_shifts[0])
    activated = jax.nn.gelu(hidden, approximate=False)
    inner_two = low(layer_norm(activated, ffn_gain, ffn_shifts[1]))
    result = low_back(jnp.dot(inner_two, back_w, precision=highest) + shifts[6])
    return middle + result

def reference(tokens, cotangent, lengths, dealing, qkv_weight, out_weight, in_weight, back_weight, norm_gains, shifts, ffn_gain, ffn_shifts):
    params = tuple((item.astype(jnp.float32) for item in (qkv_weight, out_weight, in_weight, back_weight, norm_gains, shifts, ffn_gain, ffn_shifts)))

    def per_stream(carry, item):
        stream_in, stream_cot, stream_len, stream_deal = item
        bounds = jnp.cumsum(stream_len).astype(jnp.int32)
        places, segment = row_places(0, STREAM, stream_deal.astype(jnp.int32), bounds, GROUP)

        def forward(inputs, weights):
            return layer(inputs, weights, places, segment)
        output, pullback = jax.vjp(forward, stream_in.astype(jnp.float32), params)
        input_grad, weight_grads = pullback(stream_cot.astype(jnp.float32))
        carry = jax.tree.map(jnp.add, carry, weight_grads)
        return (carry, (output.astype(jnp.bfloat16), input_grad))
    zeros = tuple((jnp.zeros(item.shape, jnp.float32) for item in params))
    sums, (outputs, input_grads) = lax.scan(per_stream, zeros, (tokens, cotangent, lengths, dealing))
    return (outputs, input_grads) + tuple(sums)
```

```python
import math

import jax
import jax.numpy as jnp
from jax import lax
from jax.experimental import pallas as pl
from jax.experimental.pallas import tpu as pltpu
from jax.sharding import PartitionSpec as P

D = 768
H = 12
DH = 64
FF = 3072
GROUP = 256
HPG = 3
TP = H // HPG
HC = HPG * DH
LANES = 256
SCALE2 = 1.4426950408889634 * DH ** -0.5
NEG = -1e30
NT = (((1,), (1,)), ((), ()))
F32 = jnp.float32
BF16 = jnp.bfloat16


def head_mask(h, shape):
    lane = lax.broadcasted_iota(jnp.int32, shape, 1)
    return (lane >= h*DH) & (lane < (h+1)*DH)

def block_bounds(group, bound_ref):
    lane = lax.broadcasted_iota(jnp.int32,(1,GROUP),1)
    q_places = group*GROUP+lane
    starts = jnp.zeros((1,GROUP),jnp.int32)
    first=jnp.int32(0); last=jnp.int32(0)
    for j in range(bound_ref.shape[0]):
        b=bound_ref[j]
        starts=jnp.where(q_places>=b,b,starts)
        first=jnp.where(group*GROUP>=b,b,first)
        last=jnp.where(group*GROUP+GROUP-1>=b,b,last)
    low=first//GROUP
    mid=jnp.minimum(group,(last+GROUP-1)//GROUP)
    return q_places,starts,low,mid

def sweep(group, low, mid, visit):
    lax.fori_loop(mid, group, lambda kg,c: visit(kg,False), None)
    def edge(t,c):
        kg=jnp.where(low+t<mid,low+t,group)
        return visit(kg,True)
    lax.fori_loop(0, mid-low+1, edge, None)

def allowed_pairs(kg,q_places,starts):
    k_places=kg*GROUP+lax.broadcasted_iota(jnp.int32,(GROUP,1),0)
    return (k_places<=q_places)&(k_places>=starts)

def forward_kernel(group_ref,slot_ref,bound_ref,q_ref,k_ref,v_ref,o_ref,ot_ref,lse_ref,vt_ref,qm_ref,acc_ref,m_ref,l_ref):
    def turn(b,c):
        rows=pl.ds(pl.multiple_of(b*GROUP,GROUP),GROUP)
        vt_ref[:,rows]=v_ref[rows,:].T
        return c
    lax.fori_loop(0,k_ref.shape[0]//GROUP,turn,None)
    def one(i,c):
        group=group_ref[i]
        rows=pl.ds(pl.multiple_of(i*GROUP,GROUP),GROUP)
        q_places,starts,low,mid=block_bounds(group,bound_ref)
        qb=q_ref[rows,:]
        for h in range(HPG):
            qm_ref[h]=jnp.where(head_mask(h,qb.shape),qb,jnp.zeros_like(qb))
        acc_ref[...]=jnp.zeros_like(acc_ref)
        m_ref[...]=jnp.full_like(m_ref,NEG)
        l_ref[...]=jnp.zeros_like(l_ref)
        def visit(kg,masked):
            slot=slot_ref[kg]
            cols=pl.ds(pl.multiple_of(slot*GROUP,GROUP),GROUP)
            kb=k_ref[cols,:]
            allowed=allowed_pairs(kg,q_places,starts) if masked else None
            for h in range(HPG):
                s=lax.dot_general(kb,qm_ref[h],NT,preferred_element_type=jnp.float32)
                if masked: s=jnp.where(allowed,s,NEG)
                old=m_ref[h:h+1,:]
                new=jnp.maximum(old,jnp.max(s,axis=0,keepdims=True))
                p=jnp.exp2((s-new)*SCALE2)
                alpha=jnp.exp2((old-new)*SCALE2)
                l_ref[h:h+1,:]=l_ref[h:h+1,:]*alpha+jnp.sum(p,axis=0,keepdims=True)
                m_ref[h:h+1,:]=new
                part=slice(h*DH,(h+1)*DH)
                acc_ref[part,:]=acc_ref[part,:]*alpha+jnp.dot(vt_ref[part,cols],p.astype(jnp.bfloat16),preferred_element_type=jnp.float32)
        sweep(group,low,mid,visit)
        for h in range(HPG):
            part=slice(h*DH,(h+1)*DH)
            acc_ref[part,:]=acc_ref[part,:]/l_ref[h:h+1,:]
        lse_ref[:,rows]=m_ref[...]*SCALE2+jnp.log2(l_ref[...])
        ot_ref[:,rows]=acc_ref[0:HPG*DH,:]
        o_ref[rows,:]=acc_ref[...].T.astype(jnp.bfloat16)
        return c
    lax.fori_loop(0,q_ref.shape[0]//GROUP,one,None)

SMEM=pltpu.MemorySpace.SMEM
VM=pltpu.MemorySpace.VMEM
def attend_forward(groups,slots,bounds,q,k,v):
    n=q.shape[0]; s=k.shape[0]
    return pl.pallas_call(forward_kernel,name="attend_forward",
        in_specs=[pl.BlockSpec(memory_space=SMEM)]*3+[pl.BlockSpec(memory_space=VM)]*3,
        out_specs=[pl.BlockSpec(memory_space=VM)]*3,
        out_shape=[jax.ShapeDtypeStruct((n,LANES),jnp.bfloat16),jax.ShapeDtypeStruct((HPG*DH,n),jnp.float32),jax.ShapeDtypeStruct((8,n),jnp.float32)],
        scratch_shapes=[pltpu.VMEM((LANES,s),jnp.bfloat16),pltpu.VMEM((HPG,GROUP,LANES),jnp.bfloat16),pltpu.VMEM((LANES,GROUP),jnp.float32),pltpu.VMEM((8,GROUP),jnp.float32),pltpu.VMEM((8,GROUP),jnp.float32)],
        cost_estimate=pl.CostEstimate(flops=n*s*LANES,transcendentals=n*s,bytes_accessed=(2*n+2*s)*LANES*2),
    )(groups,slots,bounds,q,k,v)

def backward_kernel(group_ref,slot_ref,bound_ref,q_ref,k_ref,v_ref,do_ref,ot_ref,lse_ref,dq_ref,dk_ref,dv_ref,dko_ref,dvo_ref,kt_ref,qm_ref,dm_ref,acc_ref,row_ref,dka_ref,dva_ref):
    n=q_ref.shape[0]
    def turn(b,c):
        rows=pl.ds(pl.multiple_of(b*GROUP,GROUP),GROUP)
        kt_ref[:,rows]=k_ref[rows,:].T
        dka_ref[rows,:]=jnp.zeros((GROUP,LANES),jnp.float32)
        dva_ref[rows,:]=jnp.zeros((GROUP,LANES),jnp.float32)
        return c
    lax.fori_loop(0,k_ref.shape[0]//GROUP,turn,None)
    def one(i,c):
        group=group_ref[i]
        rows=pl.ds(pl.multiple_of(i*GROUP,GROUP),GROUP)
        q_places,starts,low,mid=block_bounds(group,bound_ref)
        qb=q_ref[rows,:]; db=do_ref[rows,:]
        for h in range(HPG):
            part=slice(h*GROUP,(h+1)*GROUP)
            mask=head_mask(h,qb.shape)
            qm_ref[part,:]=jnp.where(mask,qb,jnp.zeros_like(qb))
            dm_ref[part,:]=jnp.where(mask,db,jnp.zeros_like(db))
        dt=db.T.astype(jnp.float32)
        for h in range(HPG):
            part=slice(h*DH,(h+1)*DH)
            row_ref[h:h+1,:]=jnp.sum(dt[part,:]*ot_ref[part,rows],axis=0,keepdims=True)
        acc_ref[...]=jnp.zeros_like(acc_ref)
        def visit(kg,masked):
            slot=slot_ref[kg]
            cols=pl.ds(pl.multiple_of(slot*GROUP,GROUP),GROUP)
            kb=k_ref[cols,:]; vb=v_ref[cols,:]
            allowed=allowed_pairs(kg,q_places,starts) if masked else None
            ps=[];ds=[]
            for h in range(HPG):
                part=slice(h*GROUP,(h+1)*GROUP)
                s=lax.dot_general(kb,qm_ref[part,:],NT,preferred_element_type=jnp.float32)
                if masked: s=jnp.where(allowed,s,NEG)
                p=jnp.exp2(s*SCALE2-lse_ref[h:h+1,rows])
                dp=lax.dot_general(vb,dm_ref[part,:],NT,preferred_element_type=jnp.float32)
                d=(p*(dp-row_ref[h:h+1,:])).astype(jnp.bfloat16)
                ps.append(p.astype(jnp.bfloat16)); ds.append(d)
                piece=slice(h*DH,(h+1)*DH)
                acc_ref[piece,:]+=jnp.dot(kt_ref[piece,cols],d,preferred_element_type=jnp.float32)
            dva_ref[cols,:]+=jnp.dot(jnp.concatenate(ps,axis=1),dm_ref[...],preferred_element_type=jnp.float32)
            dka_ref[cols,:]+=jnp.dot(jnp.concatenate(ds,axis=1),qm_ref[...],preferred_element_type=jnp.float32)
        sweep(group,low,mid,visit)
        dq_ref[rows,:]=(acc_ref[...]*DH**-0.5).T.astype(jnp.bfloat16)
        return c
    lax.fori_loop(0,n//GROUP,one,None)
    def store(b,c):
        rows=pl.ds(pl.multiple_of(b*GROUP,GROUP),GROUP)
        dk_ref[rows,:]=dka_ref[rows,:]*DH**-0.5
        dv_ref[rows,:]=dva_ref[rows,:]
        return c
    lax.fori_loop(0,n//GROUP,store,None)
    def other(b,c):
        rows=pl.ds(pl.multiple_of(b*GROUP,GROUP),GROUP)
        from_rows=pl.ds(pl.multiple_of(n+b*GROUP,GROUP),GROUP)
        dko_ref[rows,:]=(dka_ref[from_rows,:]*DH**-0.5).astype(jnp.bfloat16)
        dvo_ref[rows,:]=dva_ref[from_rows,:].astype(jnp.bfloat16)
        return c
    lax.fori_loop(0,(k_ref.shape[0]-n)//GROUP,other,None)

def attend_backward(groups,slots,bounds,q,k,v,do,ot,lse):
    n=q.shape[0]; s=k.shape[0]
    B=pl.BlockSpec(memory_space=VM)
    return pl.pallas_call(backward_kernel,name="attend_backward",
        in_specs=[pl.BlockSpec(memory_space=SMEM)]*3+[B]*6,
        out_specs=[B]*5,
        out_shape=[jax.ShapeDtypeStruct((n,LANES),jnp.bfloat16),jax.ShapeDtypeStruct((n,LANES),jnp.float32),jax.ShapeDtypeStruct((n,LANES),jnp.float32),jax.ShapeDtypeStruct((s-n,LANES),jnp.bfloat16),jax.ShapeDtypeStruct((s-n,LANES),jnp.bfloat16)],
        scratch_shapes=[pltpu.VMEM((LANES,s),jnp.bfloat16),pltpu.VMEM((HPG*GROUP,LANES),jnp.bfloat16),pltpu.VMEM((HPG*GROUP,LANES),jnp.bfloat16),pltpu.VMEM((LANES,GROUP),jnp.float32),pltpu.VMEM((8,GROUP),jnp.float32),pltpu.VMEM((s,LANES),jnp.float32),pltpu.VMEM((s,LANES),jnp.float32)],
        cost_estimate=pl.CostEstimate(flops=n*s*LANES*3,transcendentals=n*s,bytes_accessed=(2*n+2*s)*LANES*4),
    )(groups,slots,bounds,q,k,v,do,ot,lse)


def layer_norm(values, gain, shift):
    average = jnp.mean(values, axis=-1, keepdims=True)
    centred = values - average
    variance = jnp.mean(centred * centred, axis=-1, keepdims=True)
    return centred * lax.rsqrt(variance + 1e-05) * gain + shift


def gelu_exact(values):
    return jax.nn.gelu(values, approximate=False)


def outer_sum(left, right):
    return lax.dot_general(left, right, (((0,), (0,)), ((), ())), preferred_element_type=F32)


def times_transposed(left, matrix):
    return lax.dot_general(left, matrix, (((1,), (1,)), ((), ())), preferred_element_type=F32)


def pick(array, index, axis=0):
    return lax.dynamic_index_in_dim(array, index, axis, keepdims=False)


def make_local(ctx_size, fsdp_size):
    nq = ctx_size // TP
    fast = ctx_size == 8 and fsdp_size == 4

    def over_heads(value, mask):
        return lax.ppermute(
            value, "ctx", [(i, ((i // nq) ^ mask) * nq + i % nq) for i in range(ctx_size)]
        )

    def over_rows(value, shift):
        return lax.ppermute(
            value,
            "ctx",
            [(i, (i // nq) * nq + (i % nq - shift) % nq) for i in range(ctx_size)],
        )

    def over_fsdp(value, mask):
        return lax.ppermute(value, "fsdp", [(i, i ^ mask) for i in range(fsdp_size)])

    def exchange_heads(own, halves):
        one = over_heads(own, 1)
        two = over_heads(own, 2)
        first, second = halves
        low = over_heads(first(one), 2)
        high = over_heads(second(two), 1)
        return one, two, low, high

    def local(
        tokens,
        cotangent,
        lengths,
        dealing,
        qkv_weight,
        out_weight,
        in_weight,
        back_weight,
        norm_gains,
        shifts,
        ffn_gain,
        ffn_shifts,
    ):
        ctx = lax.axis_index("ctx")
        fs = lax.axis_index("fsdp")
        hg = ctx // nq
        qs = ctx % nq
        rows = tokens.shape[1]
        shard = qkv_weight.shape[0]
        deal_row = dealing[0]
        group_count = deal_row.shape[0]
        per = rows // GROUP
        bounds = jnp.cumsum(lengths[0])
        members = [
            [((hg ^ m) * nq + (qs + s) % nq) * per + j for m in range(TP) for j in range(per)]
            for s in range(nq)
        ]
        stored = jnp.stack([g for part in members for g in part]).astype(jnp.int32)
        onehot = (stored[:, None] == jnp.arange(group_count, dtype=jnp.int32)[None, :]).astype(
            jnp.int32
        )
        dealt = jnp.sum(onehot * deal_row[None, :], axis=1)
        q_groups = dealt[: TP * per]
        matches = (dealt[None, :] == jnp.arange(group_count, dtype=jnp.int32)[:, None]).astype(
            jnp.int32
        )
        slots = jnp.sum(matches * jnp.arange(group_count, dtype=jnp.int32)[None, :], axis=1)

        mine = tokens[0]
        half = rows // 2
        one, two, low, high = exchange_heads(mine, (lambda a: a[:half], lambda a: a[half:]))

        def columns(weight, index):
            out = []
            for part in range(3):
                value = weight[:, part * D : part * D + HC]
                for g in range(1, TP):
                    other = weight[:, part * D + g * HC : part * D + (g + 1) * HC]
                    value = jnp.where(index == g, other, value)
                out.append(value)
            return jnp.concatenate(out, axis=1)

        flat = jnp.concatenate(
            [norm_gains.reshape(-1), shifts.reshape(-1), ffn_gain, ffn_shifts.reshape(-1)]
        )
        width = 3 * HC
        small_rows = -(-flat.shape[0] // width)
        small_rows += -small_rows % 8
        small = jnp.pad(flat, (0, small_rows * width - flat.shape[0])).reshape(small_rows, width)
        packed = jnp.concatenate([columns(qkv_weight, hg), small], axis=0)
        parts = jnp.stack([packed] + [over_fsdp(packed, m) for m in range(1, fsdp_size)])
        ordered = [pick(parts, f ^ fs) for f in range(fsdp_size)]
        w_own = jnp.concatenate([p[:shard] for p in ordered], axis=0)
        flats = [p[shard:].reshape(-1) for p in ordered]

        def unpack(at, count, size):
            block = count * size
            return jnp.concatenate(
                [f[at : at + block].reshape(count, size) for f in flats], axis=1
            ).astype(F32)

        feature = norm_gains.shape[1]
        wide = ffn_gain.shape[0]
        gains = unpack(0, 3, feature)
        shift_rows = unpack(3 * feature, 7, feature)
        ffn_scale = unpack(10 * feature, 1, wide)[0]
        ffn_shift_rows = unpack(10 * feature + wide, 2, wide)

        if fast:
            in_w, back_w, out_w = gather_weights(
                in_weight, back_weight, out_weight, hg, qs, fs, over_heads, over_rows, over_fsdp
            )
        else:
            in_w = lax.all_gather(in_weight, "fsdp", axis=0, tiled=True)
            back_w = lax.all_gather(back_weight, "fsdp", axis=0, tiled=True)
            out_w = lax.all_gather(out_weight, "fsdp", axis=0, tiled=True)

        def normed_of(tok):
            return layer_norm(tok.astype(F32), gains[0], shift_rows[0]).astype(BF16)

        normed = jnp.concatenate([normed_of(t) for t in (mine, one, two, low, high)], axis=0)
        w_padded = jnp.concatenate(
            [
                jnp.pad(w_own[:, i * HC : (i + 1) * HC], ((0, 0), (0, LANES - HC)))
                for i in range(3)
            ],
            axis=1,
        )

        def own_heads(row):
            return jnp.pad(pick(row.reshape(TP, HC), hg), (0, LANES - HC))

        projected = jnp.dot(normed, w_padded, preferred_element_type=F32)
        query = (projected[:, :LANES] + own_heads(shift_rows[1])).astype(BF16)
        keyed = projected[:, LANES : 2 * LANES].astype(BF16)
        valued = (projected[:, 2 * LANES :] + own_heads(shift_rows[2])).astype(BF16)
        both = jnp.stack([keyed, valued])
        pieces = [both] + [over_rows(both, s) for s in range(1, nq)]
        keys = jnp.concatenate([p[0] for p in pieces], axis=0)
        values = jnp.concatenate([p[1] for p in pieces], axis=0)

        context_low, context_t, log_total = attend_forward(
            q_groups, slots, bounds, query, keys, values
        )

        def fold(block):
            return jnp.concatenate([block[: rows // 2, :HC], block[rows // 2 :, :HC]], axis=1)

        def unfold(block):
            return jnp.concatenate([block[:, :HC], block[:, HC:]], axis=0)

        ctx_parts = context_low.reshape(TP, rows, LANES)
        got = [ctx_parts[0][:, :HC]] + [
            unfold(over_heads(fold(ctx_parts[m]), m)) for m in range(1, TP)
        ]
        context = jnp.concatenate(got, axis=1).astype(F32)

        def relative(row):
            blocks = row.reshape(TP, HC)
            return jnp.concatenate([pick(blocks, hg ^ m) for m in range(TP)])

        gain_one = relative(gains[1])
        shift_three = relative(shift_rows[3])
        out_blocks = out_w.reshape(TP, HC, D)
        out_rel = jnp.concatenate([pick(out_blocks, hg ^ m) for m in range(TP)], axis=0)

        inputs = mine.astype(F32)
        inner = layer_norm(context, gain_one, shift_three)
        inner_low = inner.astype(BF16)
        branch = jnp.dot(inner_low, out_rel, preferred_element_type=F32) + shift_rows[4]
        middle = inputs + branch
        normed_two = layer_norm(middle, gains[2], shift_rows[5])
        normed_two_low = normed_two.astype(BF16)
        hidden = jnp.dot(normed_two_low, in_w, preferred_element_type=F32) + ffn_shift_rows[0]
        activated = gelu_exact(hidden)
        inner_two = layer_norm(activated, ffn_scale, ffn_shift_rows[1])
        inner_two_low = inner_two.astype(BF16)
        result = jnp.dot(inner_two_low, back_w, preferred_element_type=F32) + shift_rows[6]
        mixed_out = (middle + result).astype(BF16)

        upstream = cotangent[0].astype(F32)
        result_low = cotangent[0]
        grad_back_w = outer_sum(inner_two_low, result_low).astype(BF16)
        grad_back_bias = jnp.sum(upstream, axis=0)
        grad_inner_two = times_transposed(result_low, back_w)
        norm_pull = jax.vjp(layer_norm, activated, ffn_scale, ffn_shift_rows[1])[1]
        grad_activated, grad_ffn_gain, grad_ffn_shift = norm_pull(grad_inner_two)
        grad_hidden = jax.vjp(gelu_exact, hidden)[1](grad_activated)[0]
        hidden_low = grad_hidden.astype(BF16)
        grad_in_w = outer_sum(normed_two_low, hidden_low).astype(BF16)
        grad_in_bias = jnp.sum(hidden_low.astype(F32), axis=0)
        grad_normed_two = times_transposed(hidden_low, in_w)
        second_pull = jax.vjp(layer_norm, middle, gains[2], shift_rows[5])[1]
        grad_middle_part, grad_gain_two, grad_shift_five = second_pull(grad_normed_two)
        grad_middle = upstream + grad_middle_part
        branch_low = grad_middle.astype(BF16)
        grad_out_rel = outer_sum(inner_low, branch_low).astype(BF16)
        grad_out_bias = jnp.sum(branch_low.astype(F32), axis=0)
        grad_inner = times_transposed(branch_low, out_rel)
        inner_pull = jax.vjp(layer_norm, context, gain_one, shift_three)[1]
        grad_context, grad_gain_one, grad_shift_three = inner_pull(grad_inner)
        grad_context_low = grad_context.astype(BF16)

        def widen(block):
            return jnp.pad(block, ((0, 0), (0, LANES - HC)))

        sent = [grad_context_low[:, m * HC : (m + 1) * HC] for m in range(TP)]
        grad_rows = jnp.concatenate(
            [widen(sent[0])]
            + [widen(unfold(over_heads(fold(sent[m]), m))) for m in range(1, TP)],
            axis=0,
        )
        grad_q, key_own, value_own, key_other, value_other = attend_backward(
            q_groups, slots, bounds, query, keys, values, grad_rows, context_t, log_total
        )
        set_rows = TP * rows
        for s in range(1, nq):
            part = slice((s - 1) * set_rows, s * set_rows)
            came = over_rows(jnp.stack([key_other[part], value_other[part]]), nq - s)
            key_own = key_own + came[0].astype(F32)
            value_own = value_own + came[1].astype(F32)
        grads = jnp.concatenate(
            [
                grad_q[:, :HC],
                key_own.astype(BF16)[:, :HC],
                value_own.astype(BF16)[:, :HC],
            ],
            axis=1,
        )
        grad_qkv_w = outer_sum(normed, grads)
        column_sums = jnp.sum(grads.astype(F32), axis=0)

        grad_parts = grads.reshape(TP, rows, 3 * HC)
        back_parts = [grad_parts[0]] + [over_heads(grad_parts[m], m) for m in range(1, TP)]
        w_one, w_two, w_low, w_high = exchange_heads(
            w_own, (lambda a: a[: D // 2], lambda a: a[D // 2 :])
        )
        w_three = jnp.concatenate([w_low, w_high], axis=0)
        grad_normed = sum(
            times_transposed(g, w)
            for g, w in zip(back_parts, (w_own, w_one, w_two, w_three))
        )
        first_pull = jax.vjp(layer_norm, inputs, gains[0], shift_rows[0])[1]
        grad_inputs_part, grad_gain_zero, grad_shift_zero = first_pull(grad_normed)
        input_grad = grad_middle + grad_inputs_part

        def absolute(row):
            blocks = row.reshape(TP, HC)
            return jnp.concatenate([pick(blocks, hg ^ m) for m in range(TP)])

        def placed(row):
            zero = jnp.zeros((TP, HC), F32)
            return lax.dynamic_update_slice(zero, row[None], (hg, 0)).reshape(-1)

        vectors = [
            grad_gain_zero,
            absolute(grad_gain_one),
            grad_gain_two,
            grad_shift_zero,
            placed(column_sums[:HC]),
            placed(column_sums[2 * HC :]),
            absolute(grad_shift_three),
            grad_out_bias,
            grad_shift_five,
            grad_back_bias,
            grad_ffn_gain,
            grad_in_bias,
            grad_ffn_shift,
        ]
        order = ctx * fsdp_size + fs
        total_devices = ctx_size * fsdp_size
        small_terms = jnp.concatenate(vectors)
        if fast:
            small_terms = small_terms.reshape(-1, 128)
            small_terms = small_terms + over_rows(small_terms, 1)
            for m in (1, 2):
                small_terms = small_terms + over_heads(small_terms, m)
            for m in (1, 2):
                small_terms = small_terms + over_fsdp(small_terms, m)
            small_terms = small_terms.reshape(-1)
        else:
            small_terms = lax.psum(small_terms, ("ctx", "fsdp"))
        narrow = small_terms[: 10 * D].reshape(10, total_devices, D // total_devices)
        narrow = pick(narrow, order, 1)
        broad = small_terms[10 * D :].reshape(3, total_devices, FF // total_devices)
        broad = pick(broad, order, 1)
        small_out = (narrow[:3], narrow[3:], broad[0], broad[1:])

        if fast:
            grad_out_w = grad_out_rel
            back_out, in_out, out_out = reduce_weights(
                grad_back_w, grad_in_w, grad_out_rel, hg, qs, fs, over_heads, over_rows, over_fsdp
            )
            qkv_out = reduce_columns(grad_qkv_w, hg, qs, fs, over_heads, over_rows, over_fsdp)
        else:
            blocks = grad_out_rel.reshape(TP, HC, D)
            grad_out_w = jnp.concatenate([pick(blocks, hg ^ m) for m in range(TP)], axis=0)
            axes = ("ctx", "fsdp")
            back_out, in_out, out_out = (
                lax.psum_scatter(g, axes, scatter_dimension=0, tiled=True).astype(F32)
                for g in (grad_back_w, grad_in_w, grad_out_w)
            )
            zero = jnp.zeros((D, 3, TP, HC), BF16)
            full = lax.dynamic_update_slice(
                zero, grad_qkv_w.astype(BF16).reshape(D, 3, 1, HC), (0, 0, hg, 0)
            ).reshape(D, 3 * D)
            qkv_out = lax.psum_scatter(full, axes, scatter_dimension=0, tiled=True).astype(F32)
        return (
            mixed_out[None],
            input_grad[None],
            qkv_out,
            out_out,
            in_out,
            back_out,
        ) + small_out

    return local


PIECE = 216


def assemble_kernel(
    place_ref, source_ref, own_ref, near_ref, far_ref, in_ref, back_ref, out_ref
):
    step = pl.program_id(0)

    def put(ref):
        value = ref[0]
        in_ref[0:96, :] = value[0:96, 0:384]
        in_ref[96:192, :] = value[0:96, 384:768]
        back_ref[...] = value[96:192, :]
        out_ref[...] = value[192:216, :]

    pl.when(step < 8)(lambda: put(own_ref))
    pl.when((step >= 8) & (step < 20))(lambda: put(near_ref))
    pl.when(step >= 20)(lambda: put(far_ref))


def assemble(places, own, near, far):
    whole = (1, PIECE, D)
    return pl.pallas_call(
        assemble_kernel,
        name="assemble_weights",
        grid_spec=pltpu.PrefetchScalarGridSpec(
            num_scalar_prefetch=2,
            grid=(32,),
            in_specs=[
                pl.BlockSpec(whole, lambda i, p, s: (jnp.minimum(i, 7), 0, 0)),
                pl.BlockSpec(whole, lambda i, p, s: (jnp.clip(i - 8, 0, 11), 0, 0)),
                pl.BlockSpec(whole, lambda i, p, s: (jnp.clip(i - 20, 0, 11), 0, 0)),
            ],
            out_specs=[
                pl.BlockSpec((192, 384), lambda i, p, s: (p[i], s[i])),
                pl.BlockSpec((96, D), lambda i, p, s: (p[i] * 8 + s[i], 0)),
                pl.BlockSpec((24, D), lambda i, p, s: (p[i] * 8 + s[i], 0)),
            ],
        ),
        out_shape=[
            jax.ShapeDtypeStruct((D, FF), BF16),
            jax.ShapeDtypeStruct((FF, D), BF16),
            jax.ShapeDtypeStruct((D, D), BF16),
        ],
        cost_estimate=pl.CostEstimate(flops=0, transcendentals=0, bytes_accessed=21000000),
    )(places[0], places[1], own, near, far)


def gather_weights(in_weight, back_weight, out_weight, hg, qs, fs, over_heads, over_rows, over_fsdp):
    cut = [in_weight[:, c * 384 : (c + 1) * 384] for c in range(8)]
    cut = jnp.stack([jnp.concatenate([c[:96], c[96:]], axis=1) for c in cut])
    own = jnp.concatenate(
        [cut, back_weight.reshape(8, 96, D), out_weight.reshape(8, 24, D)], axis=1
    )
    piece = pick(own, hg * 2 + qs)
    foreign = jnp.stack([over_fsdp(piece, m) for m in (1, 2, 3)])
    one = over_heads(foreign, 1)
    two = over_heads(foreign, 2)
    low = over_heads(one[:, :104], 2)
    high = over_heads(two[:, 104:], 1)
    near = jnp.concatenate([foreign, one, two, jnp.concatenate([low, high], axis=1)], axis=0)
    far = over_rows(near, 1)
    own_z = [fs + 0 * c for c in range(8)]
    own_c = [c + 0 * fs for c in range(8)]
    rest_z = [fs ^ m for _ in range(4) for m in (1, 2, 3)]
    near_c = [(hg ^ h) * 2 + qs for h in range(4) for _ in range(3)]
    far_c = [(hg ^ h) * 2 + (1 - qs) for h in range(4) for _ in range(3)]
    places = (
        jnp.stack(own_z + rest_z + rest_z).astype(jnp.int32),
        jnp.stack(own_c + near_c + far_c).astype(jnp.int32),
    )
    return assemble(places, own, near, far)


def reduce_weights(back, inn, out_rel, hg, qs, fs, over_heads, over_rows, over_fsdp):
    chunks = [inn[:, j * D : (j + 1) * D].reshape(4, 2, 4, 24, D) for j in range(4)]
    outs = out_rel.reshape(4, 2, 4, 24, D)
    outs = jnp.stack([pick(outs, hg ^ h) for h in range(4)])
    packed = jnp.concatenate([back.reshape(4, 2, 4, 96, D)] + chunks + [outs], axis=3)
    packed = scatter_sum(packed, hg, qs, fs, over_heads, over_rows, over_fsdp)
    inn = jnp.concatenate([packed[96 + 24 * j : 120 + 24 * j] for j in range(4)], axis=1)
    return packed[:96], inn, packed[192:216]


def scatter_sum(packed, hg, qs, fs, over_heads, over_rows, over_fsdp):
    keep = pick(packed, qs, 1)
    keep = keep + over_rows(pick(packed, 1 - qs, 1), 1)
    x, y = hg % 2, hg // 2
    cut = 104
    first = keep[:, :, :cut].reshape(2, 2, 4, cut, D)
    second = keep[:, :, cut:].reshape(2, 2, 4, PIECE - cut, D)
    first = pick(first, x, 1) + over_heads(pick(first, 1 - x, 1), 1)
    second = pick(second, y, 0) + over_heads(pick(second, 1 - y, 0), 2)
    first = pick(first, y, 0) + over_heads(pick(first, 1 - y, 0), 2)
    second = pick(second, x, 0) + over_heads(pick(second, 1 - x, 0), 1)
    both = jnp.concatenate([first, second], axis=1)
    total = pick(both, fs).astype(F32)
    for m in (1, 2, 3):
        total = total + over_fsdp(pick(both, fs ^ m), m).astype(F32)
    return total


def reduce_columns(grad, hg, qs, fs, over_heads, over_rows, over_fsdp):
    width = 3 * HC
    blocks = grad.reshape(4, 2, 4, 24, width)
    keep = pick(blocks, qs, 1) + over_rows(pick(blocks, 1 - qs, 1).astype(BF16), 1).astype(F32)
    total = pick(keep, fs, 1)
    low = keep.astype(BF16)
    for m in (1, 2, 3):
        total = total + over_fsdp(pick(low, fs ^ m, 1), m).astype(F32)
    mine = [pick(total, hg)] + [over_heads(pick(total, hg ^ m), m) for m in (1, 2, 3)]
    mine = jnp.stack(mine)
    mine = jnp.stack([pick(mine, hg ^ m) for m in range(4)])
    return jnp.concatenate(
        [mine[g, :, p * HC : (p + 1) * HC] for p in range(3) for g in range(4)], axis=1
    )


def solution(mesh):
    ctx_size = mesh.shape["ctx"]
    fsdp_size = mesh.shape["fsdp"]
    in_specs = (
        P("fsdp", "ctx", None),
        P("fsdp", "ctx", None),
        P("fsdp", None),
        P("fsdp", None),
        P("fsdp", None),
        P("fsdp", None),
        P("fsdp", None),
        P("fsdp", None),
        P(None, "fsdp"),
        P(None, "fsdp"),
        P("fsdp"),
        P(None, "fsdp"),
    )
    out_specs = (
        P("fsdp", "ctx", None),
        P("fsdp", "ctx", None),
        P(("ctx", "fsdp"), None),
        P(("ctx", "fsdp"), None),
        P(("ctx", "fsdp"), None),
        P(("ctx", "fsdp"), None),
        P(None, ("ctx", "fsdp")),
        P(None, ("ctx", "fsdp")),
        P(("ctx", "fsdp")),
        P(None, ("ctx", "fsdp")),
    )
    return jax.shard_map(
        make_local(ctx_size, fsdp_size),
        mesh=mesh,
        in_specs=in_specs,
        out_specs=out_specs,
        check_vma=False,
    )
```

```python
import functools

import jax
import jax.numpy as jnp
from jax import lax
from jax.experimental import pallas as pl
from jax.experimental.pallas import tpu as pltpu
from jax.sharding import PartitionSpec as P

D = 768
H = 12
DH = 64
FF = 3072
GROUP = 256
HPG = 3
TP = H // HPG
HC = HPG * DH
LANES = 256
SCALE2 = 1.4426950408889634 * DH ** -0.5
NEG = -1e30
NT = (((1,), (1,)), ((), ()))
F32 = jnp.float32
BF16 = jnp.bfloat16

SMEM = pltpu.MemorySpace.SMEM
VM = pltpu.MemorySpace.VMEM
HW = 2 * DH
WIDE = HPG * HW


def cost(us):
    return pl.CostEstimate(flops=int(us * 1.1e9), transcendentals=0, bytes_accessed=100000)


def block_bounds(group, bound_ref):
    lane = lax.broadcasted_iota(jnp.int32, (1, GROUP), 1)
    q_places = group * GROUP + lane
    starts = jnp.zeros((1, GROUP), jnp.int32)
    first = jnp.int32(0)
    last = jnp.int32(0)
    for j in range(bound_ref.shape[0]):
        b = bound_ref[j]
        starts = jnp.where(q_places >= b, b, starts)
        first = jnp.where(group * GROUP >= b, b, first)
        last = jnp.where(group * GROUP + GROUP - 1 >= b, b, last)
    low = first // GROUP
    mid = jnp.minimum(group, (last + GROUP - 1) // GROUP)
    return q_places, starts, low, mid


def sweep(group, low, mid, visit):
    lax.fori_loop(mid, group, lambda kg, c: visit(kg, False), None)

    def edge(t, c):
        kg = jnp.where(low + t < mid, low + t, group)
        return visit(kg, True)

    lax.fori_loop(0, mid - low + 1, edge, None)


def allowed_pairs(kg, q_places, starts):
    k_places = kg * GROUP + lax.broadcasted_iota(jnp.int32, (GROUP, 1), 0)
    return (k_places <= q_places) & (k_places >= starts)


def group_rows(index):
    return pl.ds(pl.multiple_of(index * GROUP, GROUP), GROUP)


def project_kernel(count, *refs):
    tok_refs = refs[:count]
    w_ref, row_ref, bias_ref, a_ref, q_ref, kv_ref = refs[count:]
    at = 0
    for ref in tok_refs:

        def part(i, c, ref=ref, at=at):
            rows = pl.ds(pl.multiple_of(i * GROUP, GROUP), GROUP)
            to = pl.ds(pl.multiple_of(at + i * GROUP, GROUP), GROUP)
            value = ref[rows, :].astype(F32)
            centred = value - jnp.mean(value, axis=1, keepdims=True)
            variance = jnp.mean(centred * centred, axis=1, keepdims=True)
            normed = centred * lax.rsqrt(variance + 1e-05) * row_ref[0:1, :] + row_ref[1:2, :]
            normed = normed.astype(BF16)
            a_ref[to, :] = normed
            out = jnp.dot(normed, w_ref[...], preferred_element_type=F32) + bias_ref[0:1, :]
            kv_ref[to, :] = out[:, :WIDE].astype(BF16)
            none = jnp.zeros((GROUP, DH), BF16)
            heads = []
            for h in range(HPG):
                lane = WIDE + h * DH
                heads += [out[:, lane : lane + DH].astype(BF16), none]
            q_ref[to, :] = jnp.concatenate(heads, axis=1)
            return c

        lax.fori_loop(0, ref.shape[0] // GROUP, part, None)
        at += ref.shape[0]


def project(toks, weight, norm_rows, bias):
    n = sum(t.shape[0] for t in toks)
    return pl.pallas_call(
        functools.partial(project_kernel, len(toks)),
        name="project",
        in_specs=[pl.BlockSpec(memory_space=VM)] * (len(toks) + 3),
        out_specs=[pl.BlockSpec(memory_space=VM)] * 3,
        out_shape=[
            jax.ShapeDtypeStruct((n, D), BF16),
            jax.ShapeDtypeStruct((n, WIDE), BF16),
            jax.ShapeDtypeStruct((n, WIDE), BF16),
        ],
        cost_estimate=cost(4 + n // 512),
    )(*toks, weight, norm_rows, bias)


def forward_kernel(chunks, key_chunks, *refs):
    dealt_ref, bound_ref = refs[:2]
    q_refs = refs[2 : 2 + chunks]
    kv_refs = refs[2 + chunks : 2 + chunks + key_chunks]
    o_refs = refs[2 + chunks + key_chunks : 2 + chunks + key_chunks + TP]
    ot_ref, lse_ref, qt_ref, kv_ref, kvt_ref, o_ref, acc_ref = refs[
        2 + chunks + key_chunks + TP :
    ]
    at = 0
    for ref in kv_refs:
        for j in range(ref.shape[0] // GROUP):
            rows = group_rows(dealt_ref[at])
            block = ref[j * GROUP : (j + 1) * GROUP, :]
            kv_ref[rows, :] = block
            kvt_ref[:, rows] = block.T
            at += 1
    at = 0
    for ref in q_refs:
        for j in range(ref.shape[0] // GROUP):
            qt_ref[:, at * GROUP : (at + 1) * GROUP] = ref[j * GROUP : (j + 1) * GROUP, :].T
            at += 1

    def one(i, c):
        group = dealt_ref[i]
        rows = group_rows(i)
        q_places, starts, low, mid = block_bounds(group, bound_ref)
        acc_ref[...] = jnp.zeros_like(acc_ref)

        def visit(kg, masked, carry):
            cols = group_rows(kg)
            allowed = allowed_pairs(kg, q_places, starts) if masked else None
            out = []
            for h in range(HPG):
                lanes = slice(h * HW, (h + 1) * HW)
                s = jnp.dot(kv_ref[cols, lanes], qt_ref[lanes, rows], preferred_element_type=F32)
                if masked:
                    s = jnp.where(allowed, s, NEG)
                old, total = carry[h]
                new = jnp.maximum(old, jnp.max(s, axis=0, keepdims=True))
                p = jnp.exp2((s - new) * SCALE2)
                alpha = jnp.exp2((old - new) * SCALE2)
                total = total * alpha + jnp.sum(p, axis=0, keepdims=True)
                part = slice(h * DH, (h + 1) * DH)
                acc_ref[part, :] = acc_ref[part, :] * alpha + jnp.dot(
                    kvt_ref[h * HW + DH : (h + 1) * HW, cols],
                    p.astype(BF16),
                    preferred_element_type=F32,
                )
                out.append((new, total))
            return tuple(out)

        start = tuple(
            (jnp.full((1, GROUP), NEG, F32), jnp.zeros((1, GROUP), F32)) for _ in range(HPG)
        )
        carry = lax.fori_loop(mid, group, lambda kg, c: visit(kg, False, c), start)

        def edge(t, c):
            return visit(jnp.where(low + t < mid, low + t, group), True, c)

        carry = lax.fori_loop(0, mid - low + 1, edge, carry)
        for h in range(HPG):
            part = slice(h * DH, (h + 1) * DH)
            acc_ref[part, :] = acc_ref[part, :] / carry[h][1]
            lse_ref[h : h + 1, rows] = carry[h][0] * SCALE2 + jnp.log2(carry[h][1])
        ot_ref[:, rows] = acc_ref[0:HC, :]
        o_ref[rows, :] = acc_ref[...].T.astype(BF16)
        return c

    lax.fori_loop(0, o_ref.shape[0] // GROUP, one, None)
    for m, ref in enumerate(o_refs):
        half = ref.shape[0]
        low = o_ref[2 * m * half : (2 * m + 1) * half, :HC]
        high = o_ref[(2 * m + 1) * half : (2 * m + 2) * half, :HC]
        ref[...] = jnp.concatenate([low, high], axis=1)


def attend_forward(dealt, bounds, queries, pairs):
    n = sum(q.shape[0] for q in queries)
    s = sum(p.shape[0] for p in pairs)
    return pl.pallas_call(
        functools.partial(forward_kernel, len(queries), len(pairs)),
        name="attend_forward",
        in_specs=[pl.BlockSpec(memory_space=SMEM)] * 2
        + [pl.BlockSpec(memory_space=VM)] * (len(queries) + len(pairs)),
        out_specs=[pl.BlockSpec(memory_space=VM)] * (TP + 5),
        out_shape=[jax.ShapeDtypeStruct((n // TP // 2, 2 * HC), BF16)] * TP
        + [
            jax.ShapeDtypeStruct((HC, n), F32),
            jax.ShapeDtypeStruct((8, n), F32),
            jax.ShapeDtypeStruct((WIDE, n), BF16),
            jax.ShapeDtypeStruct((s, WIDE), BF16),
            jax.ShapeDtypeStruct((WIDE, s), BF16),
        ],
        scratch_shapes=[
            pltpu.VMEM((n, LANES), BF16),
            pltpu.VMEM((LANES, GROUP), F32),
        ],
        cost_estimate=cost(36),
    )(dealt, bounds, *queries, *pairs)


def backward_kernel(h, dealt_ref, bound_ref, qt_ref, kv_ref, kt_ref, ot_ref, lse_ref, *refs):
    do_refs = refs[:TP]
    dq_ref, own_ref, other_ref, qd_ref, qdt_ref, acc_ref, sum_ref = refs[TP:]
    n = dq_ref.shape[0]
    sum_ref[...] = jnp.zeros_like(sum_ref)
    qd_ref[...] = jnp.zeros_like(qd_ref)
    qdt_ref[...] = jnp.zeros_like(qdt_ref)
    half = do_refs[0].shape[0]
    for m, ref in enumerate(do_refs):
        for j in range(2):
            block = ref[:, j * HC + h * DH : j * HC + (h + 1) * DH]
            part = slice((2 * m + j) * half, (2 * m + j + 1) * half)
            qd_ref[1, part, DH:] = block
            qdt_ref[1, DH:, part] = block.T
    qdt_ref[0] = qt_ref[...]

    def turn(i, c):
        rows = group_rows(i)
        qd_ref[0, rows, :] = qt_ref[:, rows].T
        return c

    lax.fori_loop(0, n // GROUP, turn, None)

    def one(i, c):
        group = dealt_ref[i]
        rows = group_rows(i)
        q_places, starts, low, mid = block_bounds(group, bound_ref)
        delta = jnp.sum(qdt_ref[1, DH:, rows].astype(F32) * ot_ref[:, rows], axis=0, keepdims=True)
        lse = lse_ref[h : h + 1, rows]
        acc_ref[...] = jnp.zeros_like(acc_ref)

        def visit(kg, masked):
            cols = group_rows(kg)
            kv = kv_ref[cols, :]
            s = jnp.dot(kv, qdt_ref[0, :, rows], preferred_element_type=F32)
            dp = jnp.dot(kv, qdt_ref[1, :, rows], preferred_element_type=F32)
            if masked:
                s = jnp.where(allowed_pairs(kg, q_places, starts), s, NEG)
            p = jnp.exp2(s * SCALE2 - lse)
            d = (p * (dp - delta)).astype(BF16)
            acc_ref[...] += jnp.dot(kt_ref[0:DH, cols], d, preferred_element_type=F32)
            sum_ref[cols, :] += jnp.dot(
                d, qd_ref[0, rows, :], preferred_element_type=F32
            ) + jnp.dot(p.astype(BF16), qd_ref[1, rows, :], preferred_element_type=F32)

        sweep(group, low, mid, visit)
        dq_ref[rows, :] = (acc_ref[...] * DH**-0.5).T.astype(BF16)
        return c

    lax.fori_loop(0, n // GROUP, one, None)
    lane = lax.broadcasted_iota(jnp.int32, (1, HW), 1)
    scale = jnp.where(lane < DH, DH**-0.5, 1.0)

    def store(b, c):
        own_ref[group_rows(b), :] = sum_ref[group_rows(dealt_ref[b]), :] * scale
        return c

    lax.fori_loop(0, n // GROUP, store, None)

    def other(b, c):
        source = group_rows(dealt_ref[n // GROUP + b])
        other_ref[group_rows(b), :] = (sum_ref[source, :] * scale).astype(BF16)
        return c

    lax.fori_loop(0, other_ref.shape[0] // GROUP, other, None)


def attend_backward(h, dealt, bounds, qt, kv, kvt, ot, lse, grads):
    n = ot.shape[1]
    s = kv.shape[0]
    full = pl.BlockSpec(memory_space=VM)
    return pl.pallas_call(
        functools.partial(backward_kernel, h),
        name="attend_backward",
        grid=(1,),
        in_specs=[pl.BlockSpec(memory_space=SMEM)] * 2
        + [
            pl.BlockSpec((HW, n), lambda i: (h, 0)),
            pl.BlockSpec((s, HW), lambda i: (0, h)),
            pl.BlockSpec((HW, s), lambda i: (h, 0)),
            pl.BlockSpec((DH, n), lambda i: (h, 0)),
            full,
        ]
        + [full] * TP,
        out_specs=[full] * 3,
        out_shape=[
            jax.ShapeDtypeStruct((n, DH), BF16),
            jax.ShapeDtypeStruct((n, HW), F32),
            jax.ShapeDtypeStruct((s - n, HW), BF16),
        ],
        scratch_shapes=[
            pltpu.VMEM((2, n, HW), BF16),
            pltpu.VMEM((2, HW, n), BF16),
            pltpu.VMEM((DH, GROUP), F32),
            pltpu.VMEM((s, HW), F32),
        ],
        cost_estimate=cost(19),
    )(dealt, bounds, qt, kv, kvt, ot, lse, *grads)


def finish_kernel(shifts, *refs):
    dq_refs = refs[:HPG]
    own_refs = refs[HPG : 2 * HPG]
    came_refs = refs[2 * HPG : (2 + shifts) * HPG]
    outs = refs[(2 + shifts) * HPG :]
    sums_ref = outs[TP]
    sums_ref[...] = jnp.zeros_like(sums_ref)
    size = outs[0].shape[0]
    for m in range(TP):

        def part(i, c, m=m):
            to = pl.ds(pl.multiple_of(i * 128, 128), 128)
            rows = pl.ds(pl.multiple_of(m * size + i * 128, 128), 128)
            pieces = []
            for h in range(HPG):
                value = own_refs[h][rows, :]
                for s in range(shifts):
                    value = value + came_refs[s * HPG + h][rows, :].astype(F32)
                pieces.append(value.astype(BF16))
            for h in range(HPG):
                pieces.append(dq_refs[h][rows, :])
            whole = jnp.concatenate(pieces, axis=1)
            outs[m][to, :] = whole
            sums_ref[0:1, :] += jnp.sum(whole.astype(F32), axis=0, keepdims=True)
            return c

        lax.fori_loop(0, size // 128, part, None)


def finish(dqs, owns, cames):
    n = dqs[0].shape[0]
    full = pl.BlockSpec(memory_space=VM)
    shifts = len(cames) // HPG
    return pl.pallas_call(
        functools.partial(finish_kernel, shifts),
        name="finish",
        in_specs=[full] * ((2 + shifts) * HPG),
        out_specs=[full] * (TP + 1),
        out_shape=[jax.ShapeDtypeStruct((n // TP, 3 * HC), BF16)] * TP
        + [jax.ShapeDtypeStruct((8, 3 * HC), F32)],
        cost_estimate=cost(6),
    )(*dqs, *owns, *cames)


TN = (((0,), (0,)), ((), ()))


def columns_kernel(chunks, place_ref, *refs):
    a_refs = refs[:chunks]
    g_refs = refs[chunks : chunks + TP]
    w_ref, sums_ref, norm_ref, extra_ref = refs[chunks + TP : chunks + TP + 4]
    keep_ref, send_ref, out_ref = refs[chunks + TP + 4 :]
    width = 3 * HC
    at = 0
    size = g_refs[0].shape[0]
    spans = []
    for ref in a_refs:
        for first in range(0, ref.shape[0], size):
            spans.append((ref, first))
    for m, (ref, first) in enumerate(spans):
        value = lax.dot_general(
            ref[first : first + size, :], g_refs[m][...], TN, preferred_element_type=F32
        )
        if m:
            out_ref[:, :width] += value
        else:
            out_ref[:, :width] = value
    sums = sums_ref[0:1, :]
    weight = w_ref[...].astype(F32)
    lane = lax.broadcasted_iota(jnp.int32, (1, 64), 1)
    plain = (out_ref[:, :width] - norm_ref[:, 1:2] * sums) / norm_ref[:, 0:1]
    gain = jnp.sum(plain * weight, axis=1, keepdims=True)
    shift = jnp.sum(weight * sums, axis=1, keepdims=True)
    out_ref[:, width:] = (
        extra_ref[...] + jnp.where(lane == 0, gain, 0.0) + jnp.where(lane == 1, shift, 0.0)
    )
    turned = sums_ref[...].T
    query = turned[WIDE:, 0:1]
    value = jnp.concatenate(
        [turned[h * HW + DH : (h + 1) * HW, 0:1] for h in range(HPG)], axis=0
    )
    own = pl.ds(pl.multiple_of(place_ref[0] * HC, HC), HC)
    out_ref[own, width:] += jnp.where(lane == 4, query, 0.0) + jnp.where(lane == 5, value, 0.0)
    half = HC // 2
    for g in range(TP):
        mine = pl.multiple_of(g * HC + place_ref[1] * half, half)
        other = pl.multiple_of(g * HC + (1 - place_ref[1]) * half, half)
        keep_ref[g] = out_ref[pl.ds(mine, half), :]
        send_ref[g] = out_ref[pl.ds(other, half), :]


def columns(place, normed, grads, weight, sums, norm_columns, extra):
    full = pl.BlockSpec(memory_space=VM)
    out = jax.ShapeDtypeStruct((TP, HC // 2, 3 * HC + 64), F32)
    return pl.pallas_call(
        functools.partial(columns_kernel, len(normed)),
        name="columns",
        in_specs=[pl.BlockSpec(memory_space=SMEM)] + [full] * (len(normed) + TP + 4),
        out_specs=[full] * 2,
        out_shape=[out, out],
        scratch_shapes=[pltpu.VMEM((D, 3 * HC + 64), F32)],
        cost_estimate=cost(8),
    )(place, *normed, *grads, weight, sums, norm_columns, extra)


def weight_grads_kernel(
    place_ref,
    u_ref,
    datt_ref,
    a2_ref,
    df_ref,
    u2_ref,
    dz_ref,
    keep_ref,
    send_ref,
    back_ref,
    in_ref,
    out_ref,
    sems,
):
    hg = place_ref[0]
    qs = place_ref[1]

    def each(source, k, rows, sem, act):
        block = (k // 2) ^ hg
        to = pl.ds(rows, source.shape[0])
        kept = k % 2 == qs
        pl.when(kept)(lambda: act(pltpu.make_async_copy(source, keep_ref.at[block, to], sem)))
        pl.when(jnp.logical_not(kept))(
            lambda: act(pltpu.make_async_copy(source, send_ref.at[block, to], sem))
        )

    def start(source, k, rows, sem):
        each(source, k, rows, sem, lambda copy: copy.start())

    def wait(source, k, rows, sem):
        each(source, k, rows, sem, lambda copy: copy.wait())

    def back_block(k):
        return back_ref.at[pl.ds(pl.multiple_of(k * 384, 384), 384)]

    def in_block(k, j):
        return in_ref.at[j, pl.ds(pl.multiple_of(k * 96, 96), 96)]

    def out_block(k):
        at = ((k // 2) ^ hg) * 192 + (k % 2) * 96
        return out_ref.at[pl.ds(pl.multiple_of(at, 96), 96)]

    def back(k, c):
        lanes = pl.ds(pl.multiple_of(k * 384, 384), 384)
        back_ref[pl.ds(pl.multiple_of(k * 384, 384), 384), :] = lax.dot_general(
            u2_ref[:, lanes], dz_ref[...], TN, preferred_element_type=F32
        ).astype(BF16)
        start(back_block(k), k, 0, sems.at[0, k])
        return c

    lax.fori_loop(0, 8, back, None)

    def inner(j, c):
        lanes = pl.ds(pl.multiple_of(j * D, D), D)
        in_ref[j] = lax.dot_general(
            a2_ref[...], df_ref[:, lanes], TN, preferred_element_type=F32
        ).astype(BF16)
        return c

    lax.fori_loop(0, 4, inner, None)

    def send_inner(k, c):
        for j in range(4):
            start(in_block(k, j), k, 384 + 96 * j, sems.at[1 + j, k])
        return c

    lax.fori_loop(0, 8, send_inner, None)
    out_ref[...] = lax.dot_general(
        u_ref[...], datt_ref[...], TN, preferred_element_type=F32
    ).astype(BF16)

    def finish_all(k, c):
        start(out_block(k), k, 768, sems.at[5, k])
        wait(back_block(k), k, 0, sems.at[0, k])
        for j in range(4):
            wait(in_block(k, j), k, 384 + 96 * j, sems.at[1 + j, k])
        return c

    lax.fori_loop(0, 8, finish_all, None)

    def finish_out(k, c):
        wait(out_block(k), k, 768, sems.at[5, k])
        return c

    lax.fori_loop(0, 8, finish_out, None)


def weight_grads(place, u, datt, a2, df, u2, dz):
    full = pl.BlockSpec(memory_space=VM)
    out = jax.ShapeDtypeStruct((TP, 864, D), BF16)
    return pl.pallas_call(
        weight_grads_kernel,
        name="weight_grads",
        in_specs=[pl.BlockSpec(memory_space=SMEM)] + [full] * 6,
        out_specs=[pl.BlockSpec(memory_space=pl.ANY)] * 2,
        out_shape=[out, out],
        scratch_shapes=[
            pltpu.VMEM((FF, D), BF16),
            pltpu.VMEM((4, D, D), BF16),
            pltpu.VMEM((D, D), BF16),
            pltpu.SemaphoreType.DMA((6, 8)),
        ],
        cost_estimate=cost(14),
    )(place, u, datt, a2, df, u2, dz)


def norm_parts(value):
    centred = value - jnp.mean(value, axis=1, keepdims=True)
    scale = lax.rsqrt(jnp.mean(centred * centred, axis=1, keepdims=True) + 1e-05)
    return centred * scale, scale


def norm_back(grad, unit, scale):
    first = jnp.mean(grad, axis=1, keepdims=True)
    second = jnp.mean(grad * unit, axis=1, keepdims=True)
    return scale * (grad - first - unit * second)


def column_sum(value):
    return jnp.sum(value, axis=0, keepdims=True)


CHUNK = 768
TILE = 256


def place_weights(place_ref, own_refs, gathered, in_ref, out_ref, back_ref):
    near, axis, axis_far, corner, corner_far = gathered
    in_ref[pl.ds(pl.multiple_of(place_ref[0] * 192, 192), 192), :] = own_refs[0][...]
    out_ref[pl.ds(pl.multiple_of(place_ref[4] * 192, 192), 192), :] = own_refs[1][...]
    back_ref[pl.ds(pl.multiple_of(place_ref[0] * D, D), D), :] = own_refs[2][...]
    sources = [
        (near, 0),
        (near, 1),
        (axis, 0),
        (axis, 1),
        (axis_far, 0),
        (axis_far, 1),
        (corner, None),
        (corner_far, None),
    ]
    for k, (ref, t) in enumerate(sources):
        c = place_ref[8 + k]
        for m in range(1, 4):
            value = ref[m - 1] if t is None else ref[t, m - 1]
            z = place_ref[m]
            cols = pl.ds(pl.multiple_of(c * 384, 384), 384)
            in_ref[pl.ds(pl.multiple_of(z * 192, 96), 96), cols] = value[0:96, 0:384]
            in_ref[pl.ds(pl.multiple_of(z * 192 + 96, 96), 96), cols] = value[0:96, 384:768]
            back_ref[pl.ds(pl.multiple_of(z * D + c * 96, 96), 96), :] = value[96:192, :]
            block = jnp.concatenate([value[192:216, 0:384], value[192:216, 384:768]], axis=0)
            at = pl.ds(pl.multiple_of(place_ref[4 + m] * 192 + (c // 2) * 48, 48), 48)
            out_ref[at, pl.ds(pl.multiple_of((c % 2) * 384, 384), 384)] = block


def middle_kernel(scattered, *refs):
    piece_refs = refs[:TP]
    x_ref, cot_ref, row_ref, wide_ref = refs[TP : TP + 4]
    refs = refs[TP + 4 :]
    if scattered:
        place_ref = refs[0]
        own_refs, gathered, refs = refs[1:4], refs[4:9], refs[9:]
        out_w_ref, in_w_ref, back_w_ref = refs[-3:]
        place_weights(place_ref, own_refs, gathered, in_w_ref, out_w_ref, back_w_ref)
        refs = refs[:-3]
    else:
        in_w_ref, out_w_ref, back_w_ref = refs[:3]
        refs = refs[3:]
    do_refs = refs[:TP]
    (
        mixed_ref,
        u_ref,
        a2_ref,
        u2_ref,
        df_ref,
        datt_ref,
        dx_ref,
        narrow_ref,
        broad_ref,
        ctx_ref,
        do_ref,
        g_ref,
        slope_ref,
        d_ref,
        da_ref,
        x1_ref,
    ) = refs[TP:]
    half = piece_refs[0].shape[0]
    for m, ref in enumerate(piece_refs):
        for j in range(2):
            ctx_ref[j * half : (j + 1) * half, m * HC : (m + 1) * HC] = ref[
                :, j * HC : (j + 1) * HC
            ]
    narrow_ref[...] = jnp.zeros_like(narrow_ref)
    broad_ref[...] = jnp.zeros_like(broad_ref)

    def tile(i, c):
        rows = pl.ds(pl.multiple_of(i * TILE, TILE), TILE)
        unit_one, scale_one = norm_parts(ctx_ref[rows, :].astype(F32))
        u = (unit_one * row_ref[0:1, :] + row_ref[1:2, :]).astype(BF16)
        u_ref[rows, :] = u
        x1 = (
            x_ref[rows, :].astype(F32)
            + jnp.dot(u, out_w_ref[...], preferred_element_type=F32)
            + row_ref[2:3, :]
        )
        x1_ref[...] = x1
        unit_two, scale_two = norm_parts(x1)
        a2 = (unit_two * row_ref[3:4, :] + row_ref[4:5, :]).astype(BF16)
        a2_ref[rows, :] = a2

        def lanes_of(j):
            return pl.ds(pl.multiple_of(j * CHUNK, CHUNK), CHUNK)

        def up(j, total):
            lanes = lanes_of(j)
            f = (
                jnp.dot(a2_ref[rows, :], in_w_ref[:, lanes], preferred_element_type=F32)
                + wide_ref[0:1, lanes]
            )
            cdf = 0.5 * (1.0 + lax.erf(f * 0.7071067811865476))
            pdf = jnp.exp(-0.5 * f * f) * 0.3989422804014327
            slope_ref[:, lanes] = cdf + f * pdf
            g = f * cdf
            g_ref[:, lanes] = g
            return total + jnp.sum(g, axis=1, keepdims=True)

        average = lax.fori_loop(0, FF // CHUNK, up, jnp.zeros((TILE, 1), F32)) / FF

        def spread(j, total):
            lanes = lanes_of(j)
            centred = g_ref[:, lanes] - average
            return total + jnp.sum(centred * centred, axis=1, keepdims=True)

        variance = lax.fori_loop(0, FF // CHUNK, spread, jnp.zeros((TILE, 1), F32)) / FF
        scale = lax.rsqrt(variance + 1e-05)

        def turn(j, carry):
            first, second = carry
            lanes = lanes_of(j)
            unit = (g_ref[:, lanes] - average) * scale
            g_ref[:, lanes] = unit
            gain = wide_ref[1:2, lanes]
            u2_ref[rows, lanes] = (unit * gain + wide_ref[2:3, lanes]).astype(BF16)
            du2 = lax.dot_general(
                cot_ref[rows, :], back_w_ref[lanes, :], NT, preferred_element_type=F32
            )
            broad_ref[0:1, lanes] += column_sum(du2 * unit)
            broad_ref[2:3, lanes] += column_sum(du2)
            grad = du2 * gain
            d_ref[:, lanes] = grad
            return (
                first + jnp.sum(grad, axis=1, keepdims=True),
                second + jnp.sum(grad * unit, axis=1, keepdims=True),
            )

        none = jnp.zeros((TILE, 1), F32)
        first, second = lax.fori_loop(0, FF // CHUNK, turn, (none, none))
        first = first / FF
        second = second / FF
        da_ref[...] = jnp.zeros_like(da_ref)

        def down(j, c):
            lanes = lanes_of(j)
            grad = scale * (d_ref[:, lanes] - first - g_ref[:, lanes] * second)
            df = (grad * slope_ref[:, lanes]).astype(BF16)
            df_ref[rows, lanes] = df
            broad_ref[1:2, lanes] += column_sum(df.astype(F32))
            da_ref[...] += lax.dot_general(
                df, in_w_ref[:, lanes], NT, preferred_element_type=F32
            )
            return c

        lax.fori_loop(0, FF // CHUNK, down, None)
        da2 = da_ref[...]
        unit_two, scale_two = norm_parts(x1_ref[...])
        narrow_ref[2:3, :] += column_sum(da2 * unit_two)
        narrow_ref[3:4, :] += column_sum(da2)
        cot = cot_ref[rows, :].astype(F32)
        dx = cot + norm_back(da2 * row_ref[3:4, :], unit_two, scale_two)
        dx_ref[rows, :] = dx
        datt = dx.astype(BF16)
        datt_ref[rows, :] = datt
        narrow_ref[4:5, :] += column_sum(datt.astype(F32))
        narrow_ref[5:6, :] += column_sum(cot)
        du = lax.dot_general(datt, out_w_ref[...], NT, preferred_element_type=F32)
        unit_one, scale_one = norm_parts(ctx_ref[rows, :].astype(F32))
        narrow_ref[0:1, :] += column_sum(du * unit_one)
        narrow_ref[1:2, :] += column_sum(du)
        do_ref[rows, :] = norm_back(du * row_ref[0:1, :], unit_one, scale_one).astype(BF16)
        mixed_ref[rows, :] = (
            jnp.dot(u2_ref[rows, :], back_w_ref[...], preferred_element_type=F32)
            + row_ref[5:6, :]
            + x1_ref[...]
        ).astype(BF16)
        return c

    lax.fori_loop(0, ctx_ref.shape[0] // TILE, tile, None)
    for m, ref in enumerate(do_refs):
        lanes = slice(m * HC, (m + 1) * HC)
        ref[...] = jnp.concatenate([do_ref[:half, lanes], do_ref[half:, lanes]], axis=1)


def middle(pieces, x, cot, narrow, wide, weights):
    n = x.shape[0]
    full = pl.BlockSpec(memory_space=VM)
    shape = jax.ShapeDtypeStruct
    scattered = len(weights) > 3
    weight_specs = [full] * len(weights)
    if scattered:
        weight_specs[0] = pl.BlockSpec(memory_space=SMEM)
    return pl.pallas_call(
        functools.partial(middle_kernel, scattered),
        name="middle",
        in_specs=[full] * (TP + 4) + weight_specs,
        out_specs=[full] * (TP + 9),
        out_shape=[shape(p.shape, BF16) for p in pieces]
        + [
            shape((n, D), BF16),
            shape((n, D), BF16),
            shape((n, D), BF16),
            shape((n, FF), BF16),
            shape((n, FF), BF16),
            shape((n, D), BF16),
            shape((n, D), F32),
            shape((8, D), F32),
            shape((8, FF), F32),
        ],
        scratch_shapes=[
            pltpu.VMEM((n, D), BF16),
            pltpu.VMEM((n, D), BF16),
            pltpu.VMEM((TILE, FF), F32),
            pltpu.VMEM((TILE, FF), F32),
            pltpu.VMEM((TILE, FF), F32),
            pltpu.VMEM((TILE, D), F32),
            pltpu.VMEM((TILE, D), F32),
        ]
        + ([pltpu.VMEM(s, BF16) for s in ((D, D), (D, FF), (FF, D))] if scattered else []),
        cost_estimate=cost(36),
    )(*pieces, x, cot, narrow, wide, *weights)


def layer_norm(values, gain, shift):
    average = jnp.mean(values, axis=-1, keepdims=True)
    centred = values - average
    variance = jnp.mean(centred * centred, axis=-1, keepdims=True)
    return centred * lax.rsqrt(variance + 1e-05) * gain + shift


def outer_sum(left, right):
    return lax.dot_general(left, right, (((0,), (0,)), ((), ())), preferred_element_type=F32)


def times_transposed(left, matrix):
    return lax.dot_general(left, matrix, (((1,), (1,)), ((), ())), preferred_element_type=F32)


def tie(value, *before):
    return lax.optimization_barrier((value, before))[0]


def pick(array, index, axis=0):
    return lax.dynamic_index_in_dim(array, index, axis, keepdims=False)


def make_local(ctx_size, fsdp_size):
    nq = ctx_size // TP
    fast = ctx_size == 8 and fsdp_size == 4

    def over_heads(value, mask):
        return lax.ppermute(
            value, "ctx", [(i, ((i // nq) ^ mask) * nq + i % nq) for i in range(ctx_size)]
        )

    def over_rows(value, shift):
        return lax.ppermute(
            value,
            "ctx",
            [(i, (i // nq) * nq + (i % nq - shift) % nq) for i in range(ctx_size)],
        )

    def over_fsdp(value, mask):
        return lax.ppermute(value, "fsdp", [(i, i ^ mask) for i in range(fsdp_size)])

    def over_split(value, masks):
        return lax.ppermute(
            value,
            "ctx",
            [(i, ((i // nq) ^ masks[i % nq]) * nq + i % nq) for i in range(ctx_size)],
        )

    moves = (over_heads, over_rows, over_fsdp, over_split)

    def exchange_heads(own, halves):
        one = over_heads(own, 1)
        two = over_heads(own, 2)
        first, second = halves
        low = over_heads(first(one), 2)
        high = over_heads(second(two), 1)
        return one, two, low, high

    def local(
        tokens,
        cotangent,
        lengths,
        dealing,
        qkv_weight,
        out_weight,
        in_weight,
        back_weight,
        norm_gains,
        shifts,
        ffn_gain,
        ffn_shifts,
    ):
        ctx = lax.axis_index("ctx")
        fs = lax.axis_index("fsdp")
        hg = ctx // nq
        qs = ctx % nq
        rows = tokens.shape[1]
        shard = qkv_weight.shape[0]
        deal_row = dealing[0]
        group_count = deal_row.shape[0]
        per = rows // GROUP
        bounds = jnp.cumsum(lengths[0])
        members = [
            [((hg ^ m) * nq + (qs + s) % nq) * per + j for m in range(TP) for j in range(per)]
            for s in range(nq)
        ]
        stored = jnp.stack([g for part in members for g in part]).astype(jnp.int32)
        onehot = (stored[:, None] == jnp.arange(group_count, dtype=jnp.int32)[None, :]).astype(
            jnp.int32
        )
        dealt = jnp.sum(onehot * deal_row[None, :], axis=1)
        mine = tokens[0]
        half = rows // 2
        one, two, low, high = exchange_heads(mine, (lambda a: a[:half], lambda a: a[half:]))
        chunks = (mine, one, two, low, high)

        def own_columns(weight):
            def take(at, size):
                value = weight[:, at : at + size]
                for g in range(1, TP):
                    other = weight[:, at + g * HC : at + g * HC + size]
                    value = jnp.where(hg == g, other, value)
                return value

            out = []
            for h in range(HPG):
                out += [take(D + h * DH, DH), take(2 * D + h * DH, DH)]
            return jnp.concatenate(out + [take(0, HC)], axis=1)

        feature = norm_gains.shape[1]
        narrow_rows = jnp.concatenate([norm_gains, shifts], axis=0)
        broad_rows = jnp.concatenate([ffn_gain[None], ffn_shifts], axis=0).reshape(12, feature)
        small = jnp.concatenate(
            [
                jnp.pad(narrow_rows, ((0, 6), (0, HC - feature))),
                jnp.pad(broad_rows, ((0, 4), (0, 2 * HC - feature))),
            ],
            axis=1,
        )
        packed = jnp.concatenate([own_columns(qkv_weight), small], axis=0)
        span = packed.shape[0] // nq
        piece = pick(packed.reshape(nq, span, 3 * HC), qs)
        came = [over_fsdp(piece, m) for m in range(1, fsdp_size)]
        parts = jnp.stack([piece] + came)
        shared = [over_rows(parts, s) for s in range(1, nq)]
        parts = jnp.stack([parts] + shared)
        ordered = [
            jnp.concatenate([pick(pick(parts, (h - qs) % nq), f ^ fs) for h in range(nq)], axis=0)
            for f in range(fsdp_size)
        ]
        w_own = jnp.concatenate([p[:shard] for p in ordered], axis=0)
        tails = [p[shard:] for p in ordered]
        narrow_all = jnp.concatenate([p[:10, :feature] for p in tails], axis=1).astype(F32)
        broad_all = jnp.concatenate(
            [p[:12, HC : HC + feature].reshape(3, -1) for p in tails], axis=1
        ).astype(F32)
        gains = narrow_all[:3]
        shift_rows = narrow_all[3:]
        ffn_scale = broad_all[0]
        ffn_shift_rows = broad_all[1:]

        if fast:
            gathered = gather_weights(
                in_weight, back_weight, out_weight, shared, (low, high), hg, qs, moves
            )
        else:
            in_w = lax.all_gather(in_weight, "fsdp", axis=0, tiled=True)
            back_w = lax.all_gather(back_weight, "fsdp", axis=0, tiled=True)
            out_w = lax.all_gather(out_weight, "fsdp", axis=0, tiled=True)
            out_blocks = out_w.reshape(TP, HC, D)
            out_rel = jnp.concatenate([pick(out_blocks, hg ^ m) for m in range(TP)], axis=0)

        def own_heads(row):
            return pick(row.reshape(TP, HC), hg)

        value_bias = own_heads(shift_rows[2]).reshape(HPG, DH)
        bias = jnp.concatenate(
            [
                jnp.stack([jnp.zeros((HPG, DH), F32), value_bias], axis=1).reshape(-1),
                own_heads(shift_rows[1]),
            ]
        )[None]
        norm_rows = jnp.stack([gains[0], shift_rows[0]])
        projected = [
            project(c, w_own, norm_rows, bias) for c in ((mine, one, two), (low, high))
        ]
        normed = [p[0] for p in projected]
        queries = [p[1] for p in projected]
        pairs = [p[2] for p in projected]
        for s in range(1, nq):
            pairs = pairs + [over_rows(p[2], s) for p in projected]
        if fast:
            dealt = tie(dealt, gathered[0])

        *context_parts, context_t, log_total, q_turned, kv_rows, kv_turned = attend_forward(
            dealt, bounds, queries, pairs
        )
        if fast:
            gathered = gather_rest(*gathered, log_total, moves)

        got = [context_parts[0]] + [over_heads(context_parts[m], m) for m in range(1, TP)]

        def relative(row):
            blocks = row.reshape(TP, HC)
            return jnp.concatenate([pick(blocks, hg ^ m) for m in range(TP)])

        narrow = jnp.stack(
            [relative(gains[1]), relative(shift_rows[3]), shift_rows[4], gains[2], shift_rows[5]]
            + [shift_rows[6]] * 3
        )
        wide = jnp.pad(
            jnp.stack([ffn_shift_rows[0], ffn_scale, ffn_shift_rows[1]]), ((0, 5), (0, 0))
        )
        cot = cotangent[0]
        if fast:
            weights = (weight_places(hg, qs, fs), in_weight, out_weight, back_weight, *gathered)
            w_axis = gather_columns(w_own, got, moves)
        else:
            weights = (in_w, out_rel, back_w)
        (
            *sent,
            mixed_out,
            inner_low,
            normed_two_low,
            inner_two_low,
            hidden_low,
            branch_low,
            grad_middle,
            narrow_sums,
            broad_sums,
        ) = middle(got, mine, cot, narrow, wide, weights)
        grad_gain_one, grad_shift_three, grad_gain_two, grad_shift_five = narrow_sums[:4]
        grad_out_bias, grad_back_bias = narrow_sums[4:6]
        grad_ffn_gain, grad_in_bias, grad_ffn_shift = broad_sums[:3]

        grad_rows = [sent[0]] + [over_heads(sent[m], m) for m in range(1, TP)]
        set_rows = TP * rows
        place = jnp.stack([hg, qs, fs]).astype(jnp.int32)
        if fast:
            keep, send = weight_grads(
                tie(place, w_axis), inner_low, branch_low, normed_two_low, hidden_low, inner_two_low, cot
            )
            stage = first_stage(keep, send, moves)

        def backward_of(h, table):
            return attend_backward(
                h, table, bounds, q_turned, kv_rows, kv_turned, context_t, log_total, grad_rows
            )

        def exchange(other):
            return [
                over_rows(other[(s - 1) * set_rows : s * set_rows], nq - s) for s in range(1, nq)
            ]

        table = tie(dealt, keep) if fast else dealt
        results = [backward_of(0, table)]
        cames = [exchange(results[0][2])]
        for h in range(1, HPG):
            table = dealt
            if fast and h == 1:
                table = tie(dealt, results[0], stage)
                corners = gather_corners(tie(w_axis, results[0]), qs, moves)
            elif fast:
                w_parts = select_columns(w_axis, corners, qs, moves)
                table = tie(dealt, results[h - 1], w_parts)
            results.append(backward_of(h, table))
            cames.append(exchange(results[h][2]))
        if fast:
            second = second_stage(stage, results[-1], moves)
            cames = tie(cames, second)
        came = [cames[h][s] for s in range(nq - 1) for h in range(HPG)]
        *grads, sums = finish([r[0] for r in results], [r[1] for r in results], came)

        back_parts = [grads[0]] + [over_heads(grads[m], m) for m in range(1, TP)]
        if not fast:
            w_one, w_two, w_low, w_high = exchange_heads(
                w_own, (lambda a: a[: D // 2], lambda a: a[D // 2 :])
            )
            w_parts = (w_one, w_two, jnp.concatenate([w_low, w_high], axis=0))
        grad_normed = sum(
            times_transposed(g, w) for g, w in zip(back_parts, (w_own,) + tuple(w_parts))
        )
        inputs = mine.astype(F32)
        first_pull = jax.vjp(layer_norm, inputs, gains[0], shift_rows[0])[1]
        grad_inputs_part, grad_gain_zero, grad_shift_zero = first_pull(grad_normed)
        input_grad = grad_middle + grad_inputs_part

        def absolute(row):
            blocks = row.reshape(TP, HC)
            return jnp.concatenate([pick(blocks, hg ^ m) for m in range(TP)])

        order = ctx * fsdp_size + fs
        total_devices = ctx_size * fsdp_size
        if fast:
            zero = jnp.zeros((D,), F32)
            narrow = [
                zero,
                zero,
                absolute(grad_gain_one),
                grad_gain_two,
                zero,
                zero,
                absolute(grad_shift_three),
                grad_out_bias,
                grad_shift_five,
                grad_back_bias,
            ]
            broad = [
                v.reshape(total_devices, 4, D // total_devices).transpose(1, 0, 2).reshape(4, D)
                for v in (grad_ffn_gain, grad_in_bias, grad_ffn_shift)
            ]
            extra = jnp.concatenate(
                [jnp.stack(narrow)] + broad + [jnp.zeros((42, D), F32)], axis=0
            ).T
            norm_columns = jnp.pad(norm_rows, ((0, 6), (0, 0))).T
            kept, sent_columns = columns(
                place, normed, grads, w_own, sums, norm_columns, extra
            )
            qkv_out, tail = reduce_columns(kept, sent_columns, hg, fs, moves)
            turned = tail.T
            small_out = (
                jnp.stack([turned[0], turned[2], turned[3]]),
                jnp.concatenate([turned[1:2], turned[4:10]], axis=0),
                turned[10:14].reshape(-1),
                turned[14:22].reshape(2, -1),
            )
            back_out, in_out, out_out = later_stages(second, fs, moves)
        else:

            def placed(row):
                blank = jnp.zeros((TP, HC), F32)
                return lax.dynamic_update_slice(blank, row[None], (hg, 0)).reshape(-1)

            row = sums[0]
            value_sums = row[:WIDE].reshape(HPG, 2, DH)[:, 1].reshape(-1)
            small_terms = jnp.concatenate(
                [
                    grad_gain_zero,
                    absolute(grad_gain_one),
                    grad_gain_two,
                    grad_shift_zero,
                    placed(row[WIDE:]),
                    placed(value_sums),
                    absolute(grad_shift_three),
                    grad_out_bias,
                    grad_shift_five,
                    grad_back_bias,
                    grad_ffn_gain,
                    grad_in_bias,
                    grad_ffn_shift,
                ]
            )
            axes = ("ctx", "fsdp")
            small_terms = lax.psum(small_terms, axes)
            narrow = small_terms[: 10 * D].reshape(10, total_devices, D // total_devices)
            narrow = pick(narrow, order, 1)
            broad = small_terms[10 * D :].reshape(3, total_devices, FF // total_devices)
            broad = pick(broad, order, 1)
            small_out = (narrow[:3], narrow[3:], broad[0], broad[1:])
            blocks = outer_sum(inner_low, branch_low).reshape(TP, HC, D)
            grad_out_w = jnp.concatenate([pick(blocks, hg ^ m) for m in range(TP)], axis=0)
            grad_in_w = outer_sum(normed_two_low, hidden_low)
            grad_back_w = outer_sum(inner_two_low, cot)
            back_out, in_out, out_out = (
                lax.psum_scatter(g.astype(BF16), axes, scatter_dimension=0, tiled=True).astype(F32)
                for g in (grad_back_w, grad_in_w, grad_out_w)
            )
            grad_qkv_w = outer_sum(jnp.concatenate(normed, axis=0), jnp.concatenate(grads, axis=0))
            pairs_w = grad_qkv_w[:, :WIDE].reshape(D, HPG, 2, DH)
            three = jnp.stack(
                [
                    grad_qkv_w[:, WIDE:],
                    pairs_w[:, :, 0].reshape(D, HC),
                    pairs_w[:, :, 1].reshape(D, HC),
                ],
                axis=1,
            )
            blank = jnp.zeros((D, 3, TP, HC), BF16)
            whole = lax.dynamic_update_slice(
                blank, three.astype(BF16)[:, :, None], (0, 0, hg, 0)
            ).reshape(D, 3 * D)
            qkv_out = lax.psum_scatter(whole, axes, scatter_dimension=0, tiled=True).astype(F32)
        return (
            mixed_out[None],
            input_grad[None],
            qkv_out,
            out_out,
            in_out,
            back_out,
        ) + small_out

    return local


def gather_weights(in_weight, back_weight, out_weight, first, then, hg, qs, moves):
    over_heads, over_rows, over_fsdp, over_split = moves
    c = hg * 2 + qs
    cut = lax.dynamic_slice(in_weight, (0, c * 384), (192, 384))
    out_cut = lax.dynamic_slice(out_weight, (hg * 48, qs * 384), (48, 384))
    piece = jnp.concatenate(
        [
            jnp.concatenate([cut[:96], cut[96:]], axis=1),
            pick(back_weight.reshape(8, 96, D), c),
            jnp.concatenate([out_cut[:24], out_cut[24:]], axis=1),
        ],
        axis=0,
    )
    piece = tie(piece, *first)
    foreign = jnp.stack([over_fsdp(piece, m) for m in (1, 2, 3)])
    near = jnp.stack([foreign, over_rows(foreign, 1)])
    return near, over_split(tie(near, *then), (1, 2))


def gather_rest(near, axis, before, moves):
    over_heads, over_rows, over_fsdp, over_split = moves
    axis = tie(axis, before)
    corner = over_split(axis[0], (2, 1))
    return near, axis, over_rows(axis, 1), corner, over_rows(corner, 1)


def weight_places(hg, qs, fs):
    near_x = jnp.where(qs == 0, 1, 2)
    far_x = 3 - near_x
    return jnp.stack(
        [fs ^ m for m in range(4)]
        + [fs ^ m ^ hg for m in range(4)]
        + [hg * 2 + qs, hg * 2 + 1 - qs]
        + [(hg ^ near_x) * 2 + qs, (hg ^ near_x) * 2 + 1 - qs]
        + [(hg ^ far_x) * 2 + 1 - qs, (hg ^ far_x) * 2 + qs]
        + [(hg ^ 3) * 2 + qs, (hg ^ 3) * 2 + 1 - qs]
    ).astype(jnp.int32)


def gather_columns(weight, before, moves):
    over_heads, over_rows, over_fsdp, over_split = moves
    return over_split(tie(weight, before), (1, 2))


def gather_corners(axis, qs, moves):
    over_heads, over_rows, over_fsdp, over_split = moves
    return over_split(pick(axis.reshape(2, D // 2, -1), qs), (2, 1))


def select_columns(axis, corner, qs, moves):
    over_heads, over_rows, over_fsdp, over_split = moves
    axis_far = over_rows(axis, 1)
    corner_far = over_rows(corner, 1)
    even = qs == 0
    one = jnp.where(even, axis, axis_far)
    two = jnp.where(even, axis_far, axis)
    three = jnp.concatenate(
        [jnp.where(even, corner, corner_far), jnp.where(even, corner_far, corner)], axis=0
    )
    return one, two, three


CUT = 432


def first_stage(keep, send, moves):
    over_heads, over_rows, over_fsdp, over_split = moves
    came = over_rows(send, 1)

    def added(block, rows):
        return (keep[block, rows].astype(F32) + came[block, rows].astype(F32)).astype(BF16)

    top = slice(0, CUT)
    bottom = slice(CUT, 2 * CUT)
    first_send = jnp.stack([added(1, top), added(3, top)])
    first_keep = jnp.stack([added(0, top), added(2, top)])
    second_send = jnp.stack([added(2, bottom), added(3, bottom)])
    second_keep = jnp.stack([added(0, bottom), added(1, bottom)])
    return first_send, first_keep, second_send, second_keep


def added(mine, came):
    return (mine.astype(F32) + came.astype(F32)).astype(BF16)


def second_stage(stage, before, moves):
    over_heads, over_rows, over_fsdp, over_split = moves
    first_send, first_keep, second_send, second_keep = stage
    first_keep, second_keep = tie((first_keep, second_keep), before)
    first_came = over_heads(first_send, 1)
    second_came = over_heads(second_send, 2)
    return (
        added(first_keep[0], first_came[0]),
        added(first_keep[1], first_came[1]),
        added(second_keep[0], second_came[0]),
        added(second_keep[1], second_came[1]),
    )


def later_stages(stage, fs, moves):
    over_heads, over_rows, over_fsdp, over_split = moves
    first, first_send, second, second_send = stage
    first_last = over_heads(first_send, 2)
    second_last = over_heads(second_send, 1)
    whole = jnp.concatenate([added(first, first_last), added(second, second_last)], axis=0)
    back = whole[:384].reshape(4, 96, D)
    inner = whole[384:768].reshape(4, 4, 24, D)
    out = whole[768:].reshape(4, 24, D)

    def piece(f):
        return jnp.concatenate(
            [pick(back, f), pick(inner, f, 1).reshape(96, D), pick(out, f)], axis=0
        )

    total = piece(fs).astype(F32)
    for m in (1, 2, 3):
        total = total + over_fsdp(piece(fs ^ m), m).astype(F32)
    inner = jnp.concatenate([total[96 + 24 * j : 120 + 24 * j] for j in range(4)], axis=1)
    return total[:96], inner, total[192:216]


def reduce_columns(keep, send, hg, fs, moves):
    over_heads, over_rows, over_fsdp, over_split = moves
    kept = keep + over_rows(send, 1)
    kept = kept.reshape(TP, 4, 24, 640)
    low = kept.astype(BF16)
    total = pick(kept, fs, 1)
    for m in (1, 2, 3):
        total = total + over_fsdp(pick(low, fs ^ m, 1), m).astype(F32)
    mine = jnp.stack(
        [pick(total, hg)] + [over_heads(pick(total, hg ^ m), m) for m in (1, 2, 3)]
    )
    tail = jnp.sum(mine[:, :, 3 * HC :], axis=0)
    mine = [pick(mine, hg ^ g) for g in range(TP)]
    out = [block[:, WIDE : 3 * HC] for block in mine]
    for part in range(2):
        for block in mine:
            for h in range(HPG):
                at = h * HW + part * DH
                out.append(block[:, at : at + DH])
    return jnp.concatenate(out, axis=1), tail


def solution(mesh):
    ctx_size = mesh.shape["ctx"]
    fsdp_size = mesh.shape["fsdp"]
    in_specs = (
        P("fsdp", "ctx", None),
        P("fsdp", "ctx", None),
        P("fsdp", None),
        P("fsdp", None),
        P("fsdp", None),
        P("fsdp", None),
        P("fsdp", None),
        P("fsdp", None),
        P(None, "fsdp"),
        P(None, "fsdp"),
        P("fsdp"),
        P(None, "fsdp"),
    )
    out_specs = (
        P("fsdp", "ctx", None),
        P("fsdp", "ctx", None),
        P(("ctx", "fsdp"), None),
        P(("ctx", "fsdp"), None),
        P(("ctx", "fsdp"), None),
        P(("ctx", "fsdp"), None),
        P(None, ("ctx", "fsdp")),
        P(None, ("ctx", "fsdp")),
        P(("ctx", "fsdp")),
        P(None, ("ctx", "fsdp")),
    )
    return jax.shard_map(
        make_local(ctx_size, fsdp_size),
        mesh=mesh,
        in_specs=in_specs,
        out_specs=out_specs,
        check_vma=False,
    )
```

```python
import functools

import jax
import jax.numpy as jnp
from jax import lax
from jax.experimental import pallas as pl
from jax.experimental.pallas import tpu as pltpu
from jax.sharding import PartitionSpec as P

D = 768
H = 12
DH = 64
FF = 3072
GROUP = 256
HPG = 3
TP = H // HPG
HC = HPG * DH
LANES = 256
SCALE2 = 1.4426950408889634 * DH ** -0.5
NEG = -1e30
NT = (((1,), (1,)), ((), ()))
F32 = jnp.float32
BF16 = jnp.bfloat16

SMEM = pltpu.MemorySpace.SMEM
VM = pltpu.MemorySpace.VMEM
HW = 2 * DH
WIDE = HPG * HW


def cost(us):
    return pl.CostEstimate(flops=int(us * 4.4e9), transcendentals=0, bytes_accessed=100000)


def block_bounds(group, bound_ref):
    lane = lax.broadcasted_iota(jnp.int32, (1, GROUP), 1)
    q_places = group * GROUP + lane
    starts = jnp.zeros((1, GROUP), jnp.int32)
    first = jnp.int32(0)
    last = jnp.int32(0)
    for j in range(bound_ref.shape[0]):
        b = bound_ref[j]
        starts = jnp.where(q_places >= b, b, starts)
        first = jnp.where(group * GROUP >= b, b, first)
        last = jnp.where(group * GROUP + GROUP - 1 >= b, b, last)
    low = first // GROUP
    mid = jnp.minimum(group, (last + GROUP - 1) // GROUP)
    return q_places, starts, low, mid


def sweep(group, low, mid, visit, carry):
    pairs = (group - low + 2) // 2
    plain = jnp.clip((group - 1 - mid) // 2, 0, pairs - 1)
    carry = visit(group, True, carry)
    carry = lax.fori_loop(1, 1 + plain, lambda t, c: visit(group - 2 * t, False, c), carry)
    return lax.fori_loop(1 + plain, pairs, lambda t, c: visit(group - 2 * t, True, c), carry)


def pair_rows(top):
    first = jnp.maximum(top - 1, 0)
    return first, pl.ds(pl.multiple_of(first * GROUP, GROUP), 2 * GROUP)


def allowed_pairs(first, top, q_places, starts):
    k_places = first * GROUP + lax.broadcasted_iota(jnp.int32, (2 * GROUP, 1), 0)
    return (k_places <= jnp.minimum(q_places, top * GROUP + GROUP - 1)) & (k_places >= starts)


def group_rows(index):
    return pl.ds(pl.multiple_of(index * GROUP, GROUP), GROUP)


def project_kernel(count, pieces, *refs):
    tok_refs = refs[:count]
    if pieces:
        table_ref, own_ref, far_ref, row_ref, bias_ref, a_ref, q_ref, kv_ref, w_ref = refs[count:]
        for s, ref in enumerate((own_ref, far_ref)):
            for f in range(ref.shape[0]):
                at = pl.multiple_of(table_ref[s * ref.shape[0] + f] * 96, 96)
                w_ref[pl.ds(at, 96), :] = ref[f, :96, :]
    else:
        w_ref, row_ref, bias_ref, a_ref, q_ref, kv_ref = refs[count:]
    at = 0
    for ref in tok_refs:

        def part(i, c, ref=ref, at=at):
            rows = pl.ds(pl.multiple_of(i * GROUP, GROUP), GROUP)
            to = pl.ds(pl.multiple_of(at + i * GROUP, GROUP), GROUP)
            value = ref[rows, :].astype(F32)
            centred = value - jnp.mean(value, axis=1, keepdims=True)
            variance = jnp.mean(centred * centred, axis=1, keepdims=True)
            normed = centred * lax.rsqrt(variance + 1e-05) * row_ref[0:1, :] + row_ref[1:2, :]
            normed = normed.astype(BF16)
            a_ref[to, :] = normed
            out = jnp.dot(normed, w_ref[...], preferred_element_type=F32) + bias_ref[0:1, :]
            kv_ref[to, :] = out[:, :WIDE].astype(BF16)
            none = jnp.zeros((GROUP, DH), BF16)
            heads = []
            for h in range(HPG):
                lane = WIDE + h * DH
                heads += [(out[:, lane : lane + DH] * SCALE2).astype(BF16), none]
            q_ref[to, :] = jnp.concatenate(heads, axis=1)
            return c

        lax.fori_loop(0, ref.shape[0] // GROUP, part, None)
        at += ref.shape[0]


def project(toks, weights, norm_rows, bias):
    n = sum(t.shape[0] for t in toks)
    full = pl.BlockSpec(memory_space=VM)
    pieces = len(weights) > 1
    specs = [full] * (len(toks) + len(weights) + 2)
    outs = [
        jax.ShapeDtypeStruct((n, D), BF16),
        jax.ShapeDtypeStruct((n, WIDE), BF16),
        jax.ShapeDtypeStruct((n, WIDE), BF16),
    ]
    if pieces:
        specs[len(toks)] = pl.BlockSpec(memory_space=SMEM)
        outs.append(jax.ShapeDtypeStruct((D, 3 * HC), BF16))
    return pl.pallas_call(
        functools.partial(project_kernel, len(toks), pieces),
        name="project",
        in_specs=specs,
        out_specs=[full] * len(outs),
        out_shape=outs,
        cost_estimate=cost(4 + n // 512),
    )(*toks, *weights, norm_rows, bias)


ROWS = DH + 16


def forward_kernel(chunks, key_chunks, *refs):
    dealt_ref, bound_ref = refs[:2]
    q_refs = refs[2 : 2 + chunks]
    kv_refs = refs[2 + chunks : 2 + chunks + key_chunks]
    o_refs = refs[2 + chunks + key_chunks : 2 + chunks + key_chunks + TP]
    ot_ref, lse_ref, *kept_refs = refs[2 + chunks + key_chunks + TP :]
    qt_out, kv_out, kt_out, qt_ref, kv_ref, kt_ref, vt_ref, o_ref, acc_ref, turn_ref, sems = (
        kept_refs
    )
    copies = [
        pltpu.make_async_copy(source, to, sems.at[i])
        for i, (source, to) in enumerate(((qt_ref, qt_out), (kv_ref, kv_out), (kt_ref, kt_out)))
    ]
    for h in range(HPG):
        vt_ref[h * ROWS + DH : (h + 1) * ROWS, :] = jnp.ones((16, vt_ref.shape[1]), BF16)
    at = 0
    for ref in kv_refs:

        def load(j, c, ref=ref, at=at):
            rows = group_rows(dealt_ref[at + j])
            block = ref[group_rows(j), :]
            kv_ref[rows, :] = block
            turned = block.T
            for h in range(HPG):
                kt_ref[h * DH : (h + 1) * DH, rows] = turned[h * HW : h * HW + DH, :]
                vt_ref[h * ROWS : h * ROWS + DH, rows] = turned[h * HW + DH : (h + 1) * HW, :]
            return c

        count = ref.shape[0] // GROUP
        lax.fori_loop(0, count, load, None)
        at += count
    at = 0
    for ref in q_refs:

        def turn(j, c, ref=ref, at=at):
            qt_ref[:, group_rows(at + j)] = ref[group_rows(j), :].T
            return c

        count = ref.shape[0] // GROUP
        lax.fori_loop(0, count, turn, None)
        at += count

    for copy in copies:
        copy.start()

    def one(i, c):
        group = dealt_ref[i]
        rows = group_rows(i)
        q_places, starts, low, mid = block_bounds(group, bound_ref)
        acc_ref[...] = jnp.zeros_like(acc_ref)

        def visit(top, masked, carry):
            first, cols = pair_rows(top)
            allowed = allowed_pairs(first, top, q_places, starts) if masked else None
            out = []
            for h in range(HPG):
                lanes = slice(h * HW, (h + 1) * HW)
                s = jnp.dot(kv_ref[cols, lanes], qt_ref[lanes, rows], preferred_element_type=F32)
                if masked:
                    s = jnp.where(allowed, s, NEG)
                old = carry[h]
                new = jnp.maximum(old, jnp.max(s, axis=0, keepdims=True))
                p = jnp.exp2(s - new).astype(BF16)
                part = slice(h * ROWS, (h + 1) * ROWS)
                acc_ref[part, :] = acc_ref[part, :] * jnp.exp2(old - new) + jnp.dot(
                    vt_ref[part, cols], p, preferred_element_type=F32
                )
                out.append(new)
            return tuple(out)

        start = tuple(jnp.full((1, GROUP), NEG, F32) for _ in range(HPG))
        highest = sweep(group, low, mid, visit, start)
        for h in range(HPG):
            total = acc_ref[h * ROWS + DH : h * ROWS + DH + 1, :]
            part = slice(h * DH, (h + 1) * DH)
            turn_ref[part, :] = acc_ref[h * ROWS : h * ROWS + DH, :] / total
            lse_ref[h : h + 1, rows] = highest[h] + jnp.log2(total)
        ot_ref[:, rows] = turn_ref[0:HC, :]
        o_ref[rows, :] = turn_ref[...].T.astype(BF16)
        return c

    turn_ref[...] = jnp.zeros_like(turn_ref)
    lax.fori_loop(0, o_ref.shape[0] // GROUP, one, None)
    for m, ref in enumerate(o_refs):
        half = ref.shape[0]
        low = o_ref[2 * m * half : (2 * m + 1) * half, :HC]
        high = o_ref[(2 * m + 1) * half : (2 * m + 2) * half, :HC]
        ref[...] = jnp.concatenate([low, high], axis=1)
    for copy in copies:
        copy.wait()


def attend_forward(dealt, bounds, queries, pairs):
    n = sum(q.shape[0] for q in queries)
    s = sum(p.shape[0] for p in pairs)
    return pl.pallas_call(
        functools.partial(forward_kernel, len(queries), len(pairs)),
        name="attend_forward",
        in_specs=[pl.BlockSpec(memory_space=SMEM)] * 2
        + [pl.BlockSpec(memory_space=VM)] * (len(queries) + len(pairs)),
        out_specs=[pl.BlockSpec(memory_space=VM)] * (TP + 2)
        + [pl.BlockSpec(memory_space=pl.ANY)] * 3,
        out_shape=[jax.ShapeDtypeStruct((n // TP // 2, 2 * HC), BF16)] * TP
        + [
            jax.ShapeDtypeStruct((HC, n), F32),
            jax.ShapeDtypeStruct((8, n), F32),
            jax.ShapeDtypeStruct((WIDE, n), BF16),
            jax.ShapeDtypeStruct((s, WIDE), BF16),
            jax.ShapeDtypeStruct((HC, s), BF16),
        ],
        scratch_shapes=[
            pltpu.VMEM((WIDE, n), BF16),
            pltpu.VMEM((s, WIDE), BF16),
            pltpu.VMEM((HC, s), BF16),
            pltpu.VMEM((HPG * ROWS, s), BF16),
            pltpu.VMEM((n, LANES), BF16),
            pltpu.VMEM((HPG * ROWS, GROUP), F32),
            pltpu.VMEM((LANES, GROUP), F32),
            pltpu.SemaphoreType.DMA((3,)),
        ],
        cost_estimate=cost(30),
    )(dealt, bounds, *queries, *pairs)


def backward_kernel(base, chunks, dealt_ref, bound_ref, qt_ref, kv_ref, kt_ref, ot_ref, lse_ref, *refs):
    q_refs = refs[:chunks]
    do_refs = refs[chunks : chunks + TP]
    dq_ref, own_ref, other_ref, q_ref, do_ref, dot_ref, acc_ref, sum_ref = refs[chunks + TP :]
    h = base + pl.program_id(0)
    n = dq_ref.shape[0]
    sum_ref[...] = jnp.zeros_like(sum_ref)
    at = 0
    for ref in q_refs:
        q_ref[at : at + ref.shape[0], :] = ref[...]
        at += ref.shape[0]
    half = do_refs[0].shape[0]
    none = jnp.zeros((half, DH), BF16)
    for m, ref in enumerate(do_refs):
        for j in range(2):
            block = ref[:, j * DH : (j + 1) * DH]
            part = slice((2 * m + j) * half, (2 * m + j + 1) * half)
            wide = jnp.concatenate([none, block], axis=1)
            do_ref[part, :] = wide
            dot_ref[:, part] = wide.T

    def one(i, c):
        group = dealt_ref[i]
        rows = group_rows(i)
        q_places, starts, low, mid = block_bounds(group, bound_ref)
        delta = jnp.sum(dot_ref[DH:, rows].astype(F32) * ot_ref[:, rows], axis=0, keepdims=True)
        lse = lse_ref[pl.ds(h, 1), rows]
        acc_ref[...] = jnp.zeros_like(acc_ref)

        def visit(top, masked, c):
            first, cols = pair_rows(top)
            kv = kv_ref[cols, :]
            s = jnp.dot(kv, qt_ref[:, rows], preferred_element_type=F32)
            dp = jnp.dot(kv, dot_ref[:, rows], preferred_element_type=F32)
            if masked:
                s = jnp.where(allowed_pairs(first, top, q_places, starts), s, NEG)
            p = jnp.exp2(s - lse)
            d = (p * (dp - delta)).astype(BF16)
            acc_ref[...] += jnp.dot(kt_ref[:, cols], d, preferred_element_type=F32)
            sum_ref[cols, :] += jnp.dot(
                d, q_ref[rows, :], preferred_element_type=F32
            ) + jnp.dot(p.astype(BF16), do_ref[rows, :], preferred_element_type=F32)
            return c

        sweep(group, low, mid, visit, jnp.int32(0))
        dq_ref[rows, :] = (acc_ref[...] * DH**-0.5).T.astype(BF16)
        return c

    lax.fori_loop(0, n // GROUP, one, None)
    lane = lax.broadcasted_iota(jnp.int32, (1, HW), 1)
    scale = jnp.where(lane < DH, DH**-0.5 / SCALE2, 1.0)

    def store(b, c):
        own_ref[group_rows(b), :] = sum_ref[group_rows(dealt_ref[b]), :] * scale
        return c

    lax.fori_loop(0, n // GROUP, store, None)

    def other(b, c):
        source = group_rows(dealt_ref[n // GROUP + b])
        other_ref[group_rows(b), :] = (sum_ref[source, :] * scale).astype(BF16)
        return c

    lax.fori_loop(0, other_ref.shape[0] // GROUP, other, None)


def attend_backward(base, count, dealt, bounds, queries, qt, kv, kt, ot, lse, grads):
    n = ot.shape[1]
    s = kv.shape[0]
    full = pl.BlockSpec(memory_space=VM)
    return pl.pallas_call(
        functools.partial(backward_kernel, base, len(queries)),
        name="attend_backward",
        grid=(count,),
        in_specs=[pl.BlockSpec(memory_space=SMEM)] * 2
        + [
            pl.BlockSpec((HW, n), lambda i: (base + i, 0)),
            pl.BlockSpec((s, HW), lambda i: (0, base + i)),
            pl.BlockSpec((DH, s), lambda i: (base + i, 0)),
            pl.BlockSpec((DH, n), lambda i: (base + i, 0)),
            full,
        ]
        + [pl.BlockSpec((q.shape[0], HW), lambda i: (0, base + i)) for q in queries]
        + [pl.BlockSpec((g.shape[0], HW), lambda i: (0, base + i)) for g in grads],
        out_specs=[
            pl.BlockSpec((None, n, DH), lambda i: (i, 0, 0)),
            pl.BlockSpec((None, n, HW), lambda i: (i, 0, 0)),
            pl.BlockSpec((None, s - n, HW), lambda i: (i, 0, 0)),
        ],
        out_shape=[
            jax.ShapeDtypeStruct((count, n, DH), BF16),
            jax.ShapeDtypeStruct((count, n, HW), F32),
            jax.ShapeDtypeStruct((count, s - n, HW), BF16),
        ],
        scratch_shapes=[
            pltpu.VMEM((n, HW), BF16),
            pltpu.VMEM((n, HW), BF16),
            pltpu.VMEM((HW, n), BF16),
            pltpu.VMEM((DH, GROUP), F32),
            pltpu.VMEM((s, HW), F32),
        ],
        cost_estimate=cost(16 * count),
    )(dealt, bounds, qt, kv, kt, ot, lse, *queries, *grads)


def finish_kernel(shifts, *refs):
    sets = 2 + shifts

    def heads(k):
        first, rest = refs[2 * k : 2 * k + 2]
        return [first.at[0]] + [rest.at[h] for h in range(HPG - 1)]

    dq_refs = heads(0)
    own_refs = heads(1)
    came_refs = [ref for s in range(shifts) for ref in heads(2 + s)]
    w_ref = refs[2 * sets]
    outs = refs[2 * sets + 1 :]
    sums_ref, first_send, first_keep, second_send, second_keep = outs[TP:]
    sums_ref[...] = jnp.zeros_like(sums_ref)
    size = outs[0].shape[0]
    half = size // 2
    for m in range(TP):

        def part(i, c, m=m):
            to = pl.ds(pl.multiple_of(i * 128, 128), 128)
            rows = pl.ds(pl.multiple_of(m * size + i * 128, 128), 128)
            pieces = []
            for h in range(HPG):
                value = own_refs[h][rows, :]
                for s in range(shifts):
                    value = value + came_refs[s * HPG + h][rows, :].astype(F32)
                pieces.append(value.astype(BF16))
            for h in range(HPG):
                pieces.append(dq_refs[h][rows, :])
            whole = jnp.concatenate(pieces, axis=1)
            outs[m][to, :] = whole
            sums_ref[0:1, :] += jnp.sum(whole.astype(F32), axis=0, keepdims=True)
            return c

        lax.fori_loop(0, size // 128, part, None)
        for j in range(2):
            value = lax.dot_general(
                outs[m][j * half : (j + 1) * half, :],
                w_ref[...],
                NT,
                preferred_element_type=F32,
            ).astype(BF16)
            if j == 0:
                (first_send if m % 2 else first_keep)[m // 2] = value
            else:
                (second_send if m // 2 else second_keep)[m % 2] = value


def finish(dqs, owns, cames, weight):
    n = dqs[0].shape[1]
    full = pl.BlockSpec(memory_space=VM)
    shifts = len(cames) // 2
    shape = jax.ShapeDtypeStruct
    return pl.pallas_call(
        functools.partial(finish_kernel, shifts),
        name="finish",
        in_specs=[full] * ((2 + shifts) * 2 + 1),
        out_specs=[full] * (TP + 5),
        out_shape=[shape((n // TP, 3 * HC), BF16)] * TP
        + [shape((8, 3 * HC), F32)]
        + [shape((2, n // TP // 2, D), BF16)] * 4,
        cost_estimate=cost(10),
    )(*dqs, *owns, *cames, weight)


TN = (((0,), (0,)), ((), ()))


def columns_kernel(chunks, place_ref, *refs):
    def heads(k):
        first, rest = refs[2 * k : 2 * k + 2]
        return [first.at[0]] + [rest.at[h] for h in range(HPG - 1)]

    dq_refs, own_refs, came_refs = heads(0), heads(1), heads(2)
    w_ref, norm_ref, narrow_ref, broad_ref = refs[6:10]
    a_hbm = refs[10 : 10 + chunks]
    keep_ref, send_ref, *part_hbm = refs[10 + chunks : 16 + chunks]
    out_ref, turn_ref, a_ref, g_ref, part_ref, sums_ref, sems = refs[16 + chunks :]
    loads = []
    at = 0
    for i, ref in enumerate(a_hbm):
        to = a_ref.at[pl.ds(at, ref.shape[0])]
        loads.append(pltpu.make_async_copy(ref, to, sems.at[i]))
        at += ref.shape[0]
    for load in loads:
        load.start()
    width = 3 * HC
    size = g_ref.shape[0] // TP
    half = size // 2
    sums_ref[...] = jnp.zeros_like(sums_ref)

    def part(i, c):
        rows = group_rows(i)
        pieces = []
        for h in range(HPG):
            value = own_refs[h][rows, :] + came_refs[h][rows, :].astype(F32)
            pieces.append(value.astype(BF16))
        for h in range(HPG):
            pieces.append(dq_refs[h][rows, :])
        whole = jnp.concatenate(pieces, axis=1)
        g_ref[rows, :] = whole
        sums_ref[0:1, :] += jnp.sum(whole.astype(F32), axis=0, keepdims=True)
        return c

    lax.fori_loop(0, g_ref.shape[0] // GROUP, part, None)
    stores = [
        pltpu.make_async_copy(part_ref.at[i], part_hbm[i], sems.at[chunks + i]) for i in range(4)
    ]
    for m in range(TP):
        value = lax.dot_general(
            g_ref[m * size : (m + 1) * size, :], w_ref[...], NT, preferred_element_type=F32
        ).astype(BF16)
        part_ref[0 if m % 2 else 1, m // 2] = value[:half]
        part_ref[2 if m // 2 else 3, m % 2] = value[half:]
    for store in stores:
        store.start()
    for load in loads:
        load.wait()
    for j in range(D // GROUP):
        lanes = slice(j * GROUP, (j + 1) * GROUP)
        out_ref[lanes, :width] = lax.dot_general(
            a_ref[:, lanes], g_ref[...], TN, preferred_element_type=F32
        )
    sums = sums_ref[0:1, :]
    weight = w_ref[...].astype(F32)
    turned = sums_ref[...].T
    query = turned[WIDE:, 0:1]
    value = jnp.concatenate(
        [turned[h * HW + DH : (h + 1) * HW, 0:1] for h in range(HPG)], axis=0
    )
    lane = lax.broadcasted_iota(jnp.int32, (1, 8), 1)
    norms = norm_ref[...].T
    direct = jnp.sum(out_ref[:, :width] * weight, axis=1, keepdims=True)
    shift = jnp.sum(weight * sums, axis=1, keepdims=True)
    gain = (direct - norms[:, 1:2] * shift) / norms[:, 0:1]
    narrow = narrow_ref[...].T
    out_ref[:, width:] = jnp.zeros((D, 64), F32)
    out_ref[:, width : width + 8] = jnp.where(lane >= 2, narrow, 0.0)
    for m in range(TP):
        at = pl.ds(pl.multiple_of((place_ref[0] ^ m) * HC, HC), HC)
        piece = narrow[m * HC : (m + 1) * HC, :]
        out_ref[at, width : width + 8] += jnp.where(lane < 2, piece, 0.0)
    out_ref[:, width + 8 : width + 16] = jnp.where(lane == 0, gain, 0.0) + jnp.where(
        lane == 1, shift, 0.0
    )
    own = pl.ds(pl.multiple_of(place_ref[0] * HC, HC), HC)
    out_ref[own, width + 8 : width + 16] += jnp.where(lane == 2, query, 0.0) + jnp.where(
        lane == 3, value, 0.0
    )
    turn_ref[...] = broad_ref[...].T

    def spread(b, c):
        for q in range(4):
            source = pl.ds(pl.multiple_of(b * 96 + q * 24, 8), 24)
            at = width + 16 + 8 * q
            out_ref[pl.ds(pl.multiple_of(b * 24, 8), 24), at : at + 8] = turn_ref[source, :]
        return c

    lax.fori_loop(0, FF // 96, spread, None)
    half = HC // 2
    for g in range(TP):
        mine = pl.multiple_of(g * HC + place_ref[1] * half, half)
        other = pl.multiple_of(g * HC + (1 - place_ref[1]) * half, half)
        keep_ref[g] = out_ref[pl.ds(mine, half), :]
        send_ref[g] = out_ref[pl.ds(other, half), :]
    for store in stores:
        store.wait()


def columns(place, dqs, owns, cames, weight, norms, narrow, broad, normed):
    n = dqs[0].shape[1]
    full = pl.BlockSpec(memory_space=VM)
    away = pl.BlockSpec(memory_space=pl.ANY)
    shape = jax.ShapeDtypeStruct
    out = shape((TP, HC // 2, 3 * HC + 64), F32)
    part = (2, n // TP // 2, D)
    return pl.pallas_call(
        functools.partial(columns_kernel, len(normed)),
        name="columns",
        in_specs=[pl.BlockSpec(memory_space=SMEM)] + [full] * 10 + [away] * len(normed),
        out_specs=[full] * 2 + [away] * 4,
        out_shape=[out, out] + [shape(part, BF16)] * 4,
        scratch_shapes=[
            pltpu.VMEM((D, 3 * HC + 64), F32),
            pltpu.VMEM((FF, 8), F32),
            pltpu.VMEM((n, D), BF16),
            pltpu.VMEM((n, 3 * HC), BF16),
            pltpu.VMEM((4,) + part, BF16),
            pltpu.VMEM((8, 3 * HC), F32),
            pltpu.SemaphoreType.DMA((4 + len(normed),)),
        ],
        cost_estimate=cost(14),
    )(place, *dqs, *owns, *cames, weight, norms, narrow, broad, *normed)


def weight_grads_kernel(
    place_ref,
    u_ref,
    datt_ref,
    a2_ref,
    df_ref,
    u2_ref,
    dz_ref,
    keep_ref,
    send_ref,
    back_ref,
    in_ref,
    out_ref,
    sems,
):
    hg = place_ref[0]
    qs = place_ref[1]

    def each(source, k, rows, sem, act):
        block = (k // 2) ^ hg
        part = 0 if rows < 432 else 1
        slot = (block % 2) * 2 + block // 2 if part == 0 else block
        to = pl.ds(rows % 432, source.shape[0])
        kept = k % 2 == qs
        pl.when(kept)(
            lambda: act(pltpu.make_async_copy(source, keep_ref.at[part, slot, to], sem))
        )
        pl.when(jnp.logical_not(kept))(
            lambda: act(pltpu.make_async_copy(source, send_ref.at[part, slot, to], sem))
        )

    def start(source, k, rows, sem):
        each(source, k, rows, sem, lambda copy: copy.start())

    def wait(source, k, rows, sem):
        each(source, k, rows, sem, lambda copy: copy.wait())

    def back_block(k):
        return back_ref.at[pl.ds(pl.multiple_of(k * 384, 384), 384)]

    def in_pieces(k):
        cut = [
            (in_ref.at[0, pl.ds(pl.multiple_of(k * 96, 48), 48)], 384),
            (in_ref.at[0, pl.ds(pl.multiple_of(k * 96 + 48, 48), 48)], 432),
        ]
        whole = pl.ds(pl.multiple_of(k * 96, 96), 96)
        return cut + [(in_ref.at[j, whole], 384 + 96 * j) for j in range(1, 4)]

    def out_block(k):
        at = ((k // 2) ^ hg) * 192 + (k % 2) * 96
        return out_ref.at[pl.ds(pl.multiple_of(at, 96), 96)]

    def back(k, c):
        lanes = pl.ds(pl.multiple_of(k * 384, 384), 384)
        back_ref[pl.ds(pl.multiple_of(k * 384, 384), 384), :] = lax.dot_general(
            u2_ref[:, lanes], dz_ref[...], TN, preferred_element_type=F32
        ).astype(BF16)
        start(back_block(k), k, 0, sems.at[0, k])
        return c

    lax.fori_loop(0, 8, back, None)

    def inner(j, c):
        lanes = pl.ds(pl.multiple_of(j * D, D), D)
        in_ref[j] = lax.dot_general(
            a2_ref[...], df_ref[:, lanes], TN, preferred_element_type=F32
        ).astype(BF16)
        return c

    lax.fori_loop(0, 4, inner, None)

    def send_inner(k, c):
        for j, (source, first) in enumerate(in_pieces(k)):
            start(source, k, first, sems.at[1 + j, k])
        return c

    lax.fori_loop(0, 8, send_inner, None)
    out_ref[...] = lax.dot_general(
        u_ref[...], datt_ref[...], TN, preferred_element_type=F32
    ).astype(BF16)

    def finish_all(k, c):
        start(out_block(k), k, 768, sems.at[6, k])
        wait(back_block(k), k, 0, sems.at[0, k])
        for j, (source, first) in enumerate(in_pieces(k)):
            wait(source, k, first, sems.at[1 + j, k])
        return c

    lax.fori_loop(0, 8, finish_all, None)

    def finish_out(k, c):
        wait(out_block(k), k, 768, sems.at[6, k])
        return c

    lax.fori_loop(0, 8, finish_out, None)


def weight_grads(place, u, datt, a2, df, u2, dz):
    full = pl.BlockSpec(memory_space=VM)
    out = jax.ShapeDtypeStruct((2, TP, 432, D), BF16)
    return pl.pallas_call(
        weight_grads_kernel,
        name="weight_grads",
        in_specs=[pl.BlockSpec(memory_space=SMEM)] + [full] * 6,
        out_specs=[pl.BlockSpec(memory_space=pl.ANY)] * 2,
        out_shape=[out, out],
        scratch_shapes=[
            pltpu.VMEM((FF, D), BF16),
            pltpu.VMEM((4, D, D), BF16),
            pltpu.VMEM((D, D), BF16),
            pltpu.SemaphoreType.DMA((7, 8)),
        ],
        cost_estimate=cost(14),
    )(place, u, datt, a2, df, u2, dz)


def norm_parts(value):
    centred = value - jnp.mean(value, axis=1, keepdims=True)
    scale = lax.rsqrt(jnp.mean(centred * centred, axis=1, keepdims=True) + 1e-05)
    return centred * scale, scale


def norm_back(grad, unit, scale):
    first = jnp.mean(grad, axis=1, keepdims=True)
    second = jnp.mean(grad * unit, axis=1, keepdims=True)
    return scale * (grad - first - unit * second)


def column_sum(value):
    return jnp.sum(value, axis=0, keepdims=True)


CHUNK = 768
TILE = 256


def place_weights(place_ref, own_refs, gathered, in_ref, out_ref, back_ref):
    near, axis, axis_far, corner, corner_far = gathered
    in_ref[pl.ds(pl.multiple_of(place_ref[0] * 192, 192), 192), :] = own_refs[0][...]
    out_ref[pl.ds(pl.multiple_of(place_ref[4] * 192, 192), 192), :] = own_refs[1][...]
    back_ref[pl.ds(pl.multiple_of(place_ref[0] * D, D), D), :] = own_refs[2][...]
    sources = [
        (near, 0),
        (near, 1),
        (axis, 0),
        (axis, 1),
        (axis_far, 0),
        (axis_far, 1),
        (corner, None),
        (corner_far, None),
    ]
    for k, (ref, t) in enumerate(sources):
        c = place_ref[8 + k]
        for m in range(1, 4):
            value = ref[m - 1] if t is None else ref[t, m - 1]
            z = place_ref[m]
            cols = pl.ds(pl.multiple_of(c * 384, 384), 384)
            in_ref[pl.ds(pl.multiple_of(z * 192, 96), 96), cols] = value[0:96, 0:384]
            in_ref[pl.ds(pl.multiple_of(z * 192 + 96, 96), 96), cols] = value[0:96, 384:768]
            back_ref[pl.ds(pl.multiple_of(z * D + c * 96, 96), 96), :] = value[96:192, :]
            block = jnp.concatenate([value[192:216, 0:384], value[192:216, 384:768]], axis=0)
            at = pl.ds(pl.multiple_of(place_ref[4 + m] * 192 + (c // 2) * 48, 48), 48)
            out_ref[at, pl.ds(pl.multiple_of((c % 2) * 384, 384), 384)] = block


def middle_kernel(scattered, *refs):
    piece_refs = refs[:TP]
    x_ref, cot_ref, row_ref, wide_ref = refs[TP : TP + 4]
    refs = refs[TP + 4 :]
    if scattered:
        place_ref = refs[0]
        own_refs, gathered, refs = refs[1:4], refs[4:9], refs[9:]
        out_w_ref, in_w_ref, back_w_ref = refs[-3:]
        place_weights(place_ref, own_refs, gathered, in_w_ref, out_w_ref, back_w_ref)
        refs = refs[:-3]
    else:
        in_w_ref, out_w_ref, back_w_ref = refs[:3]
        refs = refs[3:]
    do_refs = refs[:TP]
    (
        mixed_ref,
        u_ref,
        a2_ref,
        u2_ref,
        df_ref,
        datt_ref,
        dx_ref,
        narrow_ref,
        broad_ref,
        ctx_ref,
        do_ref,
        g_ref,
        slope_ref,
        d_ref,
        da_ref,
        x1_ref,
    ) = refs[TP:]
    half = piece_refs[0].shape[0]
    for m, ref in enumerate(piece_refs):
        for j in range(2):
            ctx_ref[j * half : (j + 1) * half, m * HC : (m + 1) * HC] = ref[
                :, j * HC : (j + 1) * HC
            ]
    narrow_ref[...] = jnp.zeros_like(narrow_ref)
    broad_ref[...] = jnp.zeros_like(broad_ref)

    def tile(i, c):
        rows = pl.ds(pl.multiple_of(i * TILE, TILE), TILE)
        unit_one, scale_one = norm_parts(ctx_ref[rows, :].astype(F32))
        u = (unit_one * row_ref[0:1, :] + row_ref[1:2, :]).astype(BF16)
        u_ref[rows, :] = u
        x1 = (
            x_ref[rows, :].astype(F32)
            + jnp.dot(u, out_w_ref[...], preferred_element_type=F32)
            + row_ref[2:3, :]
        )
        x1_ref[...] = x1
        unit_two, scale_two = norm_parts(x1)
        a2 = (unit_two * row_ref[3:4, :] + row_ref[4:5, :]).astype(BF16)
        a2_ref[rows, :] = a2

        def lanes_of(j):
            return pl.ds(pl.multiple_of(j * CHUNK, CHUNK), CHUNK)

        def up(j, total):
            lanes = lanes_of(j)
            f = (
                jnp.dot(a2_ref[rows, :], in_w_ref[:, lanes], preferred_element_type=F32)
                + wide_ref[0:1, lanes]
            )
            cdf = 0.5 * (1.0 + lax.erf(f * 0.7071067811865476))
            pdf = jnp.exp(-0.5 * f * f) * 0.3989422804014327
            slope_ref[:, lanes] = cdf + f * pdf
            g = f * cdf
            g_ref[:, lanes] = g
            return total + jnp.sum(g, axis=1, keepdims=True)

        average = lax.fori_loop(0, FF // CHUNK, up, jnp.zeros((TILE, 1), F32)) / FF

        def spread(j, total):
            lanes = lanes_of(j)
            centred = g_ref[:, lanes] - average
            return total + jnp.sum(centred * centred, axis=1, keepdims=True)

        variance = lax.fori_loop(0, FF // CHUNK, spread, jnp.zeros((TILE, 1), F32)) / FF
        scale = lax.rsqrt(variance + 1e-05)

        def turn(j, carry):
            first, second = carry
            lanes = lanes_of(j)
            unit = (g_ref[:, lanes] - average) * scale
            g_ref[:, lanes] = unit
            gain = wide_ref[1:2, lanes]
            u2_ref[rows, lanes] = (unit * gain + wide_ref[2:3, lanes]).astype(BF16)
            du2 = lax.dot_general(
                cot_ref[rows, :], back_w_ref[lanes, :], NT, preferred_element_type=F32
            )
            broad_ref[0:1, lanes] += column_sum(du2 * unit)
            broad_ref[2:3, lanes] += column_sum(du2)
            grad = du2 * gain
            d_ref[:, lanes] = grad
            return (
                first + jnp.sum(grad, axis=1, keepdims=True),
                second + jnp.sum(grad * unit, axis=1, keepdims=True),
            )

        none = jnp.zeros((TILE, 1), F32)
        first, second = lax.fori_loop(0, FF // CHUNK, turn, (none, none))
        first = first / FF
        second = second / FF
        da_ref[...] = jnp.zeros_like(da_ref)

        def down(j, c):
            lanes = lanes_of(j)
            grad = scale * (d_ref[:, lanes] - first - g_ref[:, lanes] * second)
            df = (grad * slope_ref[:, lanes]).astype(BF16)
            df_ref[rows, lanes] = df
            broad_ref[1:2, lanes] += column_sum(df.astype(F32))
            da_ref[...] += lax.dot_general(
                df, in_w_ref[:, lanes], NT, preferred_element_type=F32
            )
            return c

        lax.fori_loop(0, FF // CHUNK, down, None)
        da2 = da_ref[...]
        unit_two, scale_two = norm_parts(x1_ref[...])
        narrow_ref[2:3, :] += column_sum(da2 * unit_two)
        narrow_ref[3:4, :] += column_sum(da2)
        cot = cot_ref[rows, :].astype(F32)
        dx = cot + norm_back(da2 * row_ref[3:4, :], unit_two, scale_two)
        dx_ref[rows, :] = dx
        datt = dx.astype(BF16)
        datt_ref[rows, :] = datt
        narrow_ref[4:5, :] += column_sum(datt.astype(F32))
        narrow_ref[5:6, :] += column_sum(cot)
        du = lax.dot_general(datt, out_w_ref[...], NT, preferred_element_type=F32)
        unit_one, scale_one = norm_parts(ctx_ref[rows, :].astype(F32))
        narrow_ref[0:1, :] += column_sum(du * unit_one)
        narrow_ref[1:2, :] += column_sum(du)
        do_ref[rows, :] = norm_back(du * row_ref[0:1, :], unit_one, scale_one).astype(BF16)
        mixed_ref[rows, :] = (
            jnp.dot(u2_ref[rows, :], back_w_ref[...], preferred_element_type=F32)
            + row_ref[5:6, :]
            + x1_ref[...]
        ).astype(BF16)
        return c

    lax.fori_loop(0, ctx_ref.shape[0] // TILE, tile, None)
    for m, ref in enumerate(do_refs):
        pieces = []
        for h in range(HPG):
            lanes = slice(m * HC + h * DH, m * HC + (h + 1) * DH)
            pieces += [do_ref[:half, lanes], do_ref[half:, lanes]]
        ref[...] = jnp.concatenate(pieces, axis=1)


def middle(pieces, x, cot, narrow, wide, weights):
    n = x.shape[0]
    full = pl.BlockSpec(memory_space=VM)
    shape = jax.ShapeDtypeStruct
    scattered = len(weights) > 3
    weight_specs = [full] * len(weights)
    if scattered:
        weight_specs[0] = pl.BlockSpec(memory_space=SMEM)
    return pl.pallas_call(
        functools.partial(middle_kernel, scattered),
        name="middle",
        in_specs=[full] * (TP + 4) + weight_specs,
        out_specs=[full] * (TP + 9),
        out_shape=[shape(p.shape, BF16) for p in pieces]
        + [
            shape((n, D), BF16),
            shape((n, D), BF16),
            shape((n, D), BF16),
            shape((n, FF), BF16),
            shape((n, FF), BF16),
            shape((n, D), BF16),
            shape((n, D), F32),
            shape((8, D), F32),
            shape((8, FF), F32),
        ],
        scratch_shapes=[
            pltpu.VMEM((n, D), BF16),
            pltpu.VMEM((n, D), BF16),
            pltpu.VMEM((TILE, FF), F32),
            pltpu.VMEM((TILE, FF), F32),
            pltpu.VMEM((TILE, FF), F32),
            pltpu.VMEM((TILE, D), F32),
            pltpu.VMEM((TILE, D), F32),
        ]
        + ([pltpu.VMEM(s, BF16) for s in ((D, D), (D, FF), (FF, D))] if scattered else []),
        cost_estimate=cost(36),
    )(*pieces, x, cot, narrow, wide, *weights)


def layer_norm(values, gain, shift):
    average = jnp.mean(values, axis=-1, keepdims=True)
    centred = values - average
    variance = jnp.mean(centred * centred, axis=-1, keepdims=True)
    return centred * lax.rsqrt(variance + 1e-05) * gain + shift


def outer_sum(left, right):
    return lax.dot_general(left, right, (((0,), (0,)), ((), ())), preferred_element_type=F32)


def times_transposed(left, matrix):
    return lax.dot_general(left, matrix, (((1,), (1,)), ((), ())), preferred_element_type=F32)


def tie(value, *before):
    return lax.optimization_barrier((value, before))[0]


def pick(array, index, axis=0):
    return lax.dynamic_index_in_dim(array, index, axis, keepdims=False)


def make_local(ctx_size, fsdp_size):
    nq = ctx_size // TP
    fast = ctx_size == 8 and fsdp_size == 4

    def over_heads(value, mask):
        return lax.ppermute(
            value, "ctx", [(i, ((i // nq) ^ mask) * nq + i % nq) for i in range(ctx_size)]
        )

    def over_rows(value, shift):
        return lax.ppermute(
            value,
            "ctx",
            [(i, (i // nq) * nq + (i % nq - shift) % nq) for i in range(ctx_size)],
        )

    def over_fsdp(value, mask):
        return lax.ppermute(value, "fsdp", [(i, i ^ mask) for i in range(fsdp_size)])

    def over_split(value, masks):
        return lax.ppermute(
            value,
            "ctx",
            [(i, ((i // nq) ^ masks[i % nq]) * nq + i % nq) for i in range(ctx_size)],
        )

    moves = (over_heads, over_rows, over_fsdp, over_split)

    def exchange_heads(own, halves):
        one = over_heads(own, 1)
        two = over_heads(own, 2)
        first, second = halves
        low = over_heads(first(one), 2)
        high = over_heads(second(two), 1)
        return one, two, low, high

    def local(
        tokens,
        cotangent,
        lengths,
        dealing,
        qkv_weight,
        out_weight,
        in_weight,
        back_weight,
        norm_gains,
        shifts,
        ffn_gain,
        ffn_shifts,
    ):
        ctx = lax.axis_index("ctx")
        fs = lax.axis_index("fsdp")
        hg = ctx // nq
        qs = ctx % nq
        rows = tokens.shape[1]
        shard = qkv_weight.shape[0]
        deal_row = dealing[0]
        group_count = deal_row.shape[0]
        per = rows // GROUP
        bounds = jnp.cumsum(lengths[0])
        members = [
            [((hg ^ m) * nq + (qs + s) % nq) * per + j for m in range(TP) for j in range(per)]
            for s in range(nq)
        ]
        stored = jnp.stack([g for part in members for g in part]).astype(jnp.int32)
        onehot = (stored[:, None] == jnp.arange(group_count, dtype=jnp.int32)[None, :]).astype(
            jnp.int32
        )
        dealt = jnp.sum(onehot * deal_row[None, :], axis=1)
        mine = tokens[0]
        half = rows // 2
        one, two, low, high = exchange_heads(mine, (lambda a: a[:half], lambda a: a[half:]))
        chunks = (mine, one, two, low, high)

        def own_columns(weight):
            def take(at, size):
                value = weight[:, at : at + size]
                for g in range(1, TP):
                    other = weight[:, at + g * HC : at + g * HC + size]
                    value = jnp.where(hg == g, other, value)
                return value

            out = []
            for h in range(HPG):
                out += [take(D + h * DH, DH), take(2 * D + h * DH, DH)]
            return jnp.concatenate(out + [take(0, HC)], axis=1)

        feature = norm_gains.shape[1]
        narrow_rows = jnp.concatenate([norm_gains, shifts], axis=0)
        broad_rows = jnp.concatenate([ffn_gain[None], ffn_shifts], axis=0).reshape(12, feature)
        small = jnp.concatenate(
            [
                jnp.pad(narrow_rows, ((0, 6), (0, HC - feature))),
                jnp.pad(broad_rows, ((0, 4), (0, 2 * HC - feature))),
            ],
            axis=1,
        )
        span = shard // nq
        tail = small.shape[0] // nq
        columns_half = pick(own_columns(qkv_weight).reshape(nq, span, 3 * HC), qs)
        piece = jnp.concatenate([columns_half, pick(small.reshape(nq, tail, -1), qs)], axis=0)
        came = [over_fsdp(piece, m) for m in range(1, fsdp_size)]
        parts = jnp.stack([piece] + came)
        if fast:
            foreign = gather_pieces(in_weight, back_weight, out_weight, came, hg, qs, moves)
            shared = [over_rows(tie(parts, one, two), 1)]
        else:
            shared = [over_rows(parts, s) for s in range(1, nq)]
        parts = jnp.stack([parts] + shared)
        if not fast:
            w_own = jnp.concatenate(
                [
                    pick(pick(parts, (h - qs) % nq), f ^ fs)[:span]
                    for f in range(fsdp_size)
                    for h in range(nq)
                ],
                axis=0,
            )
        tails = [
            jnp.concatenate(
                [pick(pick(parts, (h - qs) % nq), f ^ fs)[span:] for h in range(nq)], axis=0
            )
            for f in range(fsdp_size)
        ]
        narrow_all = jnp.concatenate([p[:10, :feature] for p in tails], axis=1).astype(F32)
        broad_all = jnp.concatenate(
            [p[:12, HC : HC + feature].reshape(3, -1) for p in tails], axis=1
        ).astype(F32)
        gains = narrow_all[:3]
        shift_rows = narrow_all[3:]
        ffn_scale = broad_all[0]
        ffn_shift_rows = broad_all[1:]

        if not fast:
            in_w = lax.all_gather(in_weight, "fsdp", axis=0, tiled=True)
            back_w = lax.all_gather(back_weight, "fsdp", axis=0, tiled=True)
            out_w = lax.all_gather(out_weight, "fsdp", axis=0, tiled=True)
            out_blocks = out_w.reshape(TP, HC, D)
            out_rel = jnp.concatenate([pick(out_blocks, hg ^ m) for m in range(TP)], axis=0)

        def own_heads(row):
            return pick(row.reshape(TP, HC), hg)

        value_bias = own_heads(shift_rows[2]).reshape(HPG, DH)
        bias = jnp.concatenate(
            [
                jnp.stack([jnp.zeros((HPG, DH), F32), value_bias], axis=1).reshape(-1),
                own_heads(shift_rows[1]),
            ]
        )[None]
        norm_rows = jnp.stack([gains[0], shift_rows[0]])
        norm_rows = jnp.pad(norm_rows, ((0, 6), (0, 0)))
        if fast:
            table = jnp.stack(
                [(f ^ fs) * nq + (qs + s) % nq for s in range(nq) for f in range(fsdp_size)]
            )
            *first, w_own = project(
                (mine, one, two), (table.astype(jnp.int32), parts[0], parts[1]), norm_rows, bias
            )
        else:
            first = project((mine, one, two), (w_own,), norm_rows, bias)
        if fast:
            gathered = gather_axis(tie(foreign, first[1]), (low, high), moves)
        projected = [first, project((low, high), (w_own,), norm_rows, bias)]
        normed = [p[0] for p in projected]
        queries = [p[1] for p in projected]
        pairs = [p[2] for p in projected]
        for s in range(1, nq):
            pairs = pairs + [over_rows(p[2], s) for p in projected]
        if fast:
            dealt = tie(dealt, gathered[0])

        *context_parts, context_t, log_total, q_turned, kv_rows, k_turned = attend_forward(
            dealt, bounds, queries, pairs
        )
        got = [context_parts[0]] + [over_heads(context_parts[m], m) for m in range(1, TP)]

        if fast:
            gathered = gather_rest(*gathered, log_total, got, moves)

        def relative(row):
            blocks = row.reshape(TP, HC)
            return jnp.concatenate([pick(blocks, hg ^ m) for m in range(TP)])

        narrow = jnp.stack(
            [relative(gains[1]), relative(shift_rows[3]), shift_rows[4], gains[2], shift_rows[5]]
            + [shift_rows[6]] * 3
        )
        wide = jnp.pad(
            jnp.stack([ffn_shift_rows[0], ffn_scale, ffn_shift_rows[1]]), ((0, 5), (0, 0))
        )
        cot = cotangent[0]
        if fast:
            weights = (weight_places(hg, qs, fs), in_weight, out_weight, back_weight, *gathered)
        else:
            weights = (in_w, out_rel, back_w)
        (
            *sent,
            mixed_out,
            inner_low,
            normed_two_low,
            inner_two_low,
            hidden_low,
            branch_low,
            grad_middle,
            narrow_sums,
            broad_sums,
        ) = middle(got, mine, cot, narrow, wide, weights)
        grad_gain_one, grad_shift_three, grad_gain_two, grad_shift_five = narrow_sums[:4]
        grad_out_bias, grad_back_bias = narrow_sums[4:6]
        grad_ffn_gain, grad_in_bias, grad_ffn_shift = broad_sums[:3]

        grad_rows = [sent[0]] + [over_heads(sent[m], m) for m in range(1, TP)]
        set_rows = TP * rows
        place = jnp.stack([hg, qs, fs]).astype(jnp.int32)
        if fast:
            keep, send = weight_grads(
                tie(place, grad_rows[1]), inner_low, branch_low, normed_two_low, hidden_low, inner_two_low, cot
            )
            stage = first_stage(keep, send, moves)

        def backward_of(base, count, table):
            return attend_backward(
                base,
                count,
                table,
                bounds,
                queries,
                q_turned,
                kv_rows,
                k_turned,
                context_t,
                log_total,
                grad_rows,
            )

        def exchange(other):
            return [
                over_rows(other[:, (s - 1) * set_rows : s * set_rows], nq - s)
                for s in range(1, nq)
            ]

        table = tie(dealt, keep) if fast else dealt
        first_head = backward_of(0, 1, table)
        table = tie(dealt, first_head, stage[0]) if fast else dealt
        other_heads = backward_of(1, HPG - 1, table)
        cames = [exchange(first_head[2]), exchange(other_heads[2])]
        if fast:
            second = second_stage(stage, keep, other_heads, moves)
            cames = tie(cames, second[0])
        came = [cames[i][s] for s in range(nq - 1) for i in range(2)]
        dqs = [first_head[0], other_heads[0]]
        owns = [first_head[1], other_heads[1]]
        if fast:
            kept, sent_columns, first_send, first_keep, second_send, second_keep = columns(
                place, dqs, owns, came, w_own, norm_rows, narrow_sums, broad_sums, normed
            )
        else:
            *grads, sums, first_send, first_keep, second_send, second_keep = finish(
                dqs, owns, came, w_own
            )

        def plus(mine, came):
            return mine.astype(F32) + came.astype(F32)

        first_came = over_heads(first_send, 1)
        second_came = over_heads(second_send, 2)
        first_last = over_heads(plus(first_keep[1], first_came[1]).astype(BF16), 2)
        second_last = over_heads(plus(second_keep[1], second_came[1]).astype(BF16), 1)
        grad_normed = jnp.concatenate(
            [
                plus(first_keep[0], first_came[0]) + first_last.astype(F32),
                plus(second_keep[0], second_came[0]) + second_last.astype(F32),
            ],
            axis=0,
        )
        inputs = mine.astype(F32)
        first_pull = jax.vjp(layer_norm, inputs, gains[0], shift_rows[0])[1]
        grad_inputs_part, grad_gain_zero, grad_shift_zero = first_pull(grad_normed)
        input_grad = grad_middle + grad_inputs_part

        def absolute(row):
            blocks = row.reshape(TP, HC)
            return jnp.concatenate([pick(blocks, hg ^ m) for m in range(TP)])

        order = ctx * fsdp_size + fs
        total_devices = ctx_size * fsdp_size
        if fast:
            qkv_out, tail = reduce_columns(kept, sent_columns, hg, fs, moves)
            turned = tail.T
            wide_parts = turned[16:48].reshape(4, 8, -1)
            small_out = (
                jnp.stack([turned[8], turned[0], turned[2]]),
                jnp.stack([turned[i] for i in (9, 10, 11, 1, 4, 3, 5)]),
                wide_parts[:, 0].reshape(-1),
                jnp.stack([wide_parts[:, 1].reshape(-1), wide_parts[:, 2].reshape(-1)]),
            )
            back_out, in_out, out_out = later_stages(second, kept, fs, moves)
        else:

            def placed(row):
                blank = jnp.zeros((TP, HC), F32)
                return lax.dynamic_update_slice(blank, row[None], (hg, 0)).reshape(-1)

            row = sums[0]
            value_sums = row[:WIDE].reshape(HPG, 2, DH)[:, 1].reshape(-1)
            small_terms = jnp.concatenate(
                [
                    grad_gain_zero,
                    absolute(grad_gain_one),
                    grad_gain_two,
                    grad_shift_zero,
                    placed(row[WIDE:]),
                    placed(value_sums),
                    absolute(grad_shift_three),
                    grad_out_bias,
                    grad_shift_five,
                    grad_back_bias,
                    grad_ffn_gain,
                    grad_in_bias,
                    grad_ffn_shift,
                ]
            )
            axes = ("ctx", "fsdp")
            small_terms = lax.psum(small_terms, axes)
            narrow = small_terms[: 10 * D].reshape(10, total_devices, D // total_devices)
            narrow = pick(narrow, order, 1)
            broad = small_terms[10 * D :].reshape(3, total_devices, FF // total_devices)
            broad = pick(broad, order, 1)
            small_out = (narrow[:3], narrow[3:], broad[0], broad[1:])
            blocks = outer_sum(inner_low, branch_low).reshape(TP, HC, D)
            grad_out_w = jnp.concatenate([pick(blocks, hg ^ m) for m in range(TP)], axis=0)
            grad_in_w = outer_sum(normed_two_low, hidden_low)
            grad_back_w = outer_sum(inner_two_low, cot)
            back_out, in_out, out_out = (
                lax.psum_scatter(g.astype(BF16), axes, scatter_dimension=0, tiled=True).astype(F32)
                for g in (grad_back_w, grad_in_w, grad_out_w)
            )
            grad_qkv_w = outer_sum(jnp.concatenate(normed, axis=0), jnp.concatenate(grads, axis=0))
            pairs_w = grad_qkv_w[:, :WIDE].reshape(D, HPG, 2, DH)
            three = jnp.stack(
                [
                    grad_qkv_w[:, WIDE:],
                    pairs_w[:, :, 0].reshape(D, HC),
                    pairs_w[:, :, 1].reshape(D, HC),
                ],
                axis=1,
            )
            blank = jnp.zeros((D, 3, TP, HC), BF16)
            whole = lax.dynamic_update_slice(
                blank, three.astype(BF16)[:, :, None], (0, 0, hg, 0)
            ).reshape(D, 3 * D)
            qkv_out = lax.psum_scatter(whole, axes, scatter_dimension=0, tiled=True).astype(F32)
        return (
            mixed_out[None],
            input_grad[None],
            qkv_out,
            out_out,
            in_out,
            back_out,
        ) + small_out

    return local


def gather_pieces(in_weight, back_weight, out_weight, first, hg, qs, moves):
    over_heads, over_rows, over_fsdp, over_split = moves
    c = hg * 2 + qs
    cut = lax.dynamic_slice(in_weight, (0, c * 384), (192, 384))
    out_cut = lax.dynamic_slice(out_weight, (hg * 48, qs * 384), (48, 384))
    piece = jnp.concatenate(
        [
            jnp.concatenate([cut[:96], cut[96:]], axis=1),
            pick(back_weight.reshape(8, 96, D), c),
            jnp.concatenate([out_cut[:24], out_cut[24:]], axis=1),
        ],
        axis=0,
    )
    piece = tie(piece, *first)
    return [over_fsdp(piece, m) for m in (1, 2, 3)]


def gather_axis(foreign, before, moves):
    over_heads, over_rows, over_fsdp, over_split = moves
    foreign = jnp.stack(foreign)
    near = jnp.stack([foreign, over_rows(foreign, 1)])
    return near, over_split(tie(near, *before), (1, 2))


def gather_rest(near, axis, first, then, moves):
    over_heads, over_rows, over_fsdp, over_split = moves
    axis = tie(axis, first)
    corner = over_split(axis[0], (2, 1))
    axis = tie(axis, then)
    return near, axis, over_rows(axis, 1), corner, over_rows(corner, 1)


def weight_places(hg, qs, fs):
    near_x = jnp.where(qs == 0, 1, 2)
    far_x = 3 - near_x
    return jnp.stack(
        [fs ^ m for m in range(4)]
        + [fs ^ m ^ hg for m in range(4)]
        + [hg * 2 + qs, hg * 2 + 1 - qs]
        + [(hg ^ near_x) * 2 + qs, (hg ^ near_x) * 2 + 1 - qs]
        + [(hg ^ far_x) * 2 + 1 - qs, (hg ^ far_x) * 2 + qs]
        + [(hg ^ 3) * 2 + qs, (hg ^ 3) * 2 + 1 - qs]
    ).astype(jnp.int32)


def total_of(*parts):
    return functools.reduce(jnp.add, [p.astype(F32) for p in parts])


def first_stage(keep, send, moves):
    over_heads, over_rows, over_fsdp, over_split = moves
    came = over_rows(send, 1)
    return [total_of(keep[i, 2:], came[i, 2:]).astype(BF16) for i in range(2)], came


def second_stage(stage, keep, before, moves):
    over_heads, over_rows, over_fsdp, over_split = moves
    (first_send, second_send), came = stage
    arrived = [over_heads(first_send, 1), over_heads(second_send, 2)]
    keep, came = tie((keep, came), before)
    last = [total_of(keep[i, 1], came[i, 1], arrived[i][1]).astype(BF16) for i in range(2)]
    return last, keep, came, arrived


def later_stages(stage, before, fs, moves):
    over_heads, over_rows, over_fsdp, over_split = moves
    last, keep, came, arrived = stage
    last = [over_heads(last[0], 2), over_heads(last[1], 1)]
    last = tie(last, before)
    whole = jnp.concatenate(
        [total_of(keep[i, 0], came[i, 0], arrived[i][0], last[i]).astype(BF16) for i in range(2)],
        axis=0,
    )
    back = whole[:384].reshape(4, 96, D)
    inner = whole[384:768].reshape(4, 4, 24, D)
    out = whole[768:].reshape(4, 24, D)

    def piece(f):
        return jnp.concatenate(
            [pick(back, f), pick(inner, f, 1).reshape(96, D), pick(out, f)], axis=0
        )

    total = piece(fs).astype(F32)
    for m in (1, 2, 3):
        total = total + over_fsdp(piece(fs ^ m), m).astype(F32)
    inner = jnp.concatenate([total[96 + 24 * j : 120 + 24 * j] for j in range(4)], axis=1)
    return total[:96], inner, total[192:216]


def reduce_columns(keep, send, hg, fs, moves):
    over_heads, over_rows, over_fsdp, over_split = moves
    kept = keep + over_rows(send, 1)
    kept = kept.reshape(TP, 4, 24, 640)
    low = kept.astype(BF16)
    total = pick(kept, fs, 1)
    for m in (1, 2, 3):
        total = total + over_fsdp(pick(low, fs ^ m, 1), m).astype(F32)
    mine = jnp.stack(
        [pick(total, hg)] + [over_heads(pick(total, hg ^ m), m) for m in (1, 2, 3)]
    )
    tail = jnp.sum(mine[:, :, 3 * HC :], axis=0)
    mine = [pick(mine, hg ^ g) for g in range(TP)]
    out = [block[:, WIDE : 3 * HC] for block in mine]
    for part in range(2):
        for block in mine:
            for h in range(HPG):
                at = h * HW + part * DH
                out.append(block[:, at : at + DH])
    return jnp.concatenate(out, axis=1), tail


def solution(mesh):
    ctx_size = mesh.shape["ctx"]
    fsdp_size = mesh.shape["fsdp"]
    in_specs = (
        P("fsdp", "ctx", None),
        P("fsdp", "ctx", None),
        P("fsdp", None),
        P("fsdp", None),
        P("fsdp", None),
        P("fsdp", None),
        P("fsdp", None),
        P("fsdp", None),
        P(None, "fsdp"),
        P(None, "fsdp"),
        P("fsdp"),
        P(None, "fsdp"),
    )
    out_specs = (
        P("fsdp", "ctx", None),
        P("fsdp", "ctx", None),
        P(("ctx", "fsdp"), None),
        P(("ctx", "fsdp"), None),
        P(("ctx", "fsdp"), None),
        P(("ctx", "fsdp"), None),
        P(None, ("ctx", "fsdp")),
        P(None, ("ctx", "fsdp")),
        P(("ctx", "fsdp")),
        P(None, ("ctx", "fsdp")),
    )
    return jax.shard_map(
        make_local(ctx_size, fsdp_size),
        mesh=mesh,
        in_specs=in_specs,
        out_specs=out_specs,
        check_vma=False,
    )
```

```python
import functools

import jax
import jax.numpy as jnp
from jax import lax
from jax.experimental import pallas as pl
from jax.experimental.pallas import tpu as pltpu
from jax.sharding import PartitionSpec as P

D = 768
H = 12
DH = 64
FF = 3072
GROUP = 256
HPG = 3
TP = H // HPG
HC = HPG * DH
LANES = 256
SCALE2 = 1.4426950408889634 * DH ** -0.5
NEG = -1e30
NT = (((1,), (1,)), ((), ()))
F32 = jnp.float32
BF16 = jnp.bfloat16

SMEM = pltpu.MemorySpace.SMEM
VM = pltpu.MemorySpace.VMEM
HW = 2 * DH
WIDE = HPG * HW


def cost(us):
    return pl.CostEstimate(flops=int(us * 4.4e9), transcendentals=0, bytes_accessed=100000)


def block_bounds(group, bound_ref):
    lane = lax.broadcasted_iota(jnp.int32, (1, GROUP), 1)
    q_places = group * GROUP + lane
    starts = jnp.zeros((1, GROUP), jnp.int32)
    first = jnp.int32(0)
    last = jnp.int32(0)
    for j in range(bound_ref.shape[0]):
        b = bound_ref[j]
        starts = jnp.where(q_places >= b, b, starts)
        first = jnp.where(group * GROUP >= b, b, first)
        last = jnp.where(group * GROUP + GROUP - 1 >= b, b, last)
    low = first // GROUP
    mid = jnp.minimum(group, (last + GROUP - 1) // GROUP)
    return q_places, starts, low, mid


def sweep(group, low, mid, visit, carry):
    pairs = (group - low + 2) // 2
    plain = jnp.clip((group - 1 - mid) // 2, 0, pairs - 1)
    carry = visit(group, True, carry)
    carry = lax.fori_loop(1, 1 + plain, lambda t, c: visit(group - 2 * t, False, c), carry)
    return lax.fori_loop(1 + plain, pairs, lambda t, c: visit(group - 2 * t, True, c), carry)


def pair_rows(top):
    first = jnp.maximum(top - 1, 0)
    return first, pl.ds(pl.multiple_of(first * GROUP, GROUP), 2 * GROUP)


def allowed_pairs(first, top, q_places, starts):
    k_places = first * GROUP + lax.broadcasted_iota(jnp.int32, (2 * GROUP, 1), 0)
    return (k_places <= jnp.minimum(q_places, top * GROUP + GROUP - 1)) & (k_places >= starts)


def group_rows(index):
    return pl.ds(pl.multiple_of(index * GROUP, GROUP), GROUP)


def project_kernel(count, pieces, *refs):
    tok_refs = refs[:count]
    if pieces:
        table_ref, own_ref, far_ref, row_ref, bias_ref, a_ref, q_ref, kv_ref, w_ref = refs[count:]
        for s, ref in enumerate((own_ref, far_ref)):
            for f in range(ref.shape[0]):
                at = pl.multiple_of(table_ref[s * ref.shape[0] + f] * 96, 96)
                w_ref[pl.ds(at, 96), :] = ref[f, :96, :]
    else:
        w_ref, row_ref, bias_ref, a_ref, q_ref, kv_ref = refs[count:]
    at = 0
    for ref in tok_refs:

        n = ref.shape[0]
        to = slice(at, at + n)
        value = ref[...].astype(F32)
        centred = value - jnp.mean(value, axis=1, keepdims=True)
        variance = jnp.mean(centred * centred, axis=1, keepdims=True)
        normed = centred * lax.rsqrt(variance + 1e-05) * row_ref[0:1, :] + row_ref[1:2, :]
        normed = normed.astype(BF16)
        a_ref[to, :] = normed
        out = jnp.dot(normed, w_ref[...], preferred_element_type=F32) + bias_ref[0:1, :]
        kv_ref[to, :] = out[:, :WIDE].astype(BF16)
        none = jnp.zeros((n, DH), BF16)
        heads = []
        for h in range(HPG):
            lane = WIDE + h * DH
            heads += [(out[:, lane : lane + DH] * SCALE2).astype(BF16), none]
        q_ref[to, :] = jnp.concatenate(heads, axis=1)
        at += n


def project(toks, weights, norm_rows, bias):
    n = sum(t.shape[0] for t in toks)
    full = pl.BlockSpec(memory_space=VM)
    pieces = len(weights) > 1
    specs = [full] * (len(toks) + len(weights) + 2)
    outs = [
        jax.ShapeDtypeStruct((n, D), BF16),
        jax.ShapeDtypeStruct((n, WIDE), BF16),
        jax.ShapeDtypeStruct((n, WIDE), BF16),
    ]
    if pieces:
        specs[len(toks)] = pl.BlockSpec(memory_space=SMEM)
        outs.append(jax.ShapeDtypeStruct((D, 3 * HC), BF16))
    return pl.pallas_call(
        functools.partial(project_kernel, len(toks), pieces),
        name="project",
        in_specs=specs,
        out_specs=[full] * len(outs),
        out_shape=outs,
        cost_estimate=cost(4 + n // 512),
    )(*toks, *weights, norm_rows, bias)


ROWS = DH + 16


def forward_kernel(chunks, key_chunks, *refs):
    dealt_ref, bound_ref = refs[:2]
    q_refs = refs[2 : 2 + chunks]
    kv_refs = refs[2 + chunks : 2 + chunks + key_chunks]
    o_refs = refs[2 + chunks + key_chunks : 2 + chunks + key_chunks + TP]
    ot_ref, lse_ref, *kept_refs = refs[2 + chunks + key_chunks + TP :]
    qt_out, kv_out, kt_out, qt_ref, kv_ref, kt_ref, vt_ref, o_ref, acc_ref, turn_ref, sems = (
        kept_refs
    )
    copies = [
        pltpu.make_async_copy(source, to, sems.at[i])
        for i, (source, to) in enumerate(((qt_ref, qt_out), (kv_ref, kv_out), (kt_ref, kt_out)))
    ]
    for h in range(HPG):
        vt_ref[h * ROWS + DH : (h + 1) * ROWS, :] = jnp.ones((16, vt_ref.shape[1]), BF16)
    at = 0
    for ref in kv_refs:

        def load(j, c, ref=ref, at=at):
            rows = group_rows(dealt_ref[at + j])
            block = ref[group_rows(j), :]
            kv_ref[rows, :] = block
            turned = block.T
            for h in range(HPG):
                kt_ref[h * DH : (h + 1) * DH, rows] = turned[h * HW : h * HW + DH, :]
                vt_ref[h * ROWS : h * ROWS + DH, rows] = turned[h * HW + DH : (h + 1) * HW, :]
            return c

        count = ref.shape[0] // GROUP
        lax.fori_loop(0, count, load, None)
        at += count
    at = 0
    for ref in q_refs:

        def turn(j, c, ref=ref, at=at):
            qt_ref[:, group_rows(at + j)] = ref[group_rows(j), :].T
            return c

        count = ref.shape[0] // GROUP
        lax.fori_loop(0, count, turn, None)
        at += count

    for copy in copies:
        copy.start()

    def one(i, c):
        group = dealt_ref[i]
        rows = group_rows(i)
        q_places, starts, low, mid = block_bounds(group, bound_ref)
        acc_ref[...] = jnp.zeros_like(acc_ref)

        def visit(top, masked, carry):
            first, cols = pair_rows(top)
            allowed = allowed_pairs(first, top, q_places, starts) if masked else None
            out = []
            for h in range(HPG):
                lanes = slice(h * HW, (h + 1) * HW)
                s = jnp.dot(kv_ref[cols, lanes], qt_ref[lanes, rows], preferred_element_type=F32)
                if masked:
                    s = jnp.where(allowed, s, NEG)
                old = carry[h]
                new = jnp.maximum(old, jnp.max(s, axis=0, keepdims=True))
                p = jnp.exp2(s - new).astype(BF16)
                part = slice(h * ROWS, (h + 1) * ROWS)
                acc_ref[part, :] = acc_ref[part, :] * jnp.exp2(old - new) + jnp.dot(
                    vt_ref[part, cols], p, preferred_element_type=F32
                )
                out.append(new)
            return tuple(out)

        start = tuple(jnp.full((1, GROUP), NEG, F32) for _ in range(HPG))
        highest = sweep(group, low, mid, visit, start)
        for h in range(HPG):
            total = acc_ref[h * ROWS + DH : h * ROWS + DH + 1, :]
            part = slice(h * DH, (h + 1) * DH)
            turn_ref[part, :] = acc_ref[h * ROWS : h * ROWS + DH, :] / total
            lse_ref[h : h + 1, rows] = highest[h] + jnp.log2(total)
        ot_ref[:, rows] = turn_ref[0:HC, :]
        o_ref[rows, :] = turn_ref[...].T.astype(BF16)
        return c

    turn_ref[...] = jnp.zeros_like(turn_ref)
    lax.fori_loop(0, o_ref.shape[0] // GROUP, one, None)
    for m, ref in enumerate(o_refs):
        half = ref.shape[0]
        low = o_ref[2 * m * half : (2 * m + 1) * half, :HC]
        high = o_ref[(2 * m + 1) * half : (2 * m + 2) * half, :HC]
        ref[...] = jnp.concatenate([low, high], axis=1)
    for copy in copies:
        copy.wait()


def attend_forward(dealt, bounds, queries, pairs):
    n = sum(q.shape[0] for q in queries)
    s = sum(p.shape[0] for p in pairs)
    return pl.pallas_call(
        functools.partial(forward_kernel, len(queries), len(pairs)),
        name="attend_forward",
        in_specs=[pl.BlockSpec(memory_space=SMEM)] * 2
        + [pl.BlockSpec(memory_space=VM)] * (len(queries) + len(pairs)),
        out_specs=[pl.BlockSpec(memory_space=VM)] * (TP + 2)
        + [pl.BlockSpec(memory_space=pl.ANY)] * 3,
        out_shape=[jax.ShapeDtypeStruct((n // TP // 2, 2 * HC), BF16)] * TP
        + [
            jax.ShapeDtypeStruct((HC, n), F32),
            jax.ShapeDtypeStruct((8, n), F32),
            jax.ShapeDtypeStruct((WIDE, n), BF16),
            jax.ShapeDtypeStruct((s, WIDE), BF16),
            jax.ShapeDtypeStruct((HC, s), BF16),
        ],
        scratch_shapes=[
            pltpu.VMEM((WIDE, n), BF16),
            pltpu.VMEM((s, WIDE), BF16),
            pltpu.VMEM((HC, s), BF16),
            pltpu.VMEM((HPG * ROWS, s), BF16),
            pltpu.VMEM((n, LANES), BF16),
            pltpu.VMEM((HPG * ROWS, GROUP), F32),
            pltpu.VMEM((LANES, GROUP), F32),
            pltpu.SemaphoreType.DMA((3,)),
        ],
        cost_estimate=cost(30),
    )(dealt, bounds, *queries, *pairs)


def backward_kernel(base, chunks, dealt_ref, bound_ref, qt_ref, kv_ref, kt_ref, ot_ref, lse_ref, *refs):
    q_refs = refs[:chunks]
    do_refs = refs[chunks : chunks + TP]
    dq_ref, own_ref, other_ref, q_ref, do_ref, dot_ref, acc_ref, sum_ref = refs[chunks + TP :]
    h = base + pl.program_id(0)
    n = dq_ref.shape[0]
    sum_ref[...] = jnp.zeros_like(sum_ref)
    at = 0
    for ref in q_refs:
        q_ref[at : at + ref.shape[0], :] = ref[...]
        at += ref.shape[0]
    half = do_refs[0].shape[0]
    none = jnp.zeros((half, DH), BF16)
    for m, ref in enumerate(do_refs):
        for j in range(2):
            block = ref[:, j * DH : (j + 1) * DH]
            part = slice((2 * m + j) * half, (2 * m + j + 1) * half)
            wide = jnp.concatenate([none, block], axis=1)
            do_ref[part, :] = wide
            dot_ref[:, part] = wide.T

    def one(i, c):
        group = dealt_ref[i]
        rows = group_rows(i)
        q_places, starts, low, mid = block_bounds(group, bound_ref)
        delta = jnp.sum(dot_ref[DH:, rows].astype(F32) * ot_ref[:, rows], axis=0, keepdims=True)
        lse = lse_ref[pl.ds(h, 1), rows]
        acc_ref[...] = jnp.zeros_like(acc_ref)

        def visit(top, masked, c):
            first, cols = pair_rows(top)
            kv = kv_ref[cols, :]
            s = jnp.dot(kv, qt_ref[:, rows], preferred_element_type=F32)
            dp = jnp.dot(kv, dot_ref[:, rows], preferred_element_type=F32)
            if masked:
                s = jnp.where(allowed_pairs(first, top, q_places, starts), s, NEG)
            p = jnp.exp2(s - lse)
            d = (p * (dp - delta)).astype(BF16)
            acc_ref[...] += jnp.dot(kt_ref[:, cols], d, preferred_element_type=F32)
            sum_ref[cols, :] += jnp.dot(
                d, q_ref[rows, :], preferred_element_type=F32
            ) + jnp.dot(p.astype(BF16), do_ref[rows, :], preferred_element_type=F32)
            return c

        sweep(group, low, mid, visit, jnp.int32(0))
        dq_ref[rows, :] = (acc_ref[...] * DH**-0.5).T.astype(BF16)
        return c

    lax.fori_loop(0, n // GROUP, one, None)
    lane = lax.broadcasted_iota(jnp.int32, (1, HW), 1)
    scale = jnp.where(lane < DH, DH**-0.5 / SCALE2, 1.0)

    def store(b, c):
        own_ref[group_rows(b), :] = sum_ref[group_rows(dealt_ref[b]), :] * scale
        return c

    lax.fori_loop(0, n // GROUP, store, None)

    def other(b, c):
        source = group_rows(dealt_ref[n // GROUP + b])
        other_ref[group_rows(b), :] = (sum_ref[source, :] * scale).astype(BF16)
        return c

    lax.fori_loop(0, other_ref.shape[0] // GROUP, other, None)


def attend_backward(base, count, dealt, bounds, queries, qt, kv, kt, ot, lse, grads):
    n = ot.shape[1]
    s = kv.shape[0]
    full = pl.BlockSpec(memory_space=VM)
    return pl.pallas_call(
        functools.partial(backward_kernel, base, len(queries)),
        name="attend_backward",
        grid=(count,),
        in_specs=[pl.BlockSpec(memory_space=SMEM)] * 2
        + [
            pl.BlockSpec((HW, n), lambda i: (base + i, 0)),
            pl.BlockSpec((s, HW), lambda i: (0, base + i)),
            pl.BlockSpec((DH, s), lambda i: (base + i, 0)),
            pl.BlockSpec((DH, n), lambda i: (base + i, 0)),
            full,
        ]
        + [pl.BlockSpec((q.shape[0], HW), lambda i: (0, base + i)) for q in queries]
        + [pl.BlockSpec((g.shape[0], HW), lambda i: (0, base + i)) for g in grads],
        out_specs=[
            pl.BlockSpec((None, n, DH), lambda i: (i, 0, 0)),
            pl.BlockSpec((None, n, HW), lambda i: (i, 0, 0)),
            pl.BlockSpec((None, s - n, HW), lambda i: (i, 0, 0)),
        ],
        out_shape=[
            jax.ShapeDtypeStruct((count, n, DH), BF16),
            jax.ShapeDtypeStruct((count, n, HW), F32),
            jax.ShapeDtypeStruct((count, s - n, HW), BF16),
        ],
        scratch_shapes=[
            pltpu.VMEM((n, HW), BF16),
            pltpu.VMEM((n, HW), BF16),
            pltpu.VMEM((HW, n), BF16),
            pltpu.VMEM((DH, GROUP), F32),
            pltpu.VMEM((s, HW), F32),
        ],
        cost_estimate=cost(16 * count),
    )(dealt, bounds, qt, kv, kt, ot, lse, *queries, *grads)


def finish_kernel(shifts, *refs):
    sets = 2 + shifts

    def heads(k):
        first, rest = refs[2 * k : 2 * k + 2]
        return [first.at[0]] + [rest.at[h] for h in range(HPG - 1)]

    dq_refs = heads(0)
    own_refs = heads(1)
    came_refs = [ref for s in range(shifts) for ref in heads(2 + s)]
    w_ref = refs[2 * sets]
    outs = refs[2 * sets + 1 :]
    sums_ref, first_send, first_keep, second_send, second_keep = outs[TP:]
    sums_ref[...] = jnp.zeros_like(sums_ref)
    size = outs[0].shape[0]
    half = size // 2
    for m in range(TP):

        def part(i, c, m=m):
            to = pl.ds(pl.multiple_of(i * 128, 128), 128)
            rows = pl.ds(pl.multiple_of(m * size + i * 128, 128), 128)
            pieces = []
            for h in range(HPG):
                value = own_refs[h][rows, :]
                for s in range(shifts):
                    value = value + came_refs[s * HPG + h][rows, :].astype(F32)
                pieces.append(value.astype(BF16))
            for h in range(HPG):
                pieces.append(dq_refs[h][rows, :])
            whole = jnp.concatenate(pieces, axis=1)
            outs[m][to, :] = whole
            sums_ref[0:1, :] += jnp.sum(whole.astype(F32), axis=0, keepdims=True)
            return c

        lax.fori_loop(0, size // 128, part, None)
        for j in range(2):
            value = lax.dot_general(
                outs[m][j * half : (j + 1) * half, :],
                w_ref[...],
                NT,
                preferred_element_type=F32,
            ).astype(BF16)
            if j == 0:
                (first_send if m % 2 else first_keep)[m // 2] = value
            else:
                (second_send if m // 2 else second_keep)[m % 2] = value


def finish(dqs, owns, cames, weight):
    n = dqs[0].shape[1]
    full = pl.BlockSpec(memory_space=VM)
    shifts = len(cames) // 2
    shape = jax.ShapeDtypeStruct
    return pl.pallas_call(
        functools.partial(finish_kernel, shifts),
        name="finish",
        in_specs=[full] * ((2 + shifts) * 2 + 1),
        out_specs=[full] * (TP + 5),
        out_shape=[shape((n // TP, 3 * HC), BF16)] * TP
        + [shape((8, 3 * HC), F32)]
        + [shape((2, n // TP // 2, D), BF16)] * 4,
        cost_estimate=cost(10),
    )(*dqs, *owns, *cames, weight)


TN = (((0,), (0,)), ((), ()))


def columns_kernel(chunks, place_ref, *refs):
    def heads(k):
        first, rest = refs[2 * k : 2 * k + 2]
        return [first.at[0]] + [rest.at[h] for h in range(HPG - 1)]

    dq_refs, own_refs, came_refs = heads(0), heads(1), heads(2)
    w_ref, norm_ref, narrow_ref, broad_ref = refs[6:10]
    a_hbm = refs[10 : 10 + chunks]
    keep_ref, send_ref, *part_hbm = refs[10 + chunks : 16 + chunks]
    out_ref, turn_ref, a_ref, g_ref, part_ref, sums_ref, sems = refs[16 + chunks :]
    loads = []
    at = 0
    for i, ref in enumerate(a_hbm):
        to = a_ref.at[pl.ds(at, ref.shape[0])]
        loads.append(pltpu.make_async_copy(ref, to, sems.at[i]))
        at += ref.shape[0]
    for load in loads:
        load.start()
    width = 3 * HC
    size = g_ref.shape[0] // TP
    half = size // 2
    sums_ref[...] = jnp.zeros_like(sums_ref)

    def part(i, c):
        rows = group_rows(i)
        pieces = []
        for h in range(HPG):
            value = own_refs[h][rows, :] + came_refs[h][rows, :].astype(F32)
            pieces.append(value.astype(BF16))
        for h in range(HPG):
            pieces.append(dq_refs[h][rows, :])
        whole = jnp.concatenate(pieces, axis=1)
        g_ref[rows, :] = whole
        sums_ref[0:1, :] += jnp.sum(whole.astype(F32), axis=0, keepdims=True)
        return c

    lax.fori_loop(0, g_ref.shape[0] // GROUP, part, None)
    stores = [
        pltpu.make_async_copy(part_ref.at[i], part_hbm[i], sems.at[chunks + i]) for i in range(4)
    ]
    for m in range(TP):
        value = lax.dot_general(
            g_ref[m * size : (m + 1) * size, :], w_ref[...], NT, preferred_element_type=F32
        ).astype(BF16)
        part_ref[0 if m % 2 else 1, m // 2] = value[:half]
        part_ref[2 if m // 2 else 3, m % 2] = value[half:]
    for store in stores:
        store.start()
    for load in loads:
        load.wait()
    for j in range(D // GROUP):
        lanes = slice(j * GROUP, (j + 1) * GROUP)
        out_ref[lanes, :width] = lax.dot_general(
            a_ref[:, lanes], g_ref[...], TN, preferred_element_type=F32
        )
    sums = sums_ref[0:1, :]
    weight = w_ref[...].astype(F32)
    turned = sums_ref[...].T
    query = turned[WIDE:, 0:1]
    value = jnp.concatenate(
        [turned[h * HW + DH : (h + 1) * HW, 0:1] for h in range(HPG)], axis=0
    )
    lane = lax.broadcasted_iota(jnp.int32, (1, 8), 1)
    norms = norm_ref[...].T
    direct = jnp.sum(out_ref[:, :width] * weight, axis=1, keepdims=True)
    shift = jnp.sum(weight * sums, axis=1, keepdims=True)
    gain = (direct - norms[:, 1:2] * shift) / norms[:, 0:1]
    narrow = narrow_ref[...].T
    out_ref[:, width:] = jnp.zeros((D, 64), F32)
    out_ref[:, width : width + 8] = jnp.where(lane >= 2, narrow, 0.0)
    for m in range(TP):
        at = pl.ds(pl.multiple_of((place_ref[0] ^ m) * HC, HC), HC)
        piece = narrow[m * HC : (m + 1) * HC, :]
        out_ref[at, width : width + 8] += jnp.where(lane < 2, piece, 0.0)
    out_ref[:, width + 8 : width + 16] = jnp.where(lane == 0, gain, 0.0) + jnp.where(
        lane == 1, shift, 0.0
    )
    own = pl.ds(pl.multiple_of(place_ref[0] * HC, HC), HC)
    out_ref[own, width + 8 : width + 16] += jnp.where(lane == 2, query, 0.0) + jnp.where(
        lane == 3, value, 0.0
    )
    turn_ref[...] = broad_ref[...].T

    def spread(b, c):
        for q in range(4):
            source = pl.ds(pl.multiple_of(b * 96 + q * 24, 8), 24)
            at = width + 16 + 8 * q
            out_ref[pl.ds(pl.multiple_of(b * 24, 8), 24), at : at + 8] = turn_ref[source, :]
        return c

    lax.fori_loop(0, FF // 96, spread, None)
    half = HC // 2
    for g in range(TP):
        mine = pl.multiple_of(g * HC + place_ref[1] * half, half)
        other = pl.multiple_of(g * HC + (1 - place_ref[1]) * half, half)
        keep_ref[g] = out_ref[pl.ds(mine, half), :]
        send_ref[g] = out_ref[pl.ds(other, half), :]
    for store in stores:
        store.wait()


def columns(place, dqs, owns, cames, weight, norms, narrow, broad, normed):
    n = dqs[0].shape[1]
    full = pl.BlockSpec(memory_space=VM)
    away = pl.BlockSpec(memory_space=pl.ANY)
    shape = jax.ShapeDtypeStruct
    out = shape((TP, HC // 2, 3 * HC + 64), F32)
    part = (2, n // TP // 2, D)
    return pl.pallas_call(
        functools.partial(columns_kernel, len(normed)),
        name="columns",
        in_specs=[pl.BlockSpec(memory_space=SMEM)] + [full] * 10 + [away] * len(normed),
        out_specs=[full] * 2 + [away] * 4,
        out_shape=[out, out] + [shape(part, BF16)] * 4,
        scratch_shapes=[
            pltpu.VMEM((D, 3 * HC + 64), F32),
            pltpu.VMEM((FF, 8), F32),
            pltpu.VMEM((n, D), BF16),
            pltpu.VMEM((n, 3 * HC), BF16),
            pltpu.VMEM((4,) + part, BF16),
            pltpu.VMEM((8, 3 * HC), F32),
            pltpu.SemaphoreType.DMA((4 + len(normed),)),
        ],
        cost_estimate=cost(14),
    )(place, *dqs, *owns, *cames, weight, norms, narrow, broad, *normed)


def weight_grads_kernel(
    place_ref,
    u_ref,
    datt_ref,
    a2_ref,
    df_ref,
    u2_ref,
    dz_ref,
    keep_ref,
    send_ref,
    back_ref,
    in_ref,
    out_ref,
    sems,
):
    hg = place_ref[0]
    qs = place_ref[1]

    def each(source, k, rows, sem, act):
        block = (k // 2) ^ hg
        part = 0 if rows < 432 else 1
        slot = (block % 2) * 2 + block // 2 if part == 0 else block
        to = pl.ds(rows % 432, source.shape[0])
        kept = k % 2 == qs
        pl.when(kept)(
            lambda: act(pltpu.make_async_copy(source, keep_ref.at[part, slot, to], sem))
        )
        pl.when(jnp.logical_not(kept))(
            lambda: act(pltpu.make_async_copy(source, send_ref.at[part, slot, to], sem))
        )

    def start(source, k, rows, sem):
        each(source, k, rows, sem, lambda copy: copy.start())

    def wait(source, k, rows, sem):
        each(source, k, rows, sem, lambda copy: copy.wait())

    def back_block(k):
        return back_ref.at[pl.ds(pl.multiple_of(k * 384, 384), 384)]

    def in_pieces(k):
        cut = [
            (in_ref.at[0, pl.ds(pl.multiple_of(k * 96, 48), 48)], 384),
            (in_ref.at[0, pl.ds(pl.multiple_of(k * 96 + 48, 48), 48)], 432),
        ]
        whole = pl.ds(pl.multiple_of(k * 96, 96), 96)
        return cut + [(in_ref.at[j, whole], 384 + 96 * j) for j in range(1, 4)]

    def out_block(k):
        at = ((k // 2) ^ hg) * 192 + (k % 2) * 96
        return out_ref.at[pl.ds(pl.multiple_of(at, 96), 96)]

    def back(k, c):
        lanes = pl.ds(pl.multiple_of(k * D, D), D)
        back_ref[pl.ds(pl.multiple_of(k * D, D), D), :] = lax.dot_general(
            u2_ref[:, lanes], dz_ref[...], TN, preferred_element_type=F32
        ).astype(BF16)
        for j in range(2):
            block = 2 * k + j
            start(back_block(block), block, 0, sems.at[0, block])
        return c

    lax.fori_loop(0, 4, back, None)

    def inner(j, c):
        lanes = pl.ds(pl.multiple_of(j * D, D), D)
        in_ref[j] = lax.dot_general(
            a2_ref[...], df_ref[:, lanes], TN, preferred_element_type=F32
        ).astype(BF16)
        return c

    lax.fori_loop(0, 4, inner, None)

    def send_inner(k, c):
        for j, (source, first) in enumerate(in_pieces(k)):
            start(source, k, first, sems.at[1 + j, k])
        return c

    lax.fori_loop(0, 8, send_inner, None)
    out_ref[...] = lax.dot_general(
        u_ref[...], datt_ref[...], TN, preferred_element_type=F32
    ).astype(BF16)

    def finish_all(k, c):
        start(out_block(k), k, 768, sems.at[6, k])
        wait(back_block(k), k, 0, sems.at[0, k])
        for j, (source, first) in enumerate(in_pieces(k)):
            wait(source, k, first, sems.at[1 + j, k])
        return c

    lax.fori_loop(0, 8, finish_all, None)

    def finish_out(k, c):
        wait(out_block(k), k, 768, sems.at[6, k])
        return c

    lax.fori_loop(0, 8, finish_out, None)


def weight_grads(place, u, datt, a2, df, u2, dz):
    full = pl.BlockSpec(memory_space=VM)
    out = jax.ShapeDtypeStruct((2, TP, 432, D), BF16)
    return pl.pallas_call(
        weight_grads_kernel,
        name="weight_grads",
        in_specs=[pl.BlockSpec(memory_space=SMEM)] + [full] * 6,
        out_specs=[pl.BlockSpec(memory_space=pl.ANY)] * 2,
        out_shape=[out, out],
        scratch_shapes=[
            pltpu.VMEM((FF, D), BF16),
            pltpu.VMEM((4, D, D), BF16),
            pltpu.VMEM((D, D), BF16),
            pltpu.SemaphoreType.DMA((7, 8)),
        ],
        cost_estimate=cost(14),
    )(place, u, datt, a2, df, u2, dz)


def settle_kernel(place_ref, total_ref, *refs):
    came_refs = refs[:3]
    out_ref, gains_ref, shifts_ref, wide_ref, wide_shifts_ref, mine_ref = refs[3:]
    hg = place_ref[0]
    mine_ref[0] = total_ref[hg]
    for m, ref in enumerate(came_refs):
        mine_ref[m + 1] = ref[...]
    blocks = [mine_ref[hg ^ g] for g in range(TP)]
    pieces = [block[:, WIDE : 3 * HC] for block in blocks]
    for part in range(2):
        for block in blocks:
            for h in range(HPG):
                at = h * HW + part * DH
                pieces.append(block[:, at : at + DH])
    out_ref[...] = jnp.concatenate(pieces, axis=1)
    tail = mine_ref[0] + mine_ref[1] + mine_ref[2] + mine_ref[3]
    turned = tail[:, 512:].T[64:, :]

    def rows(*which):
        return jnp.concatenate([turned[i : i + 1] for i in which], axis=0)

    gains_ref[...] = rows(8, 0, 2)
    shifts_ref[...] = rows(9, 10, 11, 1, 4, 3, 5)

    def wide(v):
        return jnp.concatenate([turned[16 + 8 * q + v : 17 + 8 * q + v] for q in range(4)], axis=1)

    wide_ref[...] = wide(0)
    wide_shifts_ref[...] = jnp.concatenate([wide(1), wide(2)], axis=0)


def settle(place, total, came):
    full = pl.BlockSpec(memory_space=VM)
    rows = came[0].shape[0]
    shape = jax.ShapeDtypeStruct
    return pl.pallas_call(
        settle_kernel,
        name="settle",
        in_specs=[pl.BlockSpec(memory_space=SMEM)] + [full] * 4,
        out_specs=[full] * 5,
        out_shape=[
            shape((rows, 3 * D), F32),
            shape((3, rows), F32),
            shape((7, rows), F32),
            shape((1, 4 * rows), F32),
            shape((2, 4 * rows), F32),
        ],
        scratch_shapes=[pltpu.VMEM((TP,) + came[0].shape, F32)],
        cost_estimate=cost(2),
    )(place, total, *came)


def outward_kernel(x_ref, norm_ref, dx_ref, *refs):
    out_ref = refs[6]
    half = x_ref.shape[0] // 2
    for i in range(2):
        keep, came, last = refs[3 * i : 3 * i + 3]
        rows = slice(i * half, (i + 1) * half)
        grad = keep[0].astype(F32) + came[0].astype(F32) + last[...].astype(F32)
        unit, scale = norm_parts(x_ref[rows, :].astype(F32))
        out_ref[rows, :] = dx_ref[rows, :] + norm_back(grad * norm_ref[0:1, :], unit, scale)


def outward(x, norms, dx, parts):
    full = pl.BlockSpec(memory_space=VM)
    return pl.pallas_call(
        outward_kernel,
        name="outward",
        in_specs=[full] * 9,
        out_specs=full,
        out_shape=jax.ShapeDtypeStruct(dx.shape, F32),
        cost_estimate=cost(4),
    )(x, norms, dx, *parts)


def norm_parts(value):
    centred = value - jnp.mean(value, axis=1, keepdims=True)
    scale = lax.rsqrt(jnp.mean(centred * centred, axis=1, keepdims=True) + 1e-05)
    return centred * scale, scale


def norm_back(grad, unit, scale):
    first = jnp.mean(grad, axis=1, keepdims=True)
    second = jnp.mean(grad * unit, axis=1, keepdims=True)
    return scale * (grad - first - unit * second)


def column_sum(value):
    return jnp.sum(value, axis=0, keepdims=True)


CHUNK = 3072
TILE = 256


def place_weights(place_ref, own_refs, gathered, in_ref, out_ref, back_ref):
    near, axis, axis_far, corner, corner_far = gathered
    in_ref[pl.ds(pl.multiple_of(place_ref[0] * 192, 192), 192), :] = own_refs[0][...]
    out_ref[pl.ds(pl.multiple_of(place_ref[4] * 192, 192), 192), :] = own_refs[1][...]
    back_ref[pl.ds(pl.multiple_of(place_ref[0] * D, D), D), :] = own_refs[2][...]
    sources = [
        (near, 0),
        (near, 1),
        (axis, 0),
        (axis, 1),
        (axis_far, 0),
        (axis_far, 1),
        (corner, None),
        (corner_far, None),
    ]
    for k, (ref, t) in enumerate(sources):
        c = place_ref[8 + k]
        for m in range(1, 4):
            value = ref[m - 1] if t is None else ref[t, m - 1]
            z = place_ref[m]
            cols = pl.ds(pl.multiple_of(c * 384, 384), 384)
            in_ref[pl.ds(pl.multiple_of(z * 192, 96), 96), cols] = value[0:96, 0:384]
            in_ref[pl.ds(pl.multiple_of(z * 192 + 96, 96), 96), cols] = value[0:96, 384:768]
            back_ref[pl.ds(pl.multiple_of(z * D + c * 96, 96), 96), :] = value[96:192, :]
            block = jnp.concatenate([value[192:216, 0:384], value[192:216, 384:768]], axis=0)
            at = pl.ds(pl.multiple_of(place_ref[4 + m] * 192 + (c // 2) * 48, 48), 48)
            out_ref[at, pl.ds(pl.multiple_of((c % 2) * 384, 384), 384)] = block


def middle_kernel(scattered, *refs):
    piece_refs = refs[:TP]
    x_ref, cot_ref, row_ref, wide_ref = refs[TP : TP + 4]
    refs = refs[TP + 4 :]
    if scattered:
        place_ref = refs[0]
        own_refs, gathered, refs = refs[1:4], refs[4:9], refs[9:]
        out_w_ref, in_w_ref, back_w_ref = refs[-3:]
        place_weights(place_ref, own_refs, gathered, in_w_ref, out_w_ref, back_w_ref)
        refs = refs[:-3]
    else:
        in_w_ref, out_w_ref, back_w_ref = refs[:3]
        refs = refs[3:]
    do_refs = refs[:TP]
    (
        mixed_ref,
        u_ref,
        a2_ref,
        u2_ref,
        df_ref,
        datt_ref,
        dx_ref,
        narrow_ref,
        broad_ref,
        ctx_ref,
        do_ref,
        g_ref,
        slope_ref,
        d_ref,
        da_ref,
        x1_ref,
    ) = refs[TP:]
    half = piece_refs[0].shape[0]
    for m, ref in enumerate(piece_refs):
        for j in range(2):
            ctx_ref[j * half : (j + 1) * half, m * HC : (m + 1) * HC] = ref[
                :, j * HC : (j + 1) * HC
            ]
    narrow_ref[...] = jnp.zeros_like(narrow_ref)
    broad_ref[...] = jnp.zeros_like(broad_ref)

    def tile(i, c):
        rows = pl.ds(pl.multiple_of(i * TILE, TILE), TILE)
        unit_one, scale_one = norm_parts(ctx_ref[rows, :].astype(F32))
        u = (unit_one * row_ref[0:1, :] + row_ref[1:2, :]).astype(BF16)
        u_ref[rows, :] = u
        x1 = (
            x_ref[rows, :].astype(F32)
            + jnp.dot(u, out_w_ref[...], preferred_element_type=F32)
            + row_ref[2:3, :]
        )
        x1_ref[...] = x1
        unit_two, scale_two = norm_parts(x1)
        a2 = (unit_two * row_ref[3:4, :] + row_ref[4:5, :]).astype(BF16)
        a2_ref[rows, :] = a2

        def lanes_of(j):
            return pl.ds(pl.multiple_of(j * CHUNK, CHUNK), CHUNK)

        def up(j, total):
            lanes = lanes_of(j)
            f = (
                jnp.dot(a2_ref[rows, :], in_w_ref[:, lanes], preferred_element_type=F32)
                + wide_ref[0:1, lanes]
            )
            cdf = 0.5 * (1.0 + lax.erf(f * 0.7071067811865476))
            pdf = jnp.exp(-0.5 * f * f) * 0.3989422804014327
            slope_ref[:, lanes] = cdf + f * pdf
            g = f * cdf
            g_ref[:, lanes] = g
            return total + jnp.sum(g, axis=1, keepdims=True)

        average = lax.fori_loop(0, FF // CHUNK, up, jnp.zeros((TILE, 1), F32)) / FF

        def spread(j, total):
            lanes = lanes_of(j)
            centred = g_ref[:, lanes] - average
            return total + jnp.sum(centred * centred, axis=1, keepdims=True)

        variance = lax.fori_loop(0, FF // CHUNK, spread, jnp.zeros((TILE, 1), F32)) / FF
        scale = lax.rsqrt(variance + 1e-05)

        def turn(j, carry):
            first, second = carry
            lanes = lanes_of(j)
            unit = (g_ref[:, lanes] - average) * scale
            g_ref[:, lanes] = unit
            gain = wide_ref[1:2, lanes]
            u2_ref[rows, lanes] = (unit * gain + wide_ref[2:3, lanes]).astype(BF16)
            du2 = lax.dot_general(
                cot_ref[rows, :], back_w_ref[lanes, :], NT, preferred_element_type=F32
            )
            broad_ref[0:1, lanes] += column_sum(du2 * unit)
            broad_ref[2:3, lanes] += column_sum(du2)
            grad = du2 * gain
            d_ref[:, lanes] = grad
            return (
                first + jnp.sum(grad, axis=1, keepdims=True),
                second + jnp.sum(grad * unit, axis=1, keepdims=True),
            )

        none = jnp.zeros((TILE, 1), F32)
        first, second = lax.fori_loop(0, FF // CHUNK, turn, (none, none))
        first = first / FF
        second = second / FF
        da_ref[...] = jnp.zeros_like(da_ref)

        def down(j, c):
            lanes = lanes_of(j)
            grad = scale * (d_ref[:, lanes] - first - g_ref[:, lanes] * second)
            df = (grad * slope_ref[:, lanes]).astype(BF16)
            df_ref[rows, lanes] = df
            broad_ref[1:2, lanes] += column_sum(df.astype(F32))
            da_ref[...] += lax.dot_general(
                df, in_w_ref[:, lanes], NT, preferred_element_type=F32
            )
            return c

        lax.fori_loop(0, FF // CHUNK, down, None)
        da2 = da_ref[...]
        unit_two, scale_two = norm_parts(x1_ref[...])
        narrow_ref[2:3, :] += column_sum(da2 * unit_two)
        narrow_ref[3:4, :] += column_sum(da2)
        cot = cot_ref[rows, :].astype(F32)
        dx = cot + norm_back(da2 * row_ref[3:4, :], unit_two, scale_two)
        dx_ref[rows, :] = dx
        datt = dx.astype(BF16)
        datt_ref[rows, :] = datt
        narrow_ref[4:5, :] += column_sum(datt.astype(F32))
        narrow_ref[5:6, :] += column_sum(cot)
        du = lax.dot_general(datt, out_w_ref[...], NT, preferred_element_type=F32)
        unit_one, scale_one = norm_parts(ctx_ref[rows, :].astype(F32))
        narrow_ref[0:1, :] += column_sum(du * unit_one)
        narrow_ref[1:2, :] += column_sum(du)
        do_ref[rows, :] = norm_back(du * row_ref[0:1, :], unit_one, scale_one).astype(BF16)
        mixed_ref[rows, :] = (
            jnp.dot(u2_ref[rows, :], back_w_ref[...], preferred_element_type=F32)
            + row_ref[5:6, :]
            + x1_ref[...]
        ).astype(BF16)
        return c

    lax.fori_loop(0, ctx_ref.shape[0] // TILE, tile, None)
    for m, ref in enumerate(do_refs):
        pieces = []
        for h in range(HPG):
            lanes = slice(m * HC + h * DH, m * HC + (h + 1) * DH)
            pieces += [do_ref[:half, lanes], do_ref[half:, lanes]]
        ref[...] = jnp.concatenate(pieces, axis=1)


def middle(pieces, x, cot, narrow, wide, weights):
    n = x.shape[0]
    full = pl.BlockSpec(memory_space=VM)
    shape = jax.ShapeDtypeStruct
    scattered = len(weights) > 3
    weight_specs = [full] * len(weights)
    if scattered:
        weight_specs[0] = pl.BlockSpec(memory_space=SMEM)
    return pl.pallas_call(
        functools.partial(middle_kernel, scattered),
        name="middle",
        in_specs=[full] * (TP + 4) + weight_specs,
        out_specs=[full] * (TP + 9),
        out_shape=[shape(p.shape, BF16) for p in pieces]
        + [
            shape((n, D), BF16),
            shape((n, D), BF16),
            shape((n, D), BF16),
            shape((n, FF), BF16),
            shape((n, FF), BF16),
            shape((n, D), BF16),
            shape((n, D), F32),
            shape((8, D), F32),
            shape((8, FF), F32),
        ],
        scratch_shapes=[
            pltpu.VMEM((n, D), BF16),
            pltpu.VMEM((n, D), BF16),
            pltpu.VMEM((TILE, FF), F32),
            pltpu.VMEM((TILE, FF), F32),
            pltpu.VMEM((TILE, FF), F32),
            pltpu.VMEM((TILE, D), F32),
            pltpu.VMEM((TILE, D), F32),
        ]
        + ([pltpu.VMEM(s, BF16) for s in ((D, D), (D, FF), (FF, D))] if scattered else []),
        cost_estimate=cost(36),
    )(*pieces, x, cot, narrow, wide, *weights)


def layer_norm(values, gain, shift):
    average = jnp.mean(values, axis=-1, keepdims=True)
    centred = values - average
    variance = jnp.mean(centred * centred, axis=-1, keepdims=True)
    return centred * lax.rsqrt(variance + 1e-05) * gain + shift


def outer_sum(left, right):
    return lax.dot_general(left, right, (((0,), (0,)), ((), ())), preferred_element_type=F32)


def times_transposed(left, matrix):
    return lax.dot_general(left, matrix, (((1,), (1,)), ((), ())), preferred_element_type=F32)


def tie(value, *before):
    return lax.optimization_barrier((value, before))[0]


def pick(array, index, axis=0):
    return lax.dynamic_index_in_dim(array, index, axis, keepdims=False)


def make_local(ctx_size, fsdp_size):
    nq = ctx_size // TP
    fast = ctx_size == 8 and fsdp_size == 4

    def over_heads(value, mask):
        return lax.ppermute(
            value, "ctx", [(i, ((i // nq) ^ mask) * nq + i % nq) for i in range(ctx_size)]
        )

    def over_rows(value, shift):
        return lax.ppermute(
            value,
            "ctx",
            [(i, (i // nq) * nq + (i % nq - shift) % nq) for i in range(ctx_size)],
        )

    def over_fsdp(value, mask):
        return lax.ppermute(value, "fsdp", [(i, i ^ mask) for i in range(fsdp_size)])

    def over_split(value, masks):
        return lax.ppermute(
            value,
            "ctx",
            [(i, ((i // nq) ^ masks[i % nq]) * nq + i % nq) for i in range(ctx_size)],
        )

    moves = (over_heads, over_rows, over_fsdp, over_split)

    def exchange_heads(own, halves):
        one = over_heads(own, 1)
        two = over_heads(own, 2)
        first, second = halves
        low = over_heads(first(one), 2)
        high = over_heads(second(two), 1)
        return one, two, low, high

    def local(
        tokens,
        cotangent,
        lengths,
        dealing,
        qkv_weight,
        out_weight,
        in_weight,
        back_weight,
        norm_gains,
        shifts,
        ffn_gain,
        ffn_shifts,
    ):
        ctx = lax.axis_index("ctx")
        fs = lax.axis_index("fsdp")
        hg = ctx // nq
        qs = ctx % nq
        rows = tokens.shape[1]
        shard = qkv_weight.shape[0]
        deal_row = dealing[0]
        group_count = deal_row.shape[0]
        per = rows // GROUP
        bounds = jnp.cumsum(lengths[0])
        members = [
            [((hg ^ m) * nq + (qs + s) % nq) * per + j for m in range(TP) for j in range(per)]
            for s in range(nq)
        ]
        stored = jnp.stack([g for part in members for g in part]).astype(jnp.int32)
        onehot = (stored[:, None] == jnp.arange(group_count, dtype=jnp.int32)[None, :]).astype(
            jnp.int32
        )
        dealt = jnp.sum(onehot * deal_row[None, :], axis=1)
        mine = tokens[0]
        half = rows // 2
        one, two, low, high = exchange_heads(mine, (lambda a: a[:half], lambda a: a[half:]))
        chunks = (mine, one, two, low, high)

        def own_columns(weight):
            def take(at, size):
                value = weight[:, at : at + size]
                for g in range(1, TP):
                    other = weight[:, at + g * HC : at + g * HC + size]
                    value = jnp.where(hg == g, other, value)
                return value

            out = []
            for h in range(HPG):
                out += [take(D + h * DH, DH), take(2 * D + h * DH, DH)]
            return jnp.concatenate(out + [take(0, HC)], axis=1)

        feature = norm_gains.shape[1]
        narrow_rows = jnp.concatenate([norm_gains, shifts], axis=0)
        broad_rows = jnp.concatenate([ffn_gain[None], ffn_shifts], axis=0).reshape(12, feature)
        small = jnp.concatenate(
            [
                jnp.pad(narrow_rows, ((0, 6), (0, HC - feature))),
                jnp.pad(broad_rows, ((0, 4), (0, 2 * HC - feature))),
            ],
            axis=1,
        )
        span = shard // nq
        tail = small.shape[0] // nq
        columns_half = pick(own_columns(qkv_weight).reshape(nq, span, 3 * HC), qs)
        piece = jnp.concatenate([columns_half, pick(small.reshape(nq, tail, -1), qs)], axis=0)
        came = [over_fsdp(piece, m) for m in range(1, fsdp_size)]
        parts = jnp.stack([piece] + came)
        if fast:
            shards = (in_weight, back_weight, out_weight)
            foreign = gather_pieces(weight_piece(*shards, hg * 2 + qs), came, moves)
            corner = gather_pieces(weight_piece(*shards, (hg ^ 3) * 2 + qs), foreign, moves)
            shared = [over_rows(tie(parts, one, two), 1)]
        else:
            shared = [over_rows(parts, s) for s in range(1, nq)]
        parts = jnp.stack([parts] + shared)
        if not fast:
            w_own = jnp.concatenate(
                [
                    pick(pick(parts, (h - qs) % nq), f ^ fs)[:span]
                    for f in range(fsdp_size)
                    for h in range(nq)
                ],
                axis=0,
            )
        tails = [
            jnp.concatenate(
                [pick(pick(parts, (h - qs) % nq), f ^ fs)[span:] for h in range(nq)], axis=0
            )
            for f in range(fsdp_size)
        ]
        narrow_all = jnp.concatenate([p[:10, :feature] for p in tails], axis=1).astype(F32)
        broad_all = jnp.concatenate(
            [p[:12, HC : HC + feature].reshape(3, -1) for p in tails], axis=1
        ).astype(F32)
        gains = narrow_all[:3]
        shift_rows = narrow_all[3:]
        ffn_scale = broad_all[0]
        ffn_shift_rows = broad_all[1:]

        if not fast:
            in_w = lax.all_gather(in_weight, "fsdp", axis=0, tiled=True)
            back_w = lax.all_gather(back_weight, "fsdp", axis=0, tiled=True)
            out_w = lax.all_gather(out_weight, "fsdp", axis=0, tiled=True)
            out_blocks = out_w.reshape(TP, HC, D)
            out_rel = jnp.concatenate([pick(out_blocks, hg ^ m) for m in range(TP)], axis=0)

        def own_heads(row):
            return pick(row.reshape(TP, HC), hg)

        value_bias = own_heads(shift_rows[2]).reshape(HPG, DH)
        bias = jnp.concatenate(
            [
                jnp.stack([jnp.zeros((HPG, DH), F32), value_bias], axis=1).reshape(-1),
                own_heads(shift_rows[1]),
            ]
        )[None]
        norm_rows = jnp.stack([gains[0], shift_rows[0]])
        norm_rows = jnp.pad(norm_rows, ((0, 6), (0, 0)))
        if fast:
            table = jnp.stack(
                [(f ^ fs) * nq + (qs + s) % nq for s in range(nq) for f in range(fsdp_size)]
            )
            *first, w_own = project(
                (mine, one, two), (table.astype(jnp.int32), parts[0], parts[1]), norm_rows, bias
            )
        else:
            first = project((mine, one, two), (w_own,), norm_rows, bias)
        if fast:
            gathered = gather_axis(tie(foreign, first[1]), (low, high), moves)
        projected = [first, project((low, high), (w_own,), norm_rows, bias)]
        normed = [p[0] for p in projected]
        queries = [p[1] for p in projected]
        pairs = [p[2] for p in projected]
        for s in range(1, nq):
            pairs = pairs + [over_rows(p[2], s) for p in projected]
        if fast:
            dealt = tie(dealt, gathered[0])

        *context_parts, context_t, log_total, q_turned, kv_rows, k_turned = attend_forward(
            dealt, bounds, queries, pairs
        )
        got = [context_parts[0]] + [over_heads(context_parts[m], m) for m in range(1, TP)]

        if fast:
            gathered = gather_rest(*gathered, corner, log_total, got, moves)

        def relative(row):
            blocks = row.reshape(TP, HC)
            return jnp.concatenate([pick(blocks, hg ^ m) for m in range(TP)])

        narrow = jnp.stack(
            [relative(gains[1]), relative(shift_rows[3]), shift_rows[4], gains[2], shift_rows[5]]
            + [shift_rows[6]] * 3
        )
        wide = jnp.pad(
            jnp.stack([ffn_shift_rows[0], ffn_scale, ffn_shift_rows[1]]), ((0, 5), (0, 0))
        )
        cot = cotangent[0]
        if fast:
            weights = (weight_places(hg, qs, fs), in_weight, out_weight, back_weight, *gathered)
        else:
            weights = (in_w, out_rel, back_w)
        (
            *sent,
            mixed_out,
            inner_low,
            normed_two_low,
            inner_two_low,
            hidden_low,
            branch_low,
            grad_middle,
            narrow_sums,
            broad_sums,
        ) = middle(got, mine, cot, narrow, wide, weights)
        grad_gain_one, grad_shift_three, grad_gain_two, grad_shift_five = narrow_sums[:4]
        grad_out_bias, grad_back_bias = narrow_sums[4:6]
        grad_ffn_gain, grad_in_bias, grad_ffn_shift = broad_sums[:3]

        grad_rows = [sent[0]] + [over_heads(sent[m], m) for m in range(1, TP)]
        set_rows = TP * rows
        place = jnp.stack([hg, qs, fs]).astype(jnp.int32)
        if fast:
            keep, send = weight_grads(
                tie(place, grad_rows[1]), inner_low, branch_low, normed_two_low, hidden_low, inner_two_low, cot
            )
            stage = first_stage(keep, send, moves)

        def backward_of(base, count, table):
            return attend_backward(
                base,
                count,
                table,
                bounds,
                queries,
                q_turned,
                kv_rows,
                k_turned,
                context_t,
                log_total,
                grad_rows,
            )

        def exchange(other):
            return [
                over_rows(other[:, (s - 1) * set_rows : s * set_rows], nq - s)
                for s in range(1, nq)
            ]

        table = tie(dealt, keep) if fast else dealt
        first_head = backward_of(0, 1, table)
        table = tie(dealt, first_head, stage[0]) if fast else dealt
        other_heads = backward_of(1, HPG - 1, table)
        cames = [exchange(first_head[2]), exchange(other_heads[2])]
        if fast:
            second = second_stage(stage, keep, other_heads, moves)
            cames = tie(cames, second[0])
        came = [cames[i][s] for s in range(nq - 1) for i in range(2)]
        dqs = [first_head[0], other_heads[0]]
        owns = [first_head[1], other_heads[1]]
        if fast:
            kept, sent_columns, first_send, first_keep, second_send, second_keep = columns(
                place, dqs, owns, came, w_own, norm_rows, narrow_sums, broad_sums, normed
            )
        else:
            *grads, sums, first_send, first_keep, second_send, second_keep = finish(
                dqs, owns, came, w_own
            )

        def plus(mine, came):
            return mine.astype(F32) + came.astype(F32)

        first_came = over_heads(first_send, 1)
        second_came = over_heads(second_send, 2)
        if fast:
            last, *second = second
            last = [over_heads(last[0], 2), over_heads(last[1], 1)]
            total, column_came = reduce_columns(kept, tie(sent_columns, last), fs, moves)
            first_keep, second_keep = tie((first_keep, second_keep), column_came)
        first_last = over_heads(plus(first_keep[1], first_came[1]).astype(BF16), 2)
        second_last = over_heads(plus(second_keep[1], second_came[1]).astype(BF16), 1)
        if fast:
            sides = (first_keep, first_came, first_last, second_keep, second_came, second_last)
            input_grad = outward(mine, norm_rows, grad_middle, sides)
        else:
            grad_normed = jnp.concatenate(
                [
                    plus(first_keep[0], first_came[0]) + first_last.astype(F32),
                    plus(second_keep[0], second_came[0]) + second_last.astype(F32),
                ],
                axis=0,
            )
            inputs = mine.astype(F32)
            first_pull = jax.vjp(layer_norm, inputs, gains[0], shift_rows[0])[1]
            grad_inputs_part, grad_gain_zero, grad_shift_zero = first_pull(grad_normed)
            input_grad = grad_middle + grad_inputs_part

        def absolute(row):
            blocks = row.reshape(TP, HC)
            return jnp.concatenate([pick(blocks, hg ^ m) for m in range(TP)])

        order = ctx * fsdp_size + fs
        total_devices = ctx_size * fsdp_size
        if fast:
            later = later_stages(last, *second, column_came, fs, moves)
            total = tie(total_of(total, *column_came), input_grad)
            came = [over_heads(pick(total, hg ^ m), m) for m in (1, 2, 3)]
            qkv_out, *small_out = settle(place, total, came)
            small_out = (small_out[0], small_out[1], small_out[2].reshape(-1), small_out[3])
            back_out, in_out, out_out = weight_outputs(*later, [qkv_out])
        else:

            def placed(row):
                blank = jnp.zeros((TP, HC), F32)
                return lax.dynamic_update_slice(blank, row[None], (hg, 0)).reshape(-1)

            row = sums[0]
            value_sums = row[:WIDE].reshape(HPG, 2, DH)[:, 1].reshape(-1)
            small_terms = jnp.concatenate(
                [
                    grad_gain_zero,
                    absolute(grad_gain_one),
                    grad_gain_two,
                    grad_shift_zero,
                    placed(row[WIDE:]),
                    placed(value_sums),
                    absolute(grad_shift_three),
                    grad_out_bias,
                    grad_shift_five,
                    grad_back_bias,
                    grad_ffn_gain,
                    grad_in_bias,
                    grad_ffn_shift,
                ]
            )
            axes = ("ctx", "fsdp")
            small_terms = lax.psum(small_terms, axes)
            narrow = small_terms[: 10 * D].reshape(10, total_devices, D // total_devices)
            narrow = pick(narrow, order, 1)
            broad = small_terms[10 * D :].reshape(3, total_devices, FF // total_devices)
            broad = pick(broad, order, 1)
            small_out = (narrow[:3], narrow[3:], broad[0], broad[1:])
            blocks = outer_sum(inner_low, branch_low).reshape(TP, HC, D)
            grad_out_w = jnp.concatenate([pick(blocks, hg ^ m) for m in range(TP)], axis=0)
            grad_in_w = outer_sum(normed_two_low, hidden_low)
            grad_back_w = outer_sum(inner_two_low, cot)
            back_out, in_out, out_out = (
                lax.psum_scatter(g.astype(BF16), axes, scatter_dimension=0, tiled=True).astype(F32)
                for g in (grad_back_w, grad_in_w, grad_out_w)
            )
            grad_qkv_w = outer_sum(jnp.concatenate(normed, axis=0), jnp.concatenate(grads, axis=0))
            pairs_w = grad_qkv_w[:, :WIDE].reshape(D, HPG, 2, DH)
            three = jnp.stack(
                [
                    grad_qkv_w[:, WIDE:],
                    pairs_w[:, :, 0].reshape(D, HC),
                    pairs_w[:, :, 1].reshape(D, HC),
                ],
                axis=1,
            )
            blank = jnp.zeros((D, 3, TP, HC), BF16)
            whole = lax.dynamic_update_slice(
                blank, three.astype(BF16)[:, :, None], (0, 0, hg, 0)
            ).reshape(D, 3 * D)
            qkv_out = lax.psum_scatter(whole, axes, scatter_dimension=0, tiled=True).astype(F32)
        return (
            mixed_out[None],
            input_grad[None],
            qkv_out,
            out_out,
            in_out,
            back_out,
        ) + small_out

    return local


def weight_piece(in_weight, back_weight, out_weight, c):
    cut = lax.dynamic_slice(in_weight, (0, c * 384), (192, 384))
    out_cut = lax.dynamic_slice(out_weight, (c // 2 * 48, c % 2 * 384), (48, 384))
    return jnp.concatenate(
        [
            jnp.concatenate([cut[:96], cut[96:]], axis=1),
            pick(back_weight.reshape(8, 96, D), c),
            jnp.concatenate([out_cut[:24], out_cut[24:]], axis=1),
        ],
        axis=0,
    )


def gather_pieces(piece, first, moves):
    over_heads, over_rows, over_fsdp, over_split = moves
    piece = tie(piece, *first)
    return [over_fsdp(piece, m) for m in (1, 2, 3)]


def gather_axis(foreign, before, moves):
    over_heads, over_rows, over_fsdp, over_split = moves
    foreign = jnp.stack(foreign)
    near = jnp.stack([foreign, over_rows(foreign, 1)])
    return near, over_split(tie(near, *before), (1, 2))


def gather_rest(near, axis, corner, first, then, moves):
    over_heads, over_rows, over_fsdp, over_split = moves
    axis, corner = tie((axis, jnp.stack(corner)), first, then)
    return near, axis, over_rows(axis, 1), corner, over_rows(corner, 1)


def weight_places(hg, qs, fs):
    near_x = jnp.where(qs == 0, 1, 2)
    far_x = 3 - near_x
    return jnp.stack(
        [fs ^ m for m in range(4)]
        + [fs ^ m ^ hg for m in range(4)]
        + [hg * 2 + qs, hg * 2 + 1 - qs]
        + [(hg ^ near_x) * 2 + qs, (hg ^ near_x) * 2 + 1 - qs]
        + [(hg ^ far_x) * 2 + 1 - qs, (hg ^ far_x) * 2 + qs]
        + [(hg ^ 3) * 2 + qs, (hg ^ 3) * 2 + 1 - qs]
    ).astype(jnp.int32)


def total_of(*parts):
    return functools.reduce(jnp.add, [p.astype(F32) for p in parts])


def first_stage(keep, send, moves):
    over_heads, over_rows, over_fsdp, over_split = moves
    came = over_rows(send, 1)
    return [total_of(keep[i, 2:], came[i, 2:]).astype(BF16) for i in range(2)], came


def second_stage(stage, keep, before, moves):
    over_heads, over_rows, over_fsdp, over_split = moves
    (first_send, second_send), came = stage
    arrived = [over_heads(first_send, 1), over_heads(second_send, 2)]
    keep, came = tie((keep, came), before)
    last = [total_of(keep[i, 1], came[i, 1], arrived[i][1]).astype(BF16) for i in range(2)]
    return last, keep, came, arrived


def later_stages(last, keep, came, arrived, before, fs, moves):
    over_heads, over_rows, over_fsdp, over_split = moves
    last = tie(last, before)
    whole = jnp.concatenate(
        [total_of(keep[i, 0], came[i, 0], arrived[i][0], last[i]).astype(BF16) for i in range(2)],
        axis=0,
    )
    back = whole[:384].reshape(4, 96, D)
    inner = whole[384:768].reshape(4, 4, 24, D)
    out = whole[768:].reshape(4, 24, D)

    def piece(f):
        return jnp.concatenate(
            [pick(back, f), pick(inner, f, 1).reshape(96, D), pick(out, f)], axis=0
        )

    return piece(fs), [over_fsdp(piece(fs ^ m), m) for m in (1, 2, 3)]


def weight_outputs(own, came, before):
    total = total_of(own, *tie(came, *before))
    inner = jnp.concatenate([total[96 + 24 * j : 120 + 24 * j] for j in range(4)], axis=1)
    return total[:96], inner, total[192:216]


def reduce_columns(keep, send, fs, moves):
    over_heads, over_rows, over_fsdp, over_split = moves
    kept = keep + over_rows(send, 1)
    kept = kept.reshape(TP, 4, 24, 640)
    low = kept.astype(BF16)
    return pick(kept, fs, 1), [over_fsdp(pick(low, fs ^ m, 1), m) for m in (1, 2, 3)]


def solution(mesh):
    ctx_size = mesh.shape["ctx"]
    fsdp_size = mesh.shape["fsdp"]
    in_specs = (
        P("fsdp", "ctx", None),
        P("fsdp", "ctx", None),
        P("fsdp", None),
        P("fsdp", None),
        P("fsdp", None),
        P("fsdp", None),
        P("fsdp", None),
        P("fsdp", None),
        P(None, "fsdp"),
        P(None, "fsdp"),
        P("fsdp"),
        P(None, "fsdp"),
    )
    out_specs = (
        P("fsdp", "ctx", None),
        P("fsdp", "ctx", None),
        P(("ctx", "fsdp"), None),
        P(("ctx", "fsdp"), None),
        P(("ctx", "fsdp"), None),
        P(("ctx", "fsdp"), None),
        P(None, ("ctx", "fsdp")),
        P(None, ("ctx", "fsdp")),
        P(("ctx", "fsdp")),
        P(None, ("ctx", "fsdp")),
    )
    return jax.shard_map(
        make_local(ctx_size, fsdp_size),
        mesh=mesh,
        in_specs=in_specs,
        out_specs=out_specs,
        check_vma=False,
    )
```

```python
import functools

import jax
import jax.numpy as jnp
from jax import lax
from jax.experimental import pallas as pl
from jax.experimental.pallas import tpu as pltpu
from jax.sharding import PartitionSpec as P

D = 768
H = 12
DH = 64
FF = 3072
GROUP = 256
HPG = 3
TP = H // HPG
HC = HPG * DH
LANES = 256
SCALE2 = 1.4426950408889634 * DH ** -0.5
NEG = -1e30
NT = (((1,), (1,)), ((), ()))
F32 = jnp.float32
BF16 = jnp.bfloat16

SMEM = pltpu.MemorySpace.SMEM
VM = pltpu.MemorySpace.VMEM
HW = 2 * DH
WIDE = HPG * HW


def cost(us):
    return pl.CostEstimate(flops=int(us * 4.4e9), transcendentals=0, bytes_accessed=100000)


def block_bounds(group, bound_ref):
    lane = lax.broadcasted_iota(jnp.int32, (1, GROUP), 1)
    q_places = group * GROUP + lane
    starts = jnp.zeros((1, GROUP), jnp.int32)
    first = jnp.int32(0)
    last = jnp.int32(0)
    for j in range(bound_ref.shape[0]):
        b = bound_ref[j]
        starts = jnp.where(q_places >= b, b, starts)
        first = jnp.where(group * GROUP >= b, b, first)
        last = jnp.where(group * GROUP + GROUP - 1 >= b, b, last)
    low = first // GROUP
    mid = jnp.minimum(group, (last + GROUP - 1) // GROUP)
    return q_places, starts, low, mid


def sweep(group, low, mid, visit, carry):
    pairs = (group - low + 2) // 2
    plain = jnp.clip((group - 1 - mid) // 2, 0, pairs - 1)
    carry = lax.fori_loop(1, 1 + plain, lambda t, c: visit(group - 2 * t, False, c), carry)

    def edge(u, c):
        t = jnp.where(u < pairs - 1 - plain, plain + 1 + u, 0)
        return visit(group - 2 * t, True, c)

    return lax.fori_loop(0, pairs - plain, edge, carry)


def pair_rows(top):
    first = jnp.maximum(top - 1, 0)
    return first, pl.ds(pl.multiple_of(first * GROUP, GROUP), 2 * GROUP)


def allowed_pairs(first, top, q_places, starts):
    k_places = first * GROUP + lax.broadcasted_iota(jnp.int32, (2 * GROUP, 1), 0)
    return (k_places <= jnp.minimum(q_places, top * GROUP + GROUP - 1)) & (k_places >= starts)


def group_rows(index):
    return pl.ds(pl.multiple_of(index * GROUP, GROUP), GROUP)


def project_kernel(count, pieces, *refs):
    tok_refs = refs[:count]
    if pieces:
        table_ref, own_ref, far_ref, row_ref, bias_ref, a_ref, q_ref, kv_ref, w_ref = refs[count:]
        for s, ref in enumerate((own_ref, far_ref)):
            for f in range(ref.shape[0]):
                at = pl.multiple_of(table_ref[s * ref.shape[0] + f] * 96, 96)
                w_ref[pl.ds(at, 96), :] = ref[f, :96, :]
    else:
        w_ref, row_ref, bias_ref, a_ref, q_ref, kv_ref = refs[count:]
    at = 0
    for ref in tok_refs:
        a_ref[at : at + ref.shape[0], :] = ref[...]
        at += ref.shape[0]
    step = 512

    def part(i, c):
        rows = pl.ds(pl.multiple_of(i * step, step), step)
        value = a_ref[rows, :].astype(F32)
        centred = value - jnp.mean(value, axis=1, keepdims=True)
        variance = jnp.mean(centred * centred, axis=1, keepdims=True)
        normed = centred * lax.rsqrt(variance + 1e-05) * row_ref[0:1, :] + row_ref[1:2, :]
        normed = normed.astype(BF16)
        a_ref[rows, :] = normed
        out = jnp.dot(normed, w_ref[...], preferred_element_type=F32) + bias_ref[0:1, :]
        kv_ref[rows, :] = out[:, :WIDE].astype(BF16)
        none = jnp.zeros((step, DH), BF16)
        heads = []
        for h in range(HPG):
            lane = WIDE + h * DH
            heads += [(out[:, lane : lane + DH] * SCALE2).astype(BF16), none]
        q_ref[rows, :] = jnp.concatenate(heads, axis=1)
        return c

    lax.fori_loop(0, a_ref.shape[0] // step, part, None)


def project(toks, weights, norm_rows, bias):
    n = sum(t.shape[0] for t in toks)
    full = pl.BlockSpec(memory_space=VM)
    pieces = len(weights) > 1
    specs = [full] * (len(toks) + len(weights) + 2)
    outs = [
        jax.ShapeDtypeStruct((n, D), BF16),
        jax.ShapeDtypeStruct((n, WIDE), BF16),
        jax.ShapeDtypeStruct((n, WIDE), BF16),
    ]
    if pieces:
        specs[len(toks)] = pl.BlockSpec(memory_space=SMEM)
        outs.append(jax.ShapeDtypeStruct((D, 3 * HC), BF16))
    return pl.pallas_call(
        functools.partial(project_kernel, len(toks), pieces),
        name="project",
        in_specs=specs,
        out_specs=[full] * len(outs),
        out_shape=outs,
        cost_estimate=cost(4 + n // 512),
    )(*toks, *weights, norm_rows, bias)


ROWS = DH + 16


def forward_kernel(chunks, key_chunks, *refs):
    dealt_ref, bound_ref = refs[:2]
    q_refs = refs[2 : 2 + chunks]
    kv_refs = refs[2 + chunks : 2 + chunks + key_chunks]
    o_refs = refs[2 + chunks + key_chunks : 2 + chunks + key_chunks + TP]
    ot_ref, lse_ref, *kept_refs = refs[2 + chunks + key_chunks + TP :]
    qt_out, kv_out, kt_out, qt_ref, kv_ref, kt_ref, vt_ref, o_ref, acc_ref, turn_ref, sems = (
        kept_refs
    )
    copies = [
        pltpu.make_async_copy(source, to, sems.at[i])
        for i, (source, to) in enumerate(((qt_ref, qt_out), (kv_ref, kv_out), (kt_ref, kt_out)))
    ]
    for h in range(HPG):
        vt_ref[h * ROWS + DH : (h + 1) * ROWS, :] = jnp.ones((16, vt_ref.shape[1]), BF16)
    at = 0
    for ref in kv_refs:

        def load(j, c, ref=ref, at=at):
            rows = group_rows(dealt_ref[at + j])
            block = ref[group_rows(j), :]
            kv_ref[rows, :] = block
            turned = block.T
            for h in range(HPG):
                kt_ref[h * DH : (h + 1) * DH, rows] = turned[h * HW : h * HW + DH, :]
                vt_ref[h * ROWS : h * ROWS + DH, rows] = turned[h * HW + DH : (h + 1) * HW, :]
            return c

        count = ref.shape[0] // GROUP
        lax.fori_loop(0, count, load, None)
        at += count
    at = 0
    for ref in q_refs:

        def turn(j, c, ref=ref, at=at):
            qt_ref[:, group_rows(at + j)] = ref[group_rows(j), :].T
            return c

        count = ref.shape[0] // GROUP
        lax.fori_loop(0, count, turn, None)
        at += count

    for copy in copies:
        copy.start()

    def one(i, c):
        group = dealt_ref[i]
        rows = group_rows(i)
        q_places, starts, low, mid = block_bounds(group, bound_ref)
        acc_ref[...] = jnp.zeros_like(acc_ref)

        def visit(top, masked, carry):
            first, cols = pair_rows(top)
            allowed = allowed_pairs(first, top, q_places, starts) if masked else None
            out = []
            for h in range(HPG):
                lanes = slice(h * HW, (h + 1) * HW)
                s = jnp.dot(kv_ref[cols, lanes], qt_ref[lanes, rows], preferred_element_type=F32)
                if masked:
                    s = jnp.where(allowed, s, NEG)
                old = carry[h]
                new = jnp.maximum(old, jnp.max(s, axis=0, keepdims=True))
                p = jnp.exp2(s - new).astype(BF16)
                part = slice(h * ROWS, (h + 1) * ROWS)
                acc_ref[part, :] = acc_ref[part, :] * jnp.exp2(old - new) + jnp.dot(
                    vt_ref[part, cols], p, preferred_element_type=F32
                )
                out.append(new)
            return tuple(out)

        start = tuple(jnp.full((1, GROUP), NEG, F32) for _ in range(HPG))
        highest = sweep(group, low, mid, visit, start)
        for h in range(HPG):
            total = acc_ref[h * ROWS + DH : h * ROWS + DH + 1, :]
            part = slice(h * DH, (h + 1) * DH)
            turn_ref[part, :] = acc_ref[h * ROWS : h * ROWS + DH, :] / total
            lse_ref[h : h + 1, rows] = highest[h] + jnp.log2(total)
        ot_ref[:, rows] = turn_ref[0:HC, :]
        o_ref[rows, :] = turn_ref[...].T.astype(BF16)
        return c

    turn_ref[...] = jnp.zeros_like(turn_ref)
    lax.fori_loop(0, o_ref.shape[0] // GROUP, one, None)
    for m, ref in enumerate(o_refs):
        half = ref.shape[0]
        low = o_ref[2 * m * half : (2 * m + 1) * half, :HC]
        high = o_ref[(2 * m + 1) * half : (2 * m + 2) * half, :HC]
        ref[...] = jnp.concatenate([low, high], axis=1)
    for copy in copies:
        copy.wait()


def attend_forward(dealt, bounds, queries, pairs):
    n = sum(q.shape[0] for q in queries)
    s = sum(p.shape[0] for p in pairs)
    return pl.pallas_call(
        functools.partial(forward_kernel, len(queries), len(pairs)),
        name="attend_forward",
        in_specs=[pl.BlockSpec(memory_space=SMEM)] * 2
        + [pl.BlockSpec(memory_space=VM)] * (len(queries) + len(pairs)),
        out_specs=[pl.BlockSpec(memory_space=VM)] * (TP + 2)
        + [pl.BlockSpec(memory_space=pl.ANY)] * 3,
        out_shape=[jax.ShapeDtypeStruct((n // TP // 2, 2 * HC), BF16)] * TP
        + [
            jax.ShapeDtypeStruct((HC, n), F32),
            jax.ShapeDtypeStruct((8, n), F32),
            jax.ShapeDtypeStruct((WIDE, n), BF16),
            jax.ShapeDtypeStruct((s, WIDE), BF16),
            jax.ShapeDtypeStruct((HC, s), BF16),
        ],
        scratch_shapes=[
            pltpu.VMEM((WIDE, n), BF16),
            pltpu.VMEM((s, WIDE), BF16),
            pltpu.VMEM((HC, s), BF16),
            pltpu.VMEM((HPG * ROWS, s), BF16),
            pltpu.VMEM((n, LANES), BF16),
            pltpu.VMEM((HPG * ROWS, GROUP), F32),
            pltpu.VMEM((LANES, GROUP), F32),
            pltpu.SemaphoreType.DMA((3,)),
        ],
        cost_estimate=cost(30),
    )(dealt, bounds, *queries, *pairs)


def backward_kernel(base, chunks, dealt_ref, bound_ref, qt_ref, kv_ref, kt_ref, ot_ref, lse_ref, *refs):
    q_refs = refs[:chunks]
    do_refs = refs[chunks : chunks + TP]
    dq_ref, own_ref, other_ref, q_ref, do_ref, dot_ref, acc_ref, sum_ref = refs[chunks + TP :]
    h = base + pl.program_id(0)
    n = dq_ref.shape[0]
    sum_ref[...] = jnp.zeros_like(sum_ref)
    at = 0
    for ref in q_refs:
        q_ref[at : at + ref.shape[0], :] = ref[...]
        at += ref.shape[0]
    half = do_refs[0].shape[0]
    none = jnp.zeros((half, DH), BF16)
    for m, ref in enumerate(do_refs):
        for j in range(2):
            block = ref[:, j * DH : (j + 1) * DH]
            part = slice((2 * m + j) * half, (2 * m + j + 1) * half)
            wide = jnp.concatenate([none, block], axis=1)
            do_ref[part, :] = wide
            dot_ref[:, part] = wide.T

    def one(i, c):
        group = dealt_ref[i]
        rows = group_rows(i)
        q_places, starts, low, mid = block_bounds(group, bound_ref)
        delta = jnp.sum(dot_ref[DH:, rows].astype(F32) * ot_ref[:, rows], axis=0, keepdims=True)
        lse = lse_ref[pl.ds(h, 1), rows]
        acc_ref[...] = jnp.zeros_like(acc_ref)

        def visit(top, masked, c):
            first, cols = pair_rows(top)
            kv = kv_ref[cols, :]
            s = jnp.dot(kv, qt_ref[:, rows], preferred_element_type=F32)
            dp = jnp.dot(kv, dot_ref[:, rows], preferred_element_type=F32)
            if masked:
                s = jnp.where(allowed_pairs(first, top, q_places, starts), s, NEG)
            p = jnp.exp2(s - lse)
            d = (p * (dp - delta)).astype(BF16)
            acc_ref[...] += jnp.dot(kt_ref[:, cols], d, preferred_element_type=F32)
            sum_ref[cols, :] += jnp.dot(
                d, q_ref[rows, :], preferred_element_type=F32
            ) + jnp.dot(p.astype(BF16), do_ref[rows, :], preferred_element_type=F32)
            return c

        sweep(group, low, mid, visit, jnp.int32(0))
        dq_ref[rows, :] = (acc_ref[...] * DH**-0.5).T.astype(BF16)
        return c

    lax.fori_loop(0, n // GROUP, one, None)
    lane = lax.broadcasted_iota(jnp.int32, (1, HW), 1)
    scale = jnp.where(lane < DH, DH**-0.5 / SCALE2, 1.0)

    def store(b, c):
        own_ref[group_rows(b), :] = sum_ref[group_rows(dealt_ref[b]), :] * scale
        return c

    lax.fori_loop(0, n // GROUP, store, None)

    def other(b, c):
        source = group_rows(dealt_ref[n // GROUP + b])
        other_ref[group_rows(b), :] = (sum_ref[source, :] * scale).astype(BF16)
        return c

    lax.fori_loop(0, other_ref.shape[0] // GROUP, other, None)


def attend_backward(base, count, dealt, bounds, queries, qt, kv, kt, ot, lse, grads):
    n = ot.shape[1]
    s = kv.shape[0]
    full = pl.BlockSpec(memory_space=VM)
    return pl.pallas_call(
        functools.partial(backward_kernel, base, len(queries)),
        name="attend_backward",
        grid=(count,),
        in_specs=[pl.BlockSpec(memory_space=SMEM)] * 2
        + [
            pl.BlockSpec((HW, n), lambda i: (base + i, 0)),
            pl.BlockSpec((s, HW), lambda i: (0, base + i)),
            pl.BlockSpec((DH, s), lambda i: (base + i, 0)),
            pl.BlockSpec((DH, n), lambda i: (base + i, 0)),
            full,
        ]
        + [pl.BlockSpec((q.shape[0], HW), lambda i: (0, base + i)) for q in queries]
        + [pl.BlockSpec((g.shape[0], HW), lambda i: (0, base + i)) for g in grads],
        out_specs=[
            pl.BlockSpec((None, n, DH), lambda i: (i, 0, 0)),
            pl.BlockSpec((None, n, HW), lambda i: (i, 0, 0)),
            pl.BlockSpec((None, s - n, HW), lambda i: (i, 0, 0)),
        ],
        out_shape=[
            jax.ShapeDtypeStruct((count, n, DH), BF16),
            jax.ShapeDtypeStruct((count, n, HW), F32),
            jax.ShapeDtypeStruct((count, s - n, HW), BF16),
        ],
        scratch_shapes=[
            pltpu.VMEM((n, HW), BF16),
            pltpu.VMEM((n, HW), BF16),
            pltpu.VMEM((HW, n), BF16),
            pltpu.VMEM((DH, GROUP), F32),
            pltpu.VMEM((s, HW), F32),
        ],
        cost_estimate=cost(16 * count),
    )(dealt, bounds, qt, kv, kt, ot, lse, *queries, *grads)


def finish_kernel(shifts, *refs):
    sets = 2 + shifts

    def heads(k):
        first, rest = refs[2 * k : 2 * k + 2]
        return [first.at[0]] + [rest.at[h] for h in range(HPG - 1)]

    dq_refs = heads(0)
    own_refs = heads(1)
    came_refs = [ref for s in range(shifts) for ref in heads(2 + s)]
    w_ref = refs[2 * sets]
    outs = refs[2 * sets + 1 :]
    sums_ref, first_send, first_keep, second_send, second_keep = outs[TP:]
    sums_ref[...] = jnp.zeros_like(sums_ref)
    size = outs[0].shape[0]
    half = size // 2
    for m in range(TP):

        def part(i, c, m=m):
            to = pl.ds(pl.multiple_of(i * 128, 128), 128)
            rows = pl.ds(pl.multiple_of(m * size + i * 128, 128), 128)
            pieces = []
            for h in range(HPG):
                value = own_refs[h][rows, :]
                for s in range(shifts):
                    value = value + came_refs[s * HPG + h][rows, :].astype(F32)
                pieces.append(value.astype(BF16))
            for h in range(HPG):
                pieces.append(dq_refs[h][rows, :])
            whole = jnp.concatenate(pieces, axis=1)
            outs[m][to, :] = whole
            sums_ref[0:1, :] += jnp.sum(whole.astype(F32), axis=0, keepdims=True)
            return c

        lax.fori_loop(0, size // 128, part, None)
        for j in range(2):
            value = lax.dot_general(
                outs[m][j * half : (j + 1) * half, :],
                w_ref[...],
                NT,
                preferred_element_type=F32,
            ).astype(BF16)
            if j == 0:
                (first_send if m % 2 else first_keep)[m // 2] = value
            else:
                (second_send if m // 2 else second_keep)[m % 2] = value


def finish(dqs, owns, cames, weight):
    n = dqs[0].shape[1]
    full = pl.BlockSpec(memory_space=VM)
    shifts = len(cames) // 2
    shape = jax.ShapeDtypeStruct
    return pl.pallas_call(
        functools.partial(finish_kernel, shifts),
        name="finish",
        in_specs=[full] * ((2 + shifts) * 2 + 1),
        out_specs=[full] * (TP + 5),
        out_shape=[shape((n // TP, 3 * HC), BF16)] * TP
        + [shape((8, 3 * HC), F32)]
        + [shape((2, n // TP // 2, D), BF16)] * 4,
        cost_estimate=cost(10),
    )(*dqs, *owns, *cames, weight)


TN = (((0,), (0,)), ((), ()))


def columns_kernel(chunks, place_ref, *refs):
    def heads(k):
        first, rest = refs[2 * k : 2 * k + 2]
        return [first.at[0]] + [rest.at[h] for h in range(HPG - 1)]

    dq_refs, own_refs, came_refs = heads(0), heads(1), heads(2)
    w_ref, norm_ref, narrow_ref, broad_ref = refs[6:10]
    a_hbm = refs[10 : 10 + chunks]
    keep_ref, send_ref, *part_hbm = refs[10 + chunks : 16 + chunks]
    out_ref, turn_ref, a_ref, g_ref, part_ref, sums_ref, sems = refs[16 + chunks :]
    loads = []
    at = 0
    for i, ref in enumerate(a_hbm):
        to = a_ref.at[pl.ds(at, ref.shape[0])]
        loads.append(pltpu.make_async_copy(ref, to, sems.at[i]))
        at += ref.shape[0]
    for load in loads:
        load.start()
    width = 3 * HC
    size = g_ref.shape[0] // TP
    half = size // 2
    sums_ref[...] = jnp.zeros_like(sums_ref)

    def part(i, c):
        rows = group_rows(i)
        pieces = []
        for h in range(HPG):
            value = own_refs[h][rows, :] + came_refs[h][rows, :].astype(F32)
            pieces.append(value.astype(BF16))
        for h in range(HPG):
            pieces.append(dq_refs[h][rows, :])
        whole = jnp.concatenate(pieces, axis=1)
        g_ref[rows, :] = whole
        sums_ref[0:1, :] += jnp.sum(whole.astype(F32), axis=0, keepdims=True)
        return c

    lax.fori_loop(0, g_ref.shape[0] // GROUP, part, None)
    stores = [
        pltpu.make_async_copy(part_ref.at[i], part_hbm[i], sems.at[chunks + i]) for i in range(4)
    ]
    def split(m, c):
        rows = pl.ds(pl.multiple_of(m * size, size), size)
        value = lax.dot_general(
            g_ref[rows, :], w_ref[...], NT, preferred_element_type=F32
        ).astype(BF16)
        part_ref[1 - m % 2, m // 2] = value[:half]
        part_ref[3 - m // 2, m % 2] = value[half:]
        return c

    lax.fori_loop(0, TP, split, None)
    for store in stores:
        store.start()
    for load in loads:
        load.wait()
    for j in range(D // GROUP):
        lanes = slice(j * GROUP, (j + 1) * GROUP)
        out_ref[lanes, :width] = lax.dot_general(
            a_ref[:, lanes], g_ref[...], TN, preferred_element_type=F32
        )
    sums = sums_ref[0:1, :]
    weight = w_ref[...].astype(F32)
    turned = sums_ref[...].T
    query = turned[WIDE:, 0:1]
    value = jnp.concatenate(
        [turned[h * HW + DH : (h + 1) * HW, 0:1] for h in range(HPG)], axis=0
    )
    lane = lax.broadcasted_iota(jnp.int32, (1, 8), 1)
    norms = norm_ref[...].T
    direct = jnp.sum(out_ref[:, :width] * weight, axis=1, keepdims=True)
    shift = jnp.sum(weight * sums, axis=1, keepdims=True)
    gain = (direct - norms[:, 1:2] * shift) / norms[:, 0:1]
    narrow = narrow_ref[...].T
    out_ref[:, width:] = jnp.zeros((D, 64), F32)
    out_ref[:, width : width + 8] = jnp.where(lane >= 2, narrow, 0.0)
    for m in range(TP):
        at = pl.ds(pl.multiple_of((place_ref[0] ^ m) * HC, HC), HC)
        piece = narrow[m * HC : (m + 1) * HC, :]
        out_ref[at, width : width + 8] += jnp.where(lane < 2, piece, 0.0)
    out_ref[:, width + 8 : width + 16] = jnp.where(lane == 0, gain, 0.0) + jnp.where(
        lane == 1, shift, 0.0
    )
    own = pl.ds(pl.multiple_of(place_ref[0] * HC, HC), HC)
    out_ref[own, width + 8 : width + 16] += jnp.where(lane == 2, query, 0.0) + jnp.where(
        lane == 3, value, 0.0
    )
    turn_ref[...] = broad_ref[...].T

    def spread(b, c):
        for q in range(4):
            source = pl.ds(pl.multiple_of(b * 96 + q * 24, 8), 24)
            at = width + 16 + 8 * q
            out_ref[pl.ds(pl.multiple_of(b * 24, 8), 24), at : at + 8] = turn_ref[source, :]
        return c

    lax.fori_loop(0, FF // 96, spread, None)
    half = HC // 2
    for g in range(TP):
        mine = pl.multiple_of(g * HC + place_ref[1] * half, half)
        other = pl.multiple_of(g * HC + (1 - place_ref[1]) * half, half)
        keep_ref[g] = out_ref[pl.ds(mine, half), :]
        send_ref[g] = out_ref[pl.ds(other, half), :]
    for store in stores:
        store.wait()


def columns(place, dqs, owns, cames, weight, norms, narrow, broad, normed):
    n = dqs[0].shape[1]
    full = pl.BlockSpec(memory_space=VM)
    away = pl.BlockSpec(memory_space=pl.ANY)
    shape = jax.ShapeDtypeStruct
    out = shape((TP, HC // 2, 3 * HC + 64), F32)
    part = (2, n // TP // 2, D)
    return pl.pallas_call(
        functools.partial(columns_kernel, len(normed)),
        name="columns",
        in_specs=[pl.BlockSpec(memory_space=SMEM)] + [full] * 10 + [away] * len(normed),
        out_specs=[full] * 2 + [away] * 4,
        out_shape=[out, out] + [shape(part, BF16)] * 4,
        scratch_shapes=[
            pltpu.VMEM((D, 3 * HC + 64), F32),
            pltpu.VMEM((FF, 8), F32),
            pltpu.VMEM((n, D), BF16),
            pltpu.VMEM((n, 3 * HC), BF16),
            pltpu.VMEM((4,) + part, BF16),
            pltpu.VMEM((8, 3 * HC), F32),
            pltpu.SemaphoreType.DMA((4 + len(normed),)),
        ],
        cost_estimate=cost(14),
    )(place, *dqs, *owns, *cames, weight, norms, narrow, broad, *normed)


def weight_grads_kernel(
    place_ref,
    u_ref,
    datt_ref,
    a2_ref,
    df_ref,
    u2_ref,
    dz_ref,
    keep_ref,
    send_ref,
    back_ref,
    in_ref,
    out_ref,
    sems,
):
    hg = place_ref[0]
    qs = place_ref[1]

    def each(source, k, rows, sem, act):
        block = (k // 2) ^ hg
        part = 0 if rows < 432 else 1
        slot = (block % 2) * 2 + block // 2 if part == 0 else block
        to = pl.ds(rows % 432, source.shape[0])
        kept = k % 2 == qs
        pl.when(kept)(
            lambda: act(pltpu.make_async_copy(source, keep_ref.at[part, slot, to], sem))
        )
        pl.when(jnp.logical_not(kept))(
            lambda: act(pltpu.make_async_copy(source, send_ref.at[part, slot, to], sem))
        )

    def start(source, k, rows, sem):
        each(source, k, rows, sem, lambda copy: copy.start())

    def wait(source, k, rows, sem):
        each(source, k, rows, sem, lambda copy: copy.wait())

    def back_block(k):
        return back_ref.at[pl.ds(pl.multiple_of(k * 384, 384), 384)]

    def in_pieces(k):
        cut = [
            (in_ref.at[0, pl.ds(pl.multiple_of(k * 96, 48), 48)], 384),
            (in_ref.at[0, pl.ds(pl.multiple_of(k * 96 + 48, 48), 48)], 432),
        ]
        whole = pl.ds(pl.multiple_of(k * 96, 96), 96)
        return cut + [(in_ref.at[j, whole], 384 + 96 * j) for j in range(1, 4)]

    def out_block(k):
        at = ((k // 2) ^ hg) * 192 + (k % 2) * 96
        return out_ref.at[pl.ds(pl.multiple_of(at, 96), 96)]

    def back(k, c):
        lanes = pl.ds(pl.multiple_of(k * D, D), D)
        back_ref[pl.ds(pl.multiple_of(k * D, D), D), :] = lax.dot_general(
            u2_ref[:, lanes], dz_ref[...], TN, preferred_element_type=F32
        ).astype(BF16)
        for j in range(2):
            block = 2 * k + j
            start(back_block(block), block, 0, sems.at[0, block])
        return c

    lax.fori_loop(0, 4, back, None)

    def inner(j, c):
        lanes = pl.ds(pl.multiple_of(j * D, D), D)
        in_ref[j] = lax.dot_general(
            a2_ref[...], df_ref[:, lanes], TN, preferred_element_type=F32
        ).astype(BF16)
        return c

    lax.fori_loop(0, 4, inner, None)

    def send_inner(k, c):
        for j, (source, first) in enumerate(in_pieces(k)):
            start(source, k, first, sems.at[1 + j, k])
        return c

    lax.fori_loop(0, 8, send_inner, None)
    out_ref[...] = lax.dot_general(
        u_ref[...], datt_ref[...], TN, preferred_element_type=F32
    ).astype(BF16)

    def finish_all(k, c):
        start(out_block(k), k, 768, sems.at[6, k])
        wait(back_block(k), k, 0, sems.at[0, k])
        for j, (source, first) in enumerate(in_pieces(k)):
            wait(source, k, first, sems.at[1 + j, k])
        return c

    lax.fori_loop(0, 8, finish_all, None)

    def finish_out(k, c):
        wait(out_block(k), k, 768, sems.at[6, k])
        return c

    lax.fori_loop(0, 8, finish_out, None)


def weight_grads(place, u, datt, a2, df, u2, dz):
    full = pl.BlockSpec(memory_space=VM)
    out = jax.ShapeDtypeStruct((2, TP, 432, D), BF16)
    return pl.pallas_call(
        weight_grads_kernel,
        name="weight_grads",
        in_specs=[pl.BlockSpec(memory_space=SMEM)] + [full] * 6,
        out_specs=[pl.BlockSpec(memory_space=pl.ANY)] * 2,
        out_shape=[out, out],
        scratch_shapes=[
            pltpu.VMEM((FF, D), BF16),
            pltpu.VMEM((4, D, D), BF16),
            pltpu.VMEM((D, D), BF16),
            pltpu.SemaphoreType.DMA((7, 8)),
        ],
        cost_estimate=cost(14),
    )(place, u, datt, a2, df, u2, dz)


def settle_kernel(place_ref, total_ref, *refs):
    came_refs = refs[:3]
    out_ref, gains_ref, shifts_ref, wide_ref, wide_shifts_ref, mine_ref = refs[3:]
    hg = place_ref[0]
    mine_ref[0] = total_ref[hg]
    for m, ref in enumerate(came_refs):
        mine_ref[m + 1] = ref[...]
    blocks = [mine_ref[hg ^ g] for g in range(TP)]
    pieces = [block[:, WIDE : 3 * HC] for block in blocks]
    for part in range(2):
        for block in blocks:
            for h in range(HPG):
                at = h * HW + part * DH
                pieces.append(block[:, at : at + DH])
    out_ref[...] = jnp.concatenate(pieces, axis=1)
    tail = mine_ref[0] + mine_ref[1] + mine_ref[2] + mine_ref[3]
    turned = tail[:, 512:].T[64:, :]

    def rows(*which):
        return jnp.concatenate([turned[i : i + 1] for i in which], axis=0)

    gains_ref[...] = rows(8, 0, 2)
    shifts_ref[...] = rows(9, 10, 11, 1, 4, 3, 5)

    def wide(v):
        return jnp.concatenate([turned[16 + 8 * q + v : 17 + 8 * q + v] for q in range(4)], axis=1)

    wide_ref[...] = wide(0)
    wide_shifts_ref[...] = jnp.concatenate([wide(1), wide(2)], axis=0)


def settle(place, total, came):
    full = pl.BlockSpec(memory_space=VM)
    rows = came[0].shape[0]
    shape = jax.ShapeDtypeStruct
    return pl.pallas_call(
        settle_kernel,
        name="settle",
        in_specs=[pl.BlockSpec(memory_space=SMEM)] + [full] * 4,
        out_specs=[full] * 5,
        out_shape=[
            shape((rows, 3 * D), F32),
            shape((3, rows), F32),
            shape((7, rows), F32),
            shape((1, 4 * rows), F32),
            shape((2, 4 * rows), F32),
        ],
        scratch_shapes=[pltpu.VMEM((TP,) + came[0].shape, F32)],
        cost_estimate=cost(2),
    )(place, total, *came)


def outward_kernel(x_ref, norm_ref, dx_ref, *refs):
    out_ref = refs[6]
    half = x_ref.shape[0] // 2
    for i in range(2):
        keep, came, last = refs[3 * i : 3 * i + 3]
        rows = slice(i * half, (i + 1) * half)
        grad = keep[0].astype(F32) + came[0].astype(F32) + last[...].astype(F32)
        unit, scale = norm_parts(x_ref[rows, :].astype(F32))
        out_ref[rows, :] = dx_ref[rows, :] + norm_back(grad * norm_ref[0:1, :], unit, scale)


def outward(x, norms, dx, parts):
    full = pl.BlockSpec(memory_space=VM)
    return pl.pallas_call(
        outward_kernel,
        name="outward",
        in_specs=[full] * 9,
        out_specs=full,
        out_shape=jax.ShapeDtypeStruct(dx.shape, F32),
        cost_estimate=cost(4),
    )(x, norms, dx, *parts)


def norm_parts(value):
    centred = value - jnp.mean(value, axis=1, keepdims=True)
    scale = lax.rsqrt(jnp.mean(centred * centred, axis=1, keepdims=True) + 1e-05)
    return centred * scale, scale


def norm_back(grad, unit, scale):
    first = jnp.mean(grad, axis=1, keepdims=True)
    second = jnp.mean(grad * unit, axis=1, keepdims=True)
    return scale * (grad - first - unit * second)


def column_sum(value):
    return jnp.sum(value, axis=0, keepdims=True)


CHUNK = 1536
TILE = 256


def place_weights(place_ref, own_refs, gathered, in_ref, out_ref, back_ref):
    near, axis, axis_far, corner, corner_far = gathered
    in_ref[pl.ds(pl.multiple_of(place_ref[0] * 192, 192), 192), :] = own_refs[0][...]
    out_ref[pl.ds(pl.multiple_of(place_ref[4] * 192, 192), 192), :] = own_refs[1][...]
    back_ref[pl.ds(pl.multiple_of(place_ref[0] * D, D), D), :] = own_refs[2][...]
    sources = [
        (near, 0),
        (near, 1),
        (axis, 0),
        (axis, 1),
        (axis_far, 0),
        (axis_far, 1),
        (corner, None),
        (corner_far, None),
    ]
    for k, (ref, t) in enumerate(sources):
        c = place_ref[8 + k]
        for m in range(1, 4):
            value = ref[m - 1] if t is None else ref[t, m - 1]
            z = place_ref[m]
            cols = pl.ds(pl.multiple_of(c * 384, 384), 384)
            in_ref[pl.ds(pl.multiple_of(z * 192, 96), 96), cols] = value[0:96, 0:384]
            in_ref[pl.ds(pl.multiple_of(z * 192 + 96, 96), 96), cols] = value[0:96, 384:768]
            back_ref[pl.ds(pl.multiple_of(z * D + c * 96, 96), 96), :] = value[96:192, :]
            block = jnp.concatenate([value[192:216, 0:384], value[192:216, 384:768]], axis=0)
            at = pl.ds(pl.multiple_of(place_ref[4 + m] * 192 + (c // 2) * 48, 48), 48)
            out_ref[at, pl.ds(pl.multiple_of((c % 2) * 384, 384), 384)] = block


def middle_kernel(scattered, *refs):
    piece_refs = refs[:TP]
    x_ref, cot_ref, row_ref, wide_ref = refs[TP : TP + 4]
    refs = refs[TP + 4 :]
    if scattered:
        place_ref = refs[0]
        own_refs, gathered, refs = refs[1:4], refs[4:9], refs[9:]
        out_w_ref, in_w_ref, back_w_ref = refs[-3:]
        place_weights(place_ref, own_refs, gathered, in_w_ref, out_w_ref, back_w_ref)
        refs = refs[:-3]
    else:
        in_w_ref, out_w_ref, back_w_ref = refs[:3]
        refs = refs[3:]
    do_refs = refs[:TP]
    (
        mixed_ref,
        u_ref,
        a2_ref,
        u2_ref,
        df_ref,
        datt_ref,
        dx_ref,
        narrow_ref,
        broad_ref,
        ctx_ref,
        do_ref,
        g_ref,
        slope_ref,
        d_ref,
        da_ref,
        x1_ref,
    ) = refs[TP:]
    half = piece_refs[0].shape[0]
    for m, ref in enumerate(piece_refs):
        for j in range(2):
            ctx_ref[j * half : (j + 1) * half, m * HC : (m + 1) * HC] = ref[
                :, j * HC : (j + 1) * HC
            ]
    narrow_ref[...] = jnp.zeros_like(narrow_ref)
    broad_ref[...] = jnp.zeros_like(broad_ref)

    def tile(i, c):
        rows = pl.ds(pl.multiple_of(i * TILE, TILE), TILE)
        unit_one, scale_one = norm_parts(ctx_ref[rows, :].astype(F32))
        u = (unit_one * row_ref[0:1, :] + row_ref[1:2, :]).astype(BF16)
        u_ref[rows, :] = u
        x1 = (
            x_ref[rows, :].astype(F32)
            + jnp.dot(u, out_w_ref[...], preferred_element_type=F32)
            + row_ref[2:3, :]
        )
        x1_ref[...] = x1
        unit_two, scale_two = norm_parts(x1)
        a2 = (unit_two * row_ref[3:4, :] + row_ref[4:5, :]).astype(BF16)
        a2_ref[rows, :] = a2

        def lanes_of(j):
            return pl.ds(pl.multiple_of(j * CHUNK, CHUNK), CHUNK)

        def up(j, total):
            lanes = lanes_of(j)
            f = (
                jnp.dot(a2_ref[rows, :], in_w_ref[:, lanes], preferred_element_type=F32)
                + wide_ref[0:1, lanes]
            )
            cdf = 0.5 * (1.0 + lax.erf(f * 0.7071067811865476))
            pdf = jnp.exp(-0.5 * f * f) * 0.3989422804014327
            slope_ref[:, lanes] = cdf + f * pdf
            g = f * cdf
            g_ref[:, lanes] = g
            return total + jnp.sum(g, axis=1, keepdims=True)

        average = lax.fori_loop(0, FF // CHUNK, up, jnp.zeros((TILE, 1), F32)) / FF

        def spread(j, total):
            lanes = lanes_of(j)
            centred = g_ref[:, lanes] - average
            return total + jnp.sum(centred * centred, axis=1, keepdims=True)

        variance = lax.fori_loop(0, FF // CHUNK, spread, jnp.zeros((TILE, 1), F32)) / FF
        scale = lax.rsqrt(variance + 1e-05)

        def turn(j, carry):
            first, second = carry
            lanes = lanes_of(j)
            unit = (g_ref[:, lanes] - average) * scale
            g_ref[:, lanes] = unit
            gain = wide_ref[1:2, lanes]
            u2_ref[rows, lanes] = (unit * gain + wide_ref[2:3, lanes]).astype(BF16)
            du2 = lax.dot_general(
                cot_ref[rows, :], back_w_ref[lanes, :], NT, preferred_element_type=F32
            )
            broad_ref[0:1, lanes] += column_sum(du2 * unit)
            broad_ref[2:3, lanes] += column_sum(du2)
            grad = du2 * gain
            d_ref[:, lanes] = grad
            return (
                first + jnp.sum(grad, axis=1, keepdims=True),
                second + jnp.sum(grad * unit, axis=1, keepdims=True),
            )

        none = jnp.zeros((TILE, 1), F32)
        first, second = lax.fori_loop(0, FF // CHUNK, turn, (none, none))
        first = first / FF
        second = second / FF
        da_ref[...] = jnp.zeros_like(da_ref)

        def down(j, c):
            lanes = lanes_of(j)
            grad = scale * (d_ref[:, lanes] - first - g_ref[:, lanes] * second)
            df = (grad * slope_ref[:, lanes]).astype(BF16)
            df_ref[rows, lanes] = df
            broad_ref[1:2, lanes] += column_sum(df.astype(F32))
            da_ref[...] += lax.dot_general(
                df, in_w_ref[:, lanes], NT, preferred_element_type=F32
            )
            return c

        lax.fori_loop(0, FF // CHUNK, down, None)
        da2 = da_ref[...]
        unit_two, scale_two = norm_parts(x1_ref[...])
        narrow_ref[2:3, :] += column_sum(da2 * unit_two)
        narrow_ref[3:4, :] += column_sum(da2)
        cot = cot_ref[rows, :].astype(F32)
        dx = cot + norm_back(da2 * row_ref[3:4, :], unit_two, scale_two)
        dx_ref[rows, :] = dx
        datt = dx.astype(BF16)
        datt_ref[rows, :] = datt
        narrow_ref[4:5, :] += column_sum(datt.astype(F32))
        narrow_ref[5:6, :] += column_sum(cot)
        du = lax.dot_general(datt, out_w_ref[...], NT, preferred_element_type=F32)
        unit_one, scale_one = norm_parts(ctx_ref[rows, :].astype(F32))
        narrow_ref[0:1, :] += column_sum(du * unit_one)
        narrow_ref[1:2, :] += column_sum(du)
        do_ref[rows, :] = norm_back(du * row_ref[0:1, :], unit_one, scale_one).astype(BF16)
        mixed_ref[rows, :] = (
            jnp.dot(u2_ref[rows, :], back_w_ref[...], preferred_element_type=F32)
            + row_ref[5:6, :]
            + x1_ref[...]
        ).astype(BF16)
        return c

    lax.fori_loop(0, ctx_ref.shape[0] // TILE, tile, None)
    for m, ref in enumerate(do_refs):
        pieces = []
        for h in range(HPG):
            lanes = slice(m * HC + h * DH, m * HC + (h + 1) * DH)
            pieces += [do_ref[:half, lanes], do_ref[half:, lanes]]
        ref[...] = jnp.concatenate(pieces, axis=1)


def middle(pieces, x, cot, narrow, wide, weights):
    n = x.shape[0]
    full = pl.BlockSpec(memory_space=VM)
    shape = jax.ShapeDtypeStruct
    scattered = len(weights) > 3
    weight_specs = [full] * len(weights)
    if scattered:
        weight_specs[0] = pl.BlockSpec(memory_space=SMEM)
    return pl.pallas_call(
        functools.partial(middle_kernel, scattered),
        name="middle",
        in_specs=[full] * (TP + 4) + weight_specs,
        out_specs=[full] * (TP + 9),
        out_shape=[shape(p.shape, BF16) for p in pieces]
        + [
            shape((n, D), BF16),
            shape((n, D), BF16),
            shape((n, D), BF16),
            shape((n, FF), BF16),
            shape((n, FF), BF16),
            shape((n, D), BF16),
            shape((n, D), F32),
            shape((8, D), F32),
            shape((8, FF), F32),
        ],
        scratch_shapes=[
            pltpu.VMEM((n, D), BF16),
            pltpu.VMEM((n, D), BF16),
            pltpu.VMEM((TILE, FF), F32),
            pltpu.VMEM((TILE, FF), F32),
            pltpu.VMEM((TILE, FF), F32),
            pltpu.VMEM((TILE, D), F32),
            pltpu.VMEM((TILE, D), F32),
        ]
        + ([pltpu.VMEM(s, BF16) for s in ((D, D), (D, FF), (FF, D))] if scattered else []),
        cost_estimate=cost(36),
    )(*pieces, x, cot, narrow, wide, *weights)


def layer_norm(values, gain, shift):
    average = jnp.mean(values, axis=-1, keepdims=True)
    centred = values - average
    variance = jnp.mean(centred * centred, axis=-1, keepdims=True)
    return centred * lax.rsqrt(variance + 1e-05) * gain + shift


def outer_sum(left, right):
    return lax.dot_general(left, right, (((0,), (0,)), ((), ())), preferred_element_type=F32)


def times_transposed(left, matrix):
    return lax.dot_general(left, matrix, (((1,), (1,)), ((), ())), preferred_element_type=F32)


def tie(value, *before):
    return lax.optimization_barrier((value, before))[0]


def pick(array, index, axis=0):
    return lax.dynamic_index_in_dim(array, index, axis, keepdims=False)


def make_local(ctx_size, fsdp_size):
    nq = ctx_size // TP
    fast = ctx_size == 8 and fsdp_size == 4

    def over_heads(value, mask):
        return lax.ppermute(
            value, "ctx", [(i, ((i // nq) ^ mask) * nq + i % nq) for i in range(ctx_size)]
        )

    def over_rows(value, shift):
        return lax.ppermute(
            value,
            "ctx",
            [(i, (i // nq) * nq + (i % nq - shift) % nq) for i in range(ctx_size)],
        )

    def over_fsdp(value, mask):
        return lax.ppermute(value, "fsdp", [(i, i ^ mask) for i in range(fsdp_size)])

    def over_split(value, masks):
        return lax.ppermute(
            value,
            "ctx",
            [(i, ((i // nq) ^ masks[i % nq]) * nq + i % nq) for i in range(ctx_size)],
        )

    moves = (over_heads, over_rows, over_fsdp, over_split)

    def exchange_heads(own, halves):
        one = over_heads(own, 1)
        two = over_heads(own, 2)
        first, second = halves
        low = over_heads(first(one), 2)
        high = over_heads(second(two), 1)
        return one, two, low, high

    def local(
        tokens,
        cotangent,
        lengths,
        dealing,
        qkv_weight,
        out_weight,
        in_weight,
        back_weight,
        norm_gains,
        shifts,
        ffn_gain,
        ffn_shifts,
    ):
        ctx = lax.axis_index("ctx")
        fs = lax.axis_index("fsdp")
        hg = ctx // nq
        qs = ctx % nq
        rows = tokens.shape[1]
        shard = qkv_weight.shape[0]
        deal_row = dealing[0]
        group_count = deal_row.shape[0]
        per = rows // GROUP
        bounds = jnp.cumsum(lengths[0])
        members = [
            [((hg ^ m) * nq + (qs + s) % nq) * per + j for m in range(TP) for j in range(per)]
            for s in range(nq)
        ]
        stored = jnp.stack([g for part in members for g in part]).astype(jnp.int32)
        onehot = (stored[:, None] == jnp.arange(group_count, dtype=jnp.int32)[None, :]).astype(
            jnp.int32
        )
        dealt = jnp.sum(onehot * deal_row[None, :], axis=1)
        mine = tokens[0]
        half = rows // 2
        one, two, low, high = exchange_heads(mine, (lambda a: a[:half], lambda a: a[half:]))
        chunks = (mine, one, two, low, high)

        def own_columns(weight):
            def take(at, size):
                value = weight[:, at : at + size]
                for g in range(1, TP):
                    other = weight[:, at + g * HC : at + g * HC + size]
                    value = jnp.where(hg == g, other, value)
                return value

            out = []
            for h in range(HPG):
                out += [take(D + h * DH, DH), take(2 * D + h * DH, DH)]
            return jnp.concatenate(out + [take(0, HC)], axis=1)

        feature = norm_gains.shape[1]
        narrow_rows = jnp.concatenate([norm_gains, shifts], axis=0)
        broad_rows = jnp.concatenate([ffn_gain[None], ffn_shifts], axis=0).reshape(12, feature)
        small = jnp.concatenate(
            [
                jnp.pad(narrow_rows, ((0, 6), (0, HC - feature))),
                jnp.pad(broad_rows, ((0, 4), (0, 2 * HC - feature))),
            ],
            axis=1,
        )
        span = shard // nq
        tail = small.shape[0] // nq
        columns_half = pick(own_columns(qkv_weight).reshape(nq, span, 3 * HC), qs)
        piece = jnp.concatenate([columns_half, pick(small.reshape(nq, tail, -1), qs)], axis=0)
        came = [over_fsdp(piece, m) for m in range(1, fsdp_size)]
        parts = jnp.stack([piece] + came)
        if fast:
            shards = (in_weight, back_weight, out_weight)
            foreign = gather_pieces(weight_piece(*shards, hg * 2 + qs), came, moves)
            corner = gather_pieces(weight_piece(*shards, (hg ^ 3) * 2 + qs), foreign, moves)
            shared = [over_rows(tie(parts, one, two), 1)]
        else:
            shared = [over_rows(parts, s) for s in range(1, nq)]
        parts = jnp.stack([parts] + shared)
        if not fast:
            w_own = jnp.concatenate(
                [
                    pick(pick(parts, (h - qs) % nq), f ^ fs)[:span]
                    for f in range(fsdp_size)
                    for h in range(nq)
                ],
                axis=0,
            )
        tails = [
            jnp.concatenate(
                [pick(pick(parts, (h - qs) % nq), f ^ fs)[span:] for h in range(nq)], axis=0
            )
            for f in range(fsdp_size)
        ]
        narrow_all = jnp.concatenate([p[:10, :feature] for p in tails], axis=1).astype(F32)
        broad_all = jnp.concatenate(
            [p[:12, HC : HC + feature].reshape(3, -1) for p in tails], axis=1
        ).astype(F32)
        gains = narrow_all[:3]
        shift_rows = narrow_all[3:]
        ffn_scale = broad_all[0]
        ffn_shift_rows = broad_all[1:]

        if not fast:
            in_w = lax.all_gather(in_weight, "fsdp", axis=0, tiled=True)
            back_w = lax.all_gather(back_weight, "fsdp", axis=0, tiled=True)
            out_w = lax.all_gather(out_weight, "fsdp", axis=0, tiled=True)
            out_blocks = out_w.reshape(TP, HC, D)
            out_rel = jnp.concatenate([pick(out_blocks, hg ^ m) for m in range(TP)], axis=0)

        def own_heads(row):
            return pick(row.reshape(TP, HC), hg)

        value_bias = own_heads(shift_rows[2]).reshape(HPG, DH)
        bias = jnp.concatenate(
            [
                jnp.stack([jnp.zeros((HPG, DH), F32), value_bias], axis=1).reshape(-1),
                own_heads(shift_rows[1]),
            ]
        )[None]
        norm_rows = jnp.stack([gains[0], shift_rows[0]])
        norm_rows = jnp.pad(norm_rows, ((0, 6), (0, 0)))
        if fast:
            table = jnp.stack(
                [(f ^ fs) * nq + (qs + s) % nq for s in range(nq) for f in range(fsdp_size)]
            )
            *first, w_own = project(
                (mine, one, two), (table.astype(jnp.int32), parts[0], parts[1]), norm_rows, bias
            )
        else:
            first = project((mine, one, two), (w_own,), norm_rows, bias)
        if fast:
            gathered = gather_axis(tie(foreign, first[1]), (low, high), moves)
        projected = [first, project((low, high), (w_own,), norm_rows, bias)]
        normed = [p[0] for p in projected]
        queries = [p[1] for p in projected]
        pairs = [p[2] for p in projected]
        for s in range(1, nq):
            pairs = pairs + [over_rows(p[2], s) for p in projected]
        if fast:
            dealt = tie(dealt, gathered[0])

        *context_parts, context_t, log_total, q_turned, kv_rows, k_turned = attend_forward(
            dealt, bounds, queries, pairs
        )
        got = [context_parts[0]] + [over_heads(context_parts[m], m) for m in range(1, TP)]

        if fast:
            gathered = gather_rest(*gathered, corner, log_total, got, moves)

        def relative(row):
            blocks = row.reshape(TP, HC)
            return jnp.concatenate([pick(blocks, hg ^ m) for m in range(TP)])

        narrow = jnp.stack(
            [relative(gains[1]), relative(shift_rows[3]), shift_rows[4], gains[2], shift_rows[5]]
            + [shift_rows[6]] * 3
        )
        wide = jnp.pad(
            jnp.stack([ffn_shift_rows[0], ffn_scale, ffn_shift_rows[1]]), ((0, 5), (0, 0))
        )
        cot = cotangent[0]
        if fast:
            weights = (weight_places(hg, qs, fs), in_weight, out_weight, back_weight, *gathered)
        else:
            weights = (in_w, out_rel, back_w)
        (
            *sent,
            mixed_out,
            inner_low,
            normed_two_low,
            inner_two_low,
            hidden_low,
            branch_low,
            grad_middle,
            narrow_sums,
            broad_sums,
        ) = middle(got, mine, cot, narrow, wide, weights)
        grad_gain_one, grad_shift_three, grad_gain_two, grad_shift_five = narrow_sums[:4]
        grad_out_bias, grad_back_bias = narrow_sums[4:6]
        grad_ffn_gain, grad_in_bias, grad_ffn_shift = broad_sums[:3]

        grad_rows = [sent[0]] + [over_heads(sent[m], m) for m in range(1, TP)]
        set_rows = TP * rows
        place = jnp.stack([hg, qs, fs]).astype(jnp.int32)
        if fast:
            keep, send = weight_grads(
                tie(place, grad_rows[1]), inner_low, branch_low, normed_two_low, hidden_low, inner_two_low, cot
            )
            stage = first_stage(keep, send, moves)

        def backward_of(base, count, table):
            return attend_backward(
                base,
                count,
                table,
                bounds,
                queries,
                q_turned,
                kv_rows,
                k_turned,
                context_t,
                log_total,
                grad_rows,
            )

        def exchange(other):
            return [
                over_rows(other[:, (s - 1) * set_rows : s * set_rows], nq - s)
                for s in range(1, nq)
            ]

        table = tie(dealt, keep) if fast else dealt
        first_head = backward_of(0, 1, table)
        table = tie(dealt, first_head, stage[0]) if fast else dealt
        other_heads = backward_of(1, HPG - 1, table)
        cames = [exchange(first_head[2]), exchange(other_heads[2])]
        if fast:
            second = second_stage(stage, keep, other_heads, moves)
            cames = tie(cames, second[0])
        came = [cames[i][s] for s in range(nq - 1) for i in range(2)]
        dqs = [first_head[0], other_heads[0]]
        owns = [first_head[1], other_heads[1]]
        if fast:
            kept, sent_columns, first_send, first_keep, second_send, second_keep = columns(
                place, dqs, owns, came, w_own, norm_rows, narrow_sums, broad_sums, normed
            )
        else:
            *grads, sums, first_send, first_keep, second_send, second_keep = finish(
                dqs, owns, came, w_own
            )

        def plus(mine, came):
            return mine.astype(F32) + came.astype(F32)

        first_came = over_heads(first_send, 1)
        second_came = over_heads(second_send, 2)
        if fast:
            last, *second = second
            last = [over_heads(last[0], 2), over_heads(last[1], 1)]
            total, column_came = reduce_columns(kept, tie(sent_columns, last), fs, moves)
            first_keep, second_keep = tie((first_keep, second_keep), column_came)
        first_last = over_heads(plus(first_keep[1], first_came[1]).astype(BF16), 2)
        second_last = over_heads(plus(second_keep[1], second_came[1]).astype(BF16), 1)
        if fast:
            sides = (first_keep, first_came, first_last, second_keep, second_came, second_last)
            input_grad = outward(mine, norm_rows, grad_middle, sides)
        else:
            grad_normed = jnp.concatenate(
                [
                    plus(first_keep[0], first_came[0]) + first_last.astype(F32),
                    plus(second_keep[0], second_came[0]) + second_last.astype(F32),
                ],
                axis=0,
            )
            inputs = mine.astype(F32)
            first_pull = jax.vjp(layer_norm, inputs, gains[0], shift_rows[0])[1]
            grad_inputs_part, grad_gain_zero, grad_shift_zero = first_pull(grad_normed)
            input_grad = grad_middle + grad_inputs_part

        def absolute(row):
            blocks = row.reshape(TP, HC)
            return jnp.concatenate([pick(blocks, hg ^ m) for m in range(TP)])

        order = ctx * fsdp_size + fs
        total_devices = ctx_size * fsdp_size
        if fast:
            later = later_stages(last, *second, column_came, fs, moves)
            total = tie(total_of(total, *column_came), input_grad)
            came = [over_heads(pick(total, hg ^ m), m) for m in (1, 2, 3)]
            qkv_out, *small_out = settle(place, total, came)
            small_out = (small_out[0], small_out[1], small_out[2].reshape(-1), small_out[3])
            back_out, in_out, out_out = weight_outputs(*later, [qkv_out])
        else:

            def placed(row):
                blank = jnp.zeros((TP, HC), F32)
                return lax.dynamic_update_slice(blank, row[None], (hg, 0)).reshape(-1)

            row = sums[0]
            value_sums = row[:WIDE].reshape(HPG, 2, DH)[:, 1].reshape(-1)
            small_terms = jnp.concatenate(
                [
                    grad_gain_zero,
                    absolute(grad_gain_one),
                    grad_gain_two,
                    grad_shift_zero,
                    placed(row[WIDE:]),
                    placed(value_sums),
                    absolute(grad_shift_three),
                    grad_out_bias,
                    grad_shift_five,
                    grad_back_bias,
                    grad_ffn_gain,
                    grad_in_bias,
                    grad_ffn_shift,
                ]
            )
            axes = ("ctx", "fsdp")
            small_terms = lax.psum(small_terms, axes)
            narrow = small_terms[: 10 * D].reshape(10, total_devices, D // total_devices)
            narrow = pick(narrow, order, 1)
            broad = small_terms[10 * D :].reshape(3, total_devices, FF // total_devices)
            broad = pick(broad, order, 1)
            small_out = (narrow[:3], narrow[3:], broad[0], broad[1:])
            blocks = outer_sum(inner_low, branch_low).reshape(TP, HC, D)
            grad_out_w = jnp.concatenate([pick(blocks, hg ^ m) for m in range(TP)], axis=0)
            grad_in_w = outer_sum(normed_two_low, hidden_low)
            grad_back_w = outer_sum(inner_two_low, cot)
            back_out, in_out, out_out = (
                lax.psum_scatter(g.astype(BF16), axes, scatter_dimension=0, tiled=True).astype(F32)
                for g in (grad_back_w, grad_in_w, grad_out_w)
            )
            grad_qkv_w = outer_sum(jnp.concatenate(normed, axis=0), jnp.concatenate(grads, axis=0))
            pairs_w = grad_qkv_w[:, :WIDE].reshape(D, HPG, 2, DH)
            three = jnp.stack(
                [
                    grad_qkv_w[:, WIDE:],
                    pairs_w[:, :, 0].reshape(D, HC),
                    pairs_w[:, :, 1].reshape(D, HC),
                ],
                axis=1,
            )
            blank = jnp.zeros((D, 3, TP, HC), BF16)
            whole = lax.dynamic_update_slice(
                blank, three.astype(BF16)[:, :, None], (0, 0, hg, 0)
            ).reshape(D, 3 * D)
            qkv_out = lax.psum_scatter(whole, axes, scatter_dimension=0, tiled=True).astype(F32)
        return (
            mixed_out[None],
            input_grad[None],
            qkv_out,
            out_out,
            in_out,
            back_out,
        ) + small_out

    return local


def weight_piece(in_weight, back_weight, out_weight, c):
    cut = lax.dynamic_slice(in_weight, (0, c * 384), (192, 384))
    out_cut = lax.dynamic_slice(out_weight, (c // 2 * 48, c % 2 * 384), (48, 384))
    return jnp.concatenate(
        [
            jnp.concatenate([cut[:96], cut[96:]], axis=1),
            pick(back_weight.reshape(8, 96, D), c),
            jnp.concatenate([out_cut[:24], out_cut[24:]], axis=1),
        ],
        axis=0,
    )


def gather_pieces(piece, first, moves):
    over_heads, over_rows, over_fsdp, over_split = moves
    piece = tie(piece, *first)
    return [over_fsdp(piece, m) for m in (1, 2, 3)]


def gather_axis(foreign, before, moves):
    over_heads, over_rows, over_fsdp, over_split = moves
    foreign = jnp.stack(foreign)
    near = jnp.stack([foreign, over_rows(foreign, 1)])
    return near, over_split(tie(near, *before), (1, 2))


def gather_rest(near, axis, corner, first, then, moves):
    over_heads, over_rows, over_fsdp, over_split = moves
    axis, corner = tie((axis, jnp.stack(corner)), first, then)
    return near, axis, over_rows(axis, 1), corner, over_rows(corner, 1)


def weight_places(hg, qs, fs):
    near_x = jnp.where(qs == 0, 1, 2)
    far_x = 3 - near_x
    return jnp.stack(
        [fs ^ m for m in range(4)]
        + [fs ^ m ^ hg for m in range(4)]
        + [hg * 2 + qs, hg * 2 + 1 - qs]
        + [(hg ^ near_x) * 2 + qs, (hg ^ near_x) * 2 + 1 - qs]
        + [(hg ^ far_x) * 2 + 1 - qs, (hg ^ far_x) * 2 + qs]
        + [(hg ^ 3) * 2 + qs, (hg ^ 3) * 2 + 1 - qs]
    ).astype(jnp.int32)


def total_of(*parts):
    return functools.reduce(jnp.add, [p.astype(F32) for p in parts])


def first_stage(keep, send, moves):
    over_heads, over_rows, over_fsdp, over_split = moves
    came = over_rows(send, 1)
    return [total_of(keep[i, 2:], came[i, 2:]).astype(BF16) for i in range(2)], came


def second_stage(stage, keep, before, moves):
    over_heads, over_rows, over_fsdp, over_split = moves
    (first_send, second_send), came = stage
    arrived = [over_heads(first_send, 1), over_heads(second_send, 2)]
    keep, came = tie((keep, came), before)
    last = [total_of(keep[i, 1], came[i, 1], arrived[i][1]).astype(BF16) for i in range(2)]
    return last, keep, came, arrived


def later_stages(last, keep, came, arrived, before, fs, moves):
    over_heads, over_rows, over_fsdp, over_split = moves
    last = tie(last, before)
    whole = jnp.concatenate(
        [total_of(keep[i, 0], came[i, 0], arrived[i][0], last[i]).astype(BF16) for i in range(2)],
        axis=0,
    )
    back = whole[:384].reshape(4, 96, D)
    inner = whole[384:768].reshape(4, 4, 24, D)
    out = whole[768:].reshape(4, 24, D)

    def piece(f):
        return jnp.concatenate(
            [pick(back, f), pick(inner, f, 1).reshape(96, D), pick(out, f)], axis=0
        )

    return piece(fs), [over_fsdp(piece(fs ^ m), m) for m in (1, 2, 3)]


def weight_outputs(own, came, before):
    total = total_of(own, *tie(came, *before))
    inner = jnp.concatenate([total[96 + 24 * j : 120 + 24 * j] for j in range(4)], axis=1)
    return total[:96], inner, total[192:216]


def reduce_columns(keep, send, fs, moves):
    over_heads, over_rows, over_fsdp, over_split = moves
    kept = keep + over_rows(send, 1)
    kept = kept.reshape(TP, 4, 24, 640)
    low = kept.astype(BF16)
    return pick(kept, fs, 1), [over_fsdp(pick(low, fs ^ m, 1), m) for m in (1, 2, 3)]


def solution(mesh):
    ctx_size = mesh.shape["ctx"]
    fsdp_size = mesh.shape["fsdp"]
    in_specs = (
        P("fsdp", "ctx", None),
        P("fsdp", "ctx", None),
        P("fsdp", None),
        P("fsdp", None),
        P("fsdp", None),
        P("fsdp", None),
        P("fsdp", None),
        P("fsdp", None),
        P(None, "fsdp"),
        P(None, "fsdp"),
        P("fsdp"),
        P(None, "fsdp"),
    )
    out_specs = (
        P("fsdp", "ctx", None),
        P("fsdp", "ctx", None),
        P(("ctx", "fsdp"), None),
        P(("ctx", "fsdp"), None),
        P(("ctx", "fsdp"), None),
        P(("ctx", "fsdp"), None),
        P(None, ("ctx", "fsdp")),
        P(None, ("ctx", "fsdp")),
        P(("ctx", "fsdp")),
        P(None, ("ctx", "fsdp")),
    )
    return jax.shard_map(
        make_local(ctx_size, fsdp_size),
        mesh=mesh,
        in_specs=in_specs,
        out_specs=out_specs,
        check_vma=False,
    )
```

```python
import functools

import jax
import jax.numpy as jnp
from jax import lax
from jax.experimental import pallas as pl
from jax.experimental.pallas import tpu as pltpu
from jax.sharding import PartitionSpec as P

D = 768
H = 12
DH = 64
FF = 3072
GROUP = 256
HPG = 3
TP = H // HPG
HC = HPG * DH
LANES = 256
SCALE2 = 1.4426950408889634 * DH ** -0.5
NEG = -1e30
NT = (((1,), (1,)), ((), ()))
F32 = jnp.float32
BF16 = jnp.bfloat16

SMEM = pltpu.MemorySpace.SMEM
VM = pltpu.MemorySpace.VMEM
HW = 2 * DH
WIDE = HPG * HW


def cost(us):
    return pl.CostEstimate(flops=int(us * 4.4e9), transcendentals=0, bytes_accessed=100000)


def block_bounds(group, bound_ref):
    lane = lax.broadcasted_iota(jnp.int32, (1, GROUP), 1)
    q_places = group * GROUP + lane
    starts = jnp.zeros((1, GROUP), jnp.int32)
    first = jnp.int32(0)
    last = jnp.int32(0)
    for j in range(bound_ref.shape[0]):
        b = bound_ref[j]
        starts = jnp.where(q_places >= b, b, starts)
        first = jnp.where(group * GROUP >= b, b, first)
        last = jnp.where(group * GROUP + GROUP - 1 >= b, b, last)
    low = first // GROUP
    mid = jnp.minimum(group, (last + GROUP - 1) // GROUP)
    return q_places, starts, low, mid


def sweep(group, low, mid, visit, carry):
    pairs = (group - low + 2) // 2
    plain = jnp.clip((group - 1 - mid) // 2, 0, pairs - 1)
    carry = lax.fori_loop(1, 1 + plain, lambda t, c: visit(group - 2 * t, False, c), carry)

    def edge(u, c):
        t = jnp.where(u < pairs - 1 - plain, plain + 1 + u, 0)
        return visit(group - 2 * t, True, c)

    return lax.fori_loop(0, pairs - plain, edge, carry)


def pair_rows(top):
    first = jnp.maximum(top - 1, 0)
    return first, pl.ds(pl.multiple_of(first * GROUP, GROUP), 2 * GROUP)


def allowed_pairs(first, top, q_places, starts):
    k_places = first * GROUP + lax.broadcasted_iota(jnp.int32, (2 * GROUP, 1), 0)
    return (k_places <= jnp.minimum(q_places, top * GROUP + GROUP - 1)) & (k_places >= starts)


def group_rows(index):
    return pl.ds(pl.multiple_of(index * GROUP, GROUP), GROUP)


def project_kernel(count, pieces, *refs):
    tok_refs = refs[:count]
    if pieces:
        table_ref, own_ref, far_ref, row_ref, bias_ref, a_ref, q_ref, kv_ref, w_ref = refs[count:]
        for s, ref in enumerate((own_ref, far_ref)):
            for f in range(ref.shape[0]):
                at = pl.multiple_of(table_ref[s * ref.shape[0] + f] * 96, 96)
                w_ref[pl.ds(at, 96), :] = ref[f, :96, :]
    else:
        w_ref, row_ref, bias_ref, a_ref, q_ref, kv_ref = refs[count:]
    at = 0
    for ref in tok_refs:
        a_ref[at : at + ref.shape[0], :] = ref[...]
        at += ref.shape[0]
    step = 512

    def part(i, c):
        rows = pl.ds(pl.multiple_of(i * step, step), step)
        value = a_ref[rows, :].astype(F32)
        centred = value - jnp.mean(value, axis=1, keepdims=True)
        variance = jnp.mean(centred * centred, axis=1, keepdims=True)
        normed = centred * lax.rsqrt(variance + 1e-05) * row_ref[0:1, :] + row_ref[1:2, :]
        normed = normed.astype(BF16)
        a_ref[rows, :] = normed
        out = jnp.dot(normed, w_ref[...], preferred_element_type=F32) + bias_ref[0:1, :]
        kv_ref[rows, :] = out[:, :WIDE].astype(BF16)
        none = jnp.zeros((step, DH), BF16)
        heads = []
        for h in range(HPG):
            lane = WIDE + h * DH
            heads += [(out[:, lane : lane + DH] * SCALE2).astype(BF16), none]
        q_ref[rows, :] = jnp.concatenate(heads, axis=1)
        return c

    lax.fori_loop(0, a_ref.shape[0] // step, part, None)


def project(toks, weights, norm_rows, bias):
    n = sum(t.shape[0] for t in toks)
    full = pl.BlockSpec(memory_space=VM)
    pieces = len(weights) > 1
    specs = [full] * (len(toks) + len(weights) + 2)
    outs = [
        jax.ShapeDtypeStruct((n, D), BF16),
        jax.ShapeDtypeStruct((n, WIDE), BF16),
        jax.ShapeDtypeStruct((n, WIDE), BF16),
    ]
    if pieces:
        specs[len(toks)] = pl.BlockSpec(memory_space=SMEM)
        outs.append(jax.ShapeDtypeStruct((D, 3 * HC), BF16))
    return pl.pallas_call(
        functools.partial(project_kernel, len(toks), pieces),
        name="project",
        in_specs=specs,
        out_specs=[full] * len(outs),
        out_shape=outs,
        cost_estimate=cost(4 + n // 512),
    )(*toks, *weights, norm_rows, bias)


ROWS = DH + 16


def forward_kernel(chunks, key_chunks, *refs):
    dealt_ref, bound_ref = refs[:2]
    q_refs = refs[2 : 2 + chunks]
    kv_refs = refs[2 + chunks : 2 + chunks + key_chunks]
    o_refs = refs[2 + chunks + key_chunks : 2 + chunks + key_chunks + TP]
    ot_ref, lse_ref, *kept_refs = refs[2 + chunks + key_chunks + TP :]
    qt_out, kv_out, kt_out, qt_ref, kv_ref, kt_ref, vt_ref, o_ref, acc_ref, turn_ref, sems = (
        kept_refs
    )
    copies = [
        pltpu.make_async_copy(source, to, sems.at[i])
        for i, (source, to) in enumerate(((qt_ref, qt_out), (kv_ref, kv_out), (kt_ref, kt_out)))
    ]
    for h in range(HPG):
        vt_ref[h * ROWS + DH : (h + 1) * ROWS, :] = jnp.ones((16, vt_ref.shape[1]), BF16)
    at = 0
    for ref in kv_refs:

        def load(j, c, ref=ref, at=at):
            rows = group_rows(dealt_ref[at + j])
            block = ref[group_rows(j), :]
            kv_ref[rows, :] = block
            turned = block.T
            for h in range(HPG):
                kt_ref[h * DH : (h + 1) * DH, rows] = turned[h * HW : h * HW + DH, :]
                vt_ref[h * ROWS : h * ROWS + DH, rows] = turned[h * HW + DH : (h + 1) * HW, :]
            return c

        count = ref.shape[0] // GROUP
        lax.fori_loop(0, count, load, None)
        at += count
    at = 0
    for ref in q_refs:

        def turn(j, c, ref=ref, at=at):
            qt_ref[:, group_rows(at + j)] = ref[group_rows(j), :].T
            return c

        count = ref.shape[0] // GROUP
        lax.fori_loop(0, count, turn, None)
        at += count

    for copy in copies:
        copy.start()

    def one(i, c):
        group = dealt_ref[i]
        rows = group_rows(i)
        q_places, starts, low, mid = block_bounds(group, bound_ref)
        acc_ref[...] = jnp.zeros_like(acc_ref)

        def visit(top, masked, carry):
            first, cols = pair_rows(top)
            allowed = allowed_pairs(first, top, q_places, starts) if masked else None
            out = []
            for h in range(HPG):
                lanes = slice(h * HW, (h + 1) * HW)
                s = jnp.dot(kv_ref[cols, lanes], qt_ref[lanes, rows], preferred_element_type=F32)
                if masked:
                    s = jnp.where(allowed, s, NEG)
                old = carry[h]
                new = jnp.maximum(old, jnp.max(s, axis=0, keepdims=True))
                p = jnp.exp2(s - new).astype(BF16)
                part = slice(h * ROWS, (h + 1) * ROWS)
                acc_ref[part, :] = acc_ref[part, :] * jnp.exp2(old - new) + jnp.dot(
                    vt_ref[part, cols], p, preferred_element_type=F32
                )
                out.append(new)
            return tuple(out)

        start = tuple(jnp.full((1, GROUP), NEG, F32) for _ in range(HPG))
        highest = sweep(group, low, mid, visit, start)
        for h in range(HPG):
            total = acc_ref[h * ROWS + DH : h * ROWS + DH + 1, :]
            part = slice(h * DH, (h + 1) * DH)
            turn_ref[part, :] = acc_ref[h * ROWS : h * ROWS + DH, :] / total
            lse_ref[h : h + 1, rows] = highest[h] + jnp.log2(total)
        ot_ref[:, rows] = turn_ref[0:HC, :]
        o_ref[rows, :] = turn_ref[...].T.astype(BF16)
        return c

    turn_ref[...] = jnp.zeros_like(turn_ref)
    lax.fori_loop(0, o_ref.shape[0] // GROUP, one, None)
    for m, ref in enumerate(o_refs):
        half = ref.shape[0]
        low = o_ref[2 * m * half : (2 * m + 1) * half, :HC]
        high = o_ref[(2 * m + 1) * half : (2 * m + 2) * half, :HC]
        ref[...] = jnp.concatenate([low, high], axis=1)
    for copy in copies:
        copy.wait()


def attend_forward(dealt, bounds, queries, pairs):
    n = sum(q.shape[0] for q in queries)
    s = sum(p.shape[0] for p in pairs)
    return pl.pallas_call(
        functools.partial(forward_kernel, len(queries), len(pairs)),
        name="attend_forward",
        in_specs=[pl.BlockSpec(memory_space=SMEM)] * 2
        + [pl.BlockSpec(memory_space=VM)] * (len(queries) + len(pairs)),
        out_specs=[pl.BlockSpec(memory_space=VM)] * (TP + 2)
        + [pl.BlockSpec(memory_space=pl.ANY)] * 3,
        out_shape=[jax.ShapeDtypeStruct((n // TP // 2, 2 * HC), BF16)] * TP
        + [
            jax.ShapeDtypeStruct((HC, n), F32),
            jax.ShapeDtypeStruct((8, n), F32),
            jax.ShapeDtypeStruct((WIDE, n), BF16),
            jax.ShapeDtypeStruct((s, WIDE), BF16),
            jax.ShapeDtypeStruct((HC, s), BF16),
        ],
        scratch_shapes=[
            pltpu.VMEM((WIDE, n), BF16),
            pltpu.VMEM((s, WIDE), BF16),
            pltpu.VMEM((HC, s), BF16),
            pltpu.VMEM((HPG * ROWS, s), BF16),
            pltpu.VMEM((n, LANES), BF16),
            pltpu.VMEM((HPG * ROWS, GROUP), F32),
            pltpu.VMEM((LANES, GROUP), F32),
            pltpu.SemaphoreType.DMA((3,)),
        ],
        cost_estimate=cost(30),
    )(dealt, bounds, *queries, *pairs)


def backward_kernel(base, chunks, dealt_ref, bound_ref, qt_ref, kv_ref, kt_ref, ot_ref, lse_ref, *refs):
    q_refs = refs[:chunks]
    do_refs = refs[chunks : chunks + TP]
    dq_ref, own_ref, other_ref, q_ref, do_ref, dot_ref, acc_ref, sum_ref = refs[chunks + TP :]
    h = base + pl.program_id(0)
    n = dq_ref.shape[0]
    sum_ref[...] = jnp.zeros_like(sum_ref)
    at = 0
    for ref in q_refs:
        q_ref[at : at + ref.shape[0], :] = ref[...]
        at += ref.shape[0]
    half = do_refs[0].shape[0]
    none = jnp.zeros((half, DH), BF16)
    for m, ref in enumerate(do_refs):
        for j in range(2):
            block = ref[:, j * DH : (j + 1) * DH]
            part = slice((2 * m + j) * half, (2 * m + j + 1) * half)
            wide = jnp.concatenate([none, block], axis=1)
            do_ref[part, :] = wide
            dot_ref[:, part] = wide.T

    def one(i, c):
        group = dealt_ref[i]
        rows = group_rows(i)
        q_places, starts, low, mid = block_bounds(group, bound_ref)
        delta = jnp.sum(dot_ref[DH:, rows].astype(F32) * ot_ref[:, rows], axis=0, keepdims=True)
        lse = lse_ref[pl.ds(h, 1), rows]
        acc_ref[...] = jnp.zeros_like(acc_ref)

        def visit(top, masked, c):
            first, cols = pair_rows(top)
            kv = kv_ref[cols, :]
            s = jnp.dot(kv, qt_ref[:, rows], preferred_element_type=F32)
            dp = jnp.dot(kv, dot_ref[:, rows], preferred_element_type=F32)
            if masked:
                s = jnp.where(allowed_pairs(first, top, q_places, starts), s, NEG)
            p = jnp.exp2(s - lse)
            d = (p * (dp - delta)).astype(BF16)
            acc_ref[...] += jnp.dot(kt_ref[:, cols], d, preferred_element_type=F32)
            sum_ref[cols, :] += jnp.dot(
                d, q_ref[rows, :], preferred_element_type=F32
            ) + jnp.dot(p.astype(BF16), do_ref[rows, :], preferred_element_type=F32)
            return c

        sweep(group, low, mid, visit, jnp.int32(0))
        dq_ref[rows, :] = (acc_ref[...] * DH**-0.5).T.astype(BF16)
        return c

    lax.fori_loop(0, n // GROUP, one, None)
    lane = lax.broadcasted_iota(jnp.int32, (1, HW), 1)
    scale = jnp.where(lane < DH, DH**-0.5 / SCALE2, 1.0)

    def store(b, c):
        own_ref[group_rows(b), :] = sum_ref[group_rows(dealt_ref[b]), :] * scale
        return c

    lax.fori_loop(0, n // GROUP, store, None)

    def other(b, c):
        source = group_rows(dealt_ref[n // GROUP + b])
        other_ref[group_rows(b), :] = (sum_ref[source, :] * scale).astype(BF16)
        return c

    lax.fori_loop(0, other_ref.shape[0] // GROUP, other, None)


def attend_backward(base, count, dealt, bounds, queries, qt, kv, kt, ot, lse, grads):
    n = ot.shape[1]
    s = kv.shape[0]
    full = pl.BlockSpec(memory_space=VM)
    return pl.pallas_call(
        functools.partial(backward_kernel, base, len(queries)),
        name="attend_backward",
        grid=(count,),
        in_specs=[pl.BlockSpec(memory_space=SMEM)] * 2
        + [
            pl.BlockSpec((HW, n), lambda i: (base + i, 0)),
            pl.BlockSpec((s, HW), lambda i: (0, base + i)),
            pl.BlockSpec((DH, s), lambda i: (base + i, 0)),
            pl.BlockSpec((DH, n), lambda i: (base + i, 0)),
            full,
        ]
        + [pl.BlockSpec((q.shape[0], HW), lambda i: (0, base + i)) for q in queries]
        + [pl.BlockSpec((g.shape[0], HW), lambda i: (0, base + i)) for g in grads],
        out_specs=[
            pl.BlockSpec((None, n, DH), lambda i: (i, 0, 0)),
            pl.BlockSpec((None, n, HW), lambda i: (i, 0, 0)),
            pl.BlockSpec((None, s - n, HW), lambda i: (i, 0, 0)),
        ],
        out_shape=[
            jax.ShapeDtypeStruct((count, n, DH), BF16),
            jax.ShapeDtypeStruct((count, n, HW), F32),
            jax.ShapeDtypeStruct((count, s - n, HW), BF16),
        ],
        scratch_shapes=[
            pltpu.VMEM((n, HW), BF16),
            pltpu.VMEM((n, HW), BF16),
            pltpu.VMEM((HW, n), BF16),
            pltpu.VMEM((DH, GROUP), F32),
            pltpu.VMEM((s, HW), F32),
        ],
        cost_estimate=cost(16 * count),
    )(dealt, bounds, qt, kv, kt, ot, lse, *queries, *grads)


def finish_kernel(shifts, *refs):
    sets = 2 + shifts

    def heads(k):
        first, rest = refs[2 * k : 2 * k + 2]
        return [first.at[0]] + [rest.at[h] for h in range(HPG - 1)]

    dq_refs = heads(0)
    own_refs = heads(1)
    came_refs = [ref for s in range(shifts) for ref in heads(2 + s)]
    w_ref = refs[2 * sets]
    outs = refs[2 * sets + 1 :]
    sums_ref, first_send, first_keep, second_send, second_keep = outs[TP:]
    sums_ref[...] = jnp.zeros_like(sums_ref)
    size = outs[0].shape[0]
    half = size // 2
    for m in range(TP):

        def part(i, c, m=m):
            to = pl.ds(pl.multiple_of(i * 128, 128), 128)
            rows = pl.ds(pl.multiple_of(m * size + i * 128, 128), 128)
            pieces = []
            for h in range(HPG):
                value = own_refs[h][rows, :]
                for s in range(shifts):
                    value = value + came_refs[s * HPG + h][rows, :].astype(F32)
                pieces.append(value.astype(BF16))
            for h in range(HPG):
                pieces.append(dq_refs[h][rows, :])
            whole = jnp.concatenate(pieces, axis=1)
            outs[m][to, :] = whole
            sums_ref[0:1, :] += jnp.sum(whole.astype(F32), axis=0, keepdims=True)
            return c

        lax.fori_loop(0, size // 128, part, None)
        for j in range(2):
            value = lax.dot_general(
                outs[m][j * half : (j + 1) * half, :],
                w_ref[...],
                NT,
                preferred_element_type=F32,
            ).astype(BF16)
            if j == 0:
                (first_send if m % 2 else first_keep)[m // 2] = value
            else:
                (second_send if m // 2 else second_keep)[m % 2] = value


def finish(dqs, owns, cames, weight):
    n = dqs[0].shape[1]
    full = pl.BlockSpec(memory_space=VM)
    shifts = len(cames) // 2
    shape = jax.ShapeDtypeStruct
    return pl.pallas_call(
        functools.partial(finish_kernel, shifts),
        name="finish",
        in_specs=[full] * ((2 + shifts) * 2 + 1),
        out_specs=[full] * (TP + 5),
        out_shape=[shape((n // TP, 3 * HC), BF16)] * TP
        + [shape((8, 3 * HC), F32)]
        + [shape((2, n // TP // 2, D), BF16)] * 4,
        cost_estimate=cost(10),
    )(*dqs, *owns, *cames, weight)


TN = (((0,), (0,)), ((), ()))


def columns_kernel(chunks, place_ref, *refs):
    def heads(k):
        first, rest = refs[2 * k : 2 * k + 2]
        return [first.at[0]] + [rest.at[h] for h in range(HPG - 1)]

    dq_refs, own_refs, came_refs = heads(0), heads(1), heads(2)
    w_ref, norm_ref, narrow_ref, broad_ref = refs[6:10]
    a_hbm = refs[10 : 10 + chunks]
    keep_ref, send_ref, *part_hbm = refs[10 + chunks : 16 + chunks]
    out_ref, turn_ref, a_ref, g_ref, part_ref, sums_ref, sems = refs[16 + chunks :]
    loads = []
    at = 0
    for i, ref in enumerate(a_hbm):
        to = a_ref.at[pl.ds(at, ref.shape[0])]
        loads.append(pltpu.make_async_copy(ref, to, sems.at[i]))
        at += ref.shape[0]
    for load in loads:
        load.start()
    width = 3 * HC
    size = g_ref.shape[0] // TP
    half = size // 2
    sums_ref[...] = jnp.zeros_like(sums_ref)

    def part(i, c):
        rows = group_rows(i)
        pieces = []
        for h in range(HPG):
            value = own_refs[h][rows, :] + came_refs[h][rows, :].astype(F32)
            pieces.append(value.astype(BF16))
        for h in range(HPG):
            pieces.append(dq_refs[h][rows, :])
        whole = jnp.concatenate(pieces, axis=1)
        g_ref[rows, :] = whole
        sums_ref[0:1, :] += jnp.sum(whole.astype(F32), axis=0, keepdims=True)
        return c

    lax.fori_loop(0, g_ref.shape[0] // GROUP, part, None)
    stores = [
        pltpu.make_async_copy(part_ref.at[i], part_hbm[i], sems.at[chunks + i]) for i in range(4)
    ]
    def split(m, c):
        rows = pl.ds(pl.multiple_of(m * size, size), size)
        value = lax.dot_general(
            g_ref[rows, :], w_ref[...], NT, preferred_element_type=F32
        ).astype(BF16)
        part_ref[1 - m % 2, m // 2] = value[:half]
        part_ref[3 - m // 2, m % 2] = value[half:]
        return c

    lax.fori_loop(0, TP, split, None)
    for store in stores:
        store.start()
    for load in loads:
        load.wait()
    for j in range(D // GROUP):
        lanes = slice(j * GROUP, (j + 1) * GROUP)
        out_ref[lanes, :width] = lax.dot_general(
            a_ref[:, lanes], g_ref[...], TN, preferred_element_type=F32
        )
    sums = sums_ref[0:1, :]
    weight = w_ref[...].astype(F32)
    turned = sums_ref[...].T
    query = turned[WIDE:, 0:1]
    value = jnp.concatenate(
        [turned[h * HW + DH : (h + 1) * HW, 0:1] for h in range(HPG)], axis=0
    )
    lane = lax.broadcasted_iota(jnp.int32, (1, 8), 1)
    norms = norm_ref[...].T
    direct = jnp.sum(out_ref[:, :width] * weight, axis=1, keepdims=True)
    shift = jnp.sum(weight * sums, axis=1, keepdims=True)
    gain = (direct - norms[:, 1:2] * shift) / norms[:, 0:1]
    narrow = narrow_ref[...].T
    out_ref[:, width:] = jnp.zeros((D, 64), F32)
    out_ref[:, width : width + 8] = jnp.where(lane >= 2, narrow, 0.0)
    for m in range(TP):
        at = pl.ds(pl.multiple_of((place_ref[0] ^ m) * HC, HC), HC)
        piece = narrow[m * HC : (m + 1) * HC, :]
        out_ref[at, width : width + 8] += jnp.where(lane < 2, piece, 0.0)
    out_ref[:, width + 8 : width + 16] = jnp.where(lane == 0, gain, 0.0) + jnp.where(
        lane == 1, shift, 0.0
    )
    own = pl.ds(pl.multiple_of(place_ref[0] * HC, HC), HC)
    out_ref[own, width + 8 : width + 16] += jnp.where(lane == 2, query, 0.0) + jnp.where(
        lane == 3, value, 0.0
    )
    turn_ref[...] = broad_ref[...].T

    def spread(b, c):
        for q in range(4):
            source = pl.ds(pl.multiple_of(b * 96 + q * 24, 8), 24)
            at = width + 16 + 8 * q
            out_ref[pl.ds(pl.multiple_of(b * 24, 8), 24), at : at + 8] = turn_ref[source, :]
        return c

    lax.fori_loop(0, FF // 96, spread, None)
    half = HC // 2
    for g in range(TP):
        mine = pl.multiple_of(g * HC + place_ref[1] * half, half)
        other = pl.multiple_of(g * HC + (1 - place_ref[1]) * half, half)
        keep_ref[g] = out_ref[pl.ds(mine, half), :]
        send_ref[g] = out_ref[pl.ds(other, half), :]
    for store in stores:
        store.wait()


def columns(place, dqs, owns, cames, weight, norms, narrow, broad, normed):
    n = dqs[0].shape[1]
    full = pl.BlockSpec(memory_space=VM)
    away = pl.BlockSpec(memory_space=pl.ANY)
    shape = jax.ShapeDtypeStruct
    out = shape((TP, HC // 2, 3 * HC + 64), F32)
    part = (2, n // TP // 2, D)
    return pl.pallas_call(
        functools.partial(columns_kernel, len(normed)),
        name="columns",
        in_specs=[pl.BlockSpec(memory_space=SMEM)] + [full] * 10 + [away] * len(normed),
        out_specs=[full] * 2 + [away] * 4,
        out_shape=[out, out] + [shape(part, BF16)] * 4,
        scratch_shapes=[
            pltpu.VMEM((D, 3 * HC + 64), F32),
            pltpu.VMEM((FF, 8), F32),
            pltpu.VMEM((n, D), BF16),
            pltpu.VMEM((n, 3 * HC), BF16),
            pltpu.VMEM((4,) + part, BF16),
            pltpu.VMEM((8, 3 * HC), F32),
            pltpu.SemaphoreType.DMA((4 + len(normed),)),
        ],
        cost_estimate=cost(14),
    )(place, *dqs, *owns, *cames, weight, norms, narrow, broad, *normed)


def weight_grads_kernel(
    place_ref,
    u_ref,
    datt_ref,
    a2_ref,
    df_ref,
    u2_ref,
    dz_ref,
    keep_ref,
    send_ref,
    back_ref,
    in_ref,
    out_ref,
    sems,
):
    hg = place_ref[0]
    qs = place_ref[1]

    def each(source, k, rows, sem, act):
        block = (k // 2) ^ hg
        part = 0 if rows < 432 else 1
        slot = (block % 2) * 2 + block // 2 if part == 0 else block
        to = pl.ds(rows % 432, source.shape[0])
        kept = k % 2 == qs
        pl.when(kept)(
            lambda: act(pltpu.make_async_copy(source, keep_ref.at[part, slot, to], sem))
        )
        pl.when(jnp.logical_not(kept))(
            lambda: act(pltpu.make_async_copy(source, send_ref.at[part, slot, to], sem))
        )

    def start(source, k, rows, sem):
        each(source, k, rows, sem, lambda copy: copy.start())

    def wait(source, k, rows, sem):
        each(source, k, rows, sem, lambda copy: copy.wait())

    def back_block(k):
        return back_ref.at[pl.ds(pl.multiple_of(k * 384, 384), 384)]

    def in_pieces(k):
        cut = [
            (in_ref.at[0, pl.ds(pl.multiple_of(k * 96, 48), 48)], 384),
            (in_ref.at[0, pl.ds(pl.multiple_of(k * 96 + 48, 48), 48)], 432),
        ]
        whole = pl.ds(pl.multiple_of(k * 96, 96), 96)
        return cut + [(in_ref.at[j, whole], 384 + 96 * j) for j in range(1, 4)]

    def out_block(k):
        at = ((k // 2) ^ hg) * 192 + (k % 2) * 96
        return out_ref.at[pl.ds(pl.multiple_of(at, 96), 96)]

    def back(k, c):
        lanes = pl.ds(pl.multiple_of(k * D, D), D)
        back_ref[pl.ds(pl.multiple_of(k * D, D), D), :] = lax.dot_general(
            u2_ref[:, lanes], dz_ref[...], TN, preferred_element_type=F32
        ).astype(BF16)
        for j in range(2):
            block = 2 * k + j
            start(back_block(block), block, 0, sems.at[0, block])
        return c

    lax.fori_loop(0, 4, back, None)

    def inner(j, c):
        lanes = pl.ds(pl.multiple_of(j * D, D), D)
        in_ref[j] = lax.dot_general(
            a2_ref[...], df_ref[:, lanes], TN, preferred_element_type=F32
        ).astype(BF16)
        return c

    lax.fori_loop(0, 4, inner, None)

    def send_inner(k, c):
        for j, (source, first) in enumerate(in_pieces(k)):
            start(source, k, first, sems.at[1 + j, k])
        return c

    lax.fori_loop(0, 8, send_inner, None)
    out_ref[...] = lax.dot_general(
        u_ref[...], datt_ref[...], TN, preferred_element_type=F32
    ).astype(BF16)

    def finish_all(k, c):
        start(out_block(k), k, 768, sems.at[6, k])
        wait(back_block(k), k, 0, sems.at[0, k])
        for j, (source, first) in enumerate(in_pieces(k)):
            wait(source, k, first, sems.at[1 + j, k])
        return c

    lax.fori_loop(0, 8, finish_all, None)

    def finish_out(k, c):
        wait(out_block(k), k, 768, sems.at[6, k])
        return c

    lax.fori_loop(0, 8, finish_out, None)


def weight_grads(place, u, datt, a2, df, u2, dz):
    full = pl.BlockSpec(memory_space=VM)
    out = jax.ShapeDtypeStruct((2, TP, 432, D), BF16)
    return pl.pallas_call(
        weight_grads_kernel,
        name="weight_grads",
        in_specs=[pl.BlockSpec(memory_space=SMEM)] + [full] * 6,
        out_specs=[pl.BlockSpec(memory_space=pl.ANY)] * 2,
        out_shape=[out, out],
        scratch_shapes=[
            pltpu.VMEM((FF, D), BF16),
            pltpu.VMEM((4, D, D), BF16),
            pltpu.VMEM((D, D), BF16),
            pltpu.SemaphoreType.DMA((7, 8)),
        ],
        cost_estimate=cost(14),
    )(place, u, datt, a2, df, u2, dz)


def settle_kernel(place_ref, total_ref, *refs):
    came_refs = refs[:3]
    out_ref, gains_ref, shifts_ref, wide_ref, wide_shifts_ref, mine_ref = refs[3:]
    hg = place_ref[0]
    mine_ref[0] = total_ref[hg]
    for m, ref in enumerate(came_refs):
        mine_ref[m + 1] = ref[...]
    blocks = [mine_ref[hg ^ g] for g in range(TP)]
    pieces = [block[:, WIDE : 3 * HC] for block in blocks]
    for part in range(2):
        for block in blocks:
            for h in range(HPG):
                at = h * HW + part * DH
                pieces.append(block[:, at : at + DH])
    out_ref[...] = jnp.concatenate(pieces, axis=1)
    tail = mine_ref[0] + mine_ref[1] + mine_ref[2] + mine_ref[3]
    turned = tail[:, 512:].T[64:, :]

    def rows(*which):
        return jnp.concatenate([turned[i : i + 1] for i in which], axis=0)

    gains_ref[...] = rows(8, 0, 2)
    shifts_ref[...] = rows(9, 10, 11, 1, 4, 3, 5)

    def wide(v):
        return jnp.concatenate([turned[16 + 8 * q + v : 17 + 8 * q + v] for q in range(4)], axis=1)

    wide_ref[...] = wide(0)
    wide_shifts_ref[...] = jnp.concatenate([wide(1), wide(2)], axis=0)


def settle(place, total, came):
    full = pl.BlockSpec(memory_space=VM)
    rows = came[0].shape[0]
    shape = jax.ShapeDtypeStruct
    return pl.pallas_call(
        settle_kernel,
        name="settle",
        in_specs=[pl.BlockSpec(memory_space=SMEM)] + [full] * 4,
        out_specs=[full] * 5,
        out_shape=[
            shape((rows, 3 * D), F32),
            shape((3, rows), F32),
            shape((7, rows), F32),
            shape((1, 4 * rows), F32),
            shape((2, 4 * rows), F32),
        ],
        scratch_shapes=[pltpu.VMEM((TP,) + came[0].shape, F32)],
        cost_estimate=cost(0.02),
    )(place, total, *came)


def outward_kernel(x_ref, norm_ref, dx_ref, *refs):
    out_ref = refs[6]
    half = x_ref.shape[0] // 2
    for i in range(2):
        keep, came, last = refs[3 * i : 3 * i + 3]
        rows = slice(i * half, (i + 1) * half)
        grad = keep[0].astype(F32) + came[0].astype(F32) + last[...].astype(F32)
        unit, scale = norm_parts(x_ref[rows, :].astype(F32))
        out_ref[rows, :] = dx_ref[rows, :] + norm_back(grad * norm_ref[0:1, :], unit, scale)


def outward(x, norms, dx, parts):
    full = pl.BlockSpec(memory_space=VM)
    return pl.pallas_call(
        outward_kernel,
        name="outward",
        in_specs=[full] * 9,
        out_specs=full,
        out_shape=jax.ShapeDtypeStruct(dx.shape, F32),
        cost_estimate=cost(0.02),
    )(x, norms, dx, *parts)


def norm_parts(value):
    centred = value - jnp.mean(value, axis=1, keepdims=True)
    scale = lax.rsqrt(jnp.mean(centred * centred, axis=1, keepdims=True) + 1e-05)
    return centred * scale, scale


def norm_back(grad, unit, scale):
    first = jnp.mean(grad, axis=1, keepdims=True)
    second = jnp.mean(grad * unit, axis=1, keepdims=True)
    return scale * (grad - first - unit * second)


def column_sum(value):
    return jnp.sum(value, axis=0, keepdims=True)


CHUNK = 3072
TILE = 256


def place_weights(place_ref, own_refs, gathered, in_ref, out_ref, back_ref):
    near, axis, axis_far, corner, corner_far = gathered
    in_ref[pl.ds(pl.multiple_of(place_ref[0] * 192, 192), 192), :] = own_refs[0][...]
    out_ref[pl.ds(pl.multiple_of(place_ref[4] * 192, 192), 192), :] = own_refs[1][...]
    back_ref[pl.ds(pl.multiple_of(place_ref[0] * D, D), D), :] = own_refs[2][...]
    sources = [
        (near, 0),
        (near, 1),
        (axis, 0),
        (axis, 1),
        (axis_far, 0),
        (axis_far, 1),
        (corner, None),
        (corner_far, None),
    ]
    for k, (ref, t) in enumerate(sources):
        c = place_ref[8 + k]
        for m in range(1, 4):
            value = ref[m - 1] if t is None else ref[t, m - 1]
            z = place_ref[m]
            cols = pl.ds(pl.multiple_of(c * 384, 384), 384)
            in_ref[pl.ds(pl.multiple_of(z * 192, 96), 96), cols] = value[0:96, 0:384]
            in_ref[pl.ds(pl.multiple_of(z * 192 + 96, 96), 96), cols] = value[0:96, 384:768]
            back_ref[pl.ds(pl.multiple_of(z * D + c * 96, 96), 96), :] = value[96:192, :]
            block = jnp.concatenate([value[192:216, 0:384], value[192:216, 384:768]], axis=0)
            at = pl.ds(pl.multiple_of(place_ref[4 + m] * 192 + (c // 2) * 48, 48), 48)
            out_ref[at, pl.ds(pl.multiple_of((c % 2) * 384, 384), 384)] = block


def middle_kernel(scattered, *refs):
    piece_refs = refs[:TP]
    x_ref, cot_ref, row_ref, wide_ref = refs[TP : TP + 4]
    refs = refs[TP + 4 :]
    if scattered:
        place_ref = refs[0]
        own_refs, gathered, refs = refs[1:4], refs[4:9], refs[9:]
        out_w_ref, in_w_ref, back_w_ref = refs[-3:]
        place_weights(place_ref, own_refs, gathered, in_w_ref, out_w_ref, back_w_ref)
        refs = refs[:-3]
    else:
        in_w_ref, out_w_ref, back_w_ref = refs[:3]
        refs = refs[3:]
    do_refs = refs[:TP]
    (
        mixed_ref,
        u_ref,
        a2_ref,
        u2_ref,
        df_ref,
        datt_ref,
        dx_ref,
        narrow_ref,
        broad_ref,
        ctx_ref,
        do_ref,
        g_ref,
        slope_ref,
        d_ref,
        da_ref,
        x1_ref,
    ) = refs[TP:]
    half = piece_refs[0].shape[0]
    for m, ref in enumerate(piece_refs):
        for j in range(2):
            ctx_ref[j * half : (j + 1) * half, m * HC : (m + 1) * HC] = ref[
                :, j * HC : (j + 1) * HC
            ]
    narrow_ref[...] = jnp.zeros_like(narrow_ref)
    broad_ref[...] = jnp.zeros_like(broad_ref)

    def tile(i, c):
        rows = pl.ds(pl.multiple_of(i * TILE, TILE), TILE)
        unit_one, scale_one = norm_parts(ctx_ref[rows, :].astype(F32))
        u = (unit_one * row_ref[0:1, :] + row_ref[1:2, :]).astype(BF16)
        u_ref[rows, :] = u
        x1 = (
            x_ref[rows, :].astype(F32)
            + jnp.dot(u, out_w_ref[...], preferred_element_type=F32)
            + row_ref[2:3, :]
        )
        x1_ref[...] = x1
        unit_two, scale_two = norm_parts(x1)
        a2 = (unit_two * row_ref[3:4, :] + row_ref[4:5, :]).astype(BF16)
        a2_ref[rows, :] = a2

        def lanes_of(j):
            return pl.ds(pl.multiple_of(j * CHUNK, CHUNK), CHUNK)

        def up(j, total):
            lanes = lanes_of(j)
            f = (
                jnp.dot(a2_ref[rows, :], in_w_ref[:, lanes], preferred_element_type=F32)
                + wide_ref[0:1, lanes]
            )
            cdf = 0.5 * (1.0 + lax.erf(f * 0.7071067811865476))
            pdf = jnp.exp(-0.5 * f * f) * 0.3989422804014327
            slope_ref[:, lanes] = cdf + f * pdf
            g = f * cdf
            g_ref[:, lanes] = g
            return total + jnp.sum(g, axis=1, keepdims=True)

        average = lax.fori_loop(0, FF // CHUNK, up, jnp.zeros((TILE, 1), F32)) / FF

        def spread(j, total):
            lanes = lanes_of(j)
            centred = g_ref[:, lanes] - average
            return total + jnp.sum(centred * centred, axis=1, keepdims=True)

        variance = lax.fori_loop(0, FF // CHUNK, spread, jnp.zeros((TILE, 1), F32)) / FF
        scale = lax.rsqrt(variance + 1e-05)

        def turn(j, carry):
            first, second = carry
            lanes = lanes_of(j)
            unit = (g_ref[:, lanes] - average) * scale
            g_ref[:, lanes] = unit
            gain = wide_ref[1:2, lanes]
            u2_ref[rows, lanes] = (unit * gain + wide_ref[2:3, lanes]).astype(BF16)
            du2 = lax.dot_general(
                cot_ref[rows, :], back_w_ref[lanes, :], NT, preferred_element_type=F32
            )
            broad_ref[0:1, lanes] += column_sum(du2 * unit)
            broad_ref[2:3, lanes] += column_sum(du2)
            grad = du2 * gain
            d_ref[:, lanes] = grad
            return (
                first + jnp.sum(grad, axis=1, keepdims=True),
                second + jnp.sum(grad * unit, axis=1, keepdims=True),
            )

        none = jnp.zeros((TILE, 1), F32)
        first, second = lax.fori_loop(0, FF // CHUNK, turn, (none, none))
        first = first / FF
        second = second / FF
        da_ref[...] = jnp.zeros_like(da_ref)

        def down(j, c):
            lanes = lanes_of(j)
            grad = scale * (d_ref[:, lanes] - first - g_ref[:, lanes] * second)
            df = (grad * slope_ref[:, lanes]).astype(BF16)
            df_ref[rows, lanes] = df
            broad_ref[1:2, lanes] += column_sum(df.astype(F32))
            da_ref[...] += lax.dot_general(
                df, in_w_ref[:, lanes], NT, preferred_element_type=F32
            )
            return c

        lax.fori_loop(0, FF // CHUNK, down, None)
        da2 = da_ref[...]
        unit_two, scale_two = norm_parts(x1_ref[...])
        narrow_ref[2:3, :] += column_sum(da2 * unit_two)
        narrow_ref[3:4, :] += column_sum(da2)
        cot = cot_ref[rows, :].astype(F32)
        dx = cot + norm_back(da2 * row_ref[3:4, :], unit_two, scale_two)
        dx_ref[rows, :] = dx
        datt = dx.astype(BF16)
        datt_ref[rows, :] = datt
        narrow_ref[4:5, :] += column_sum(datt.astype(F32))
        narrow_ref[5:6, :] += column_sum(cot)
        du = lax.dot_general(datt, out_w_ref[...], NT, preferred_element_type=F32)
        unit_one, scale_one = norm_parts(ctx_ref[rows, :].astype(F32))
        narrow_ref[0:1, :] += column_sum(du * unit_one)
        narrow_ref[1:2, :] += column_sum(du)
        do_ref[rows, :] = norm_back(du * row_ref[0:1, :], unit_one, scale_one).astype(BF16)
        mixed_ref[rows, :] = (
            jnp.dot(u2_ref[rows, :], back_w_ref[...], preferred_element_type=F32)
            + row_ref[5:6, :]
            + x1_ref[...]
        ).astype(BF16)
        return c

    lax.fori_loop(0, ctx_ref.shape[0] // TILE, tile, None)
    for m, ref in enumerate(do_refs):
        pieces = []
        for h in range(HPG):
            lanes = slice(m * HC + h * DH, m * HC + (h + 1) * DH)
            pieces += [do_ref[:half, lanes], do_ref[half:, lanes]]
        ref[...] = jnp.concatenate(pieces, axis=1)


def middle(pieces, x, cot, narrow, wide, weights):
    n = x.shape[0]
    full = pl.BlockSpec(memory_space=VM)
    shape = jax.ShapeDtypeStruct
    scattered = len(weights) > 3
    weight_specs = [full] * len(weights)
    if scattered:
        weight_specs[0] = pl.BlockSpec(memory_space=SMEM)
    return pl.pallas_call(
        functools.partial(middle_kernel, scattered),
        name="middle",
        in_specs=[full] * (TP + 4) + weight_specs,
        out_specs=[full] * (TP + 9),
        out_shape=[shape(p.shape, BF16) for p in pieces]
        + [
            shape((n, D), BF16),
            shape((n, D), BF16),
            shape((n, D), BF16),
            shape((n, FF), BF16),
            shape((n, FF), BF16),
            shape((n, D), BF16),
            shape((n, D), F32),
            shape((8, D), F32),
            shape((8, FF), F32),
        ],
        scratch_shapes=[
            pltpu.VMEM((n, D), BF16),
            pltpu.VMEM((n, D), BF16),
            pltpu.VMEM((TILE, FF), F32),
            pltpu.VMEM((TILE, FF), F32),
            pltpu.VMEM((TILE, FF), F32),
            pltpu.VMEM((TILE, D), F32),
            pltpu.VMEM((TILE, D), F32),
        ]
        + ([pltpu.VMEM(s, BF16) for s in ((D, D), (D, FF), (FF, D))] if scattered else []),
        cost_estimate=cost(36),
    )(*pieces, x, cot, narrow, wide, *weights)


def layer_norm(values, gain, shift):
    average = jnp.mean(values, axis=-1, keepdims=True)
    centred = values - average
    variance = jnp.mean(centred * centred, axis=-1, keepdims=True)
    return centred * lax.rsqrt(variance + 1e-05) * gain + shift


def outer_sum(left, right):
    return lax.dot_general(left, right, (((0,), (0,)), ((), ())), preferred_element_type=F32)


def times_transposed(left, matrix):
    return lax.dot_general(left, matrix, (((1,), (1,)), ((), ())), preferred_element_type=F32)


def tie(value, *before):
    return lax.optimization_barrier((value, before))[0]


def pick(array, index, axis=0):
    return lax.dynamic_index_in_dim(array, index, axis, keepdims=False)


def make_local(ctx_size, fsdp_size):
    nq = ctx_size // TP
    fast = ctx_size == 8 and fsdp_size == 4

    def over_heads(value, mask):
        return lax.ppermute(
            value, "ctx", [(i, ((i // nq) ^ mask) * nq + i % nq) for i in range(ctx_size)]
        )

    def over_rows(value, shift):
        return lax.ppermute(
            value,
            "ctx",
            [(i, (i // nq) * nq + (i % nq - shift) % nq) for i in range(ctx_size)],
        )

    def over_fsdp(value, mask):
        return lax.ppermute(value, "fsdp", [(i, i ^ mask) for i in range(fsdp_size)])

    def over_split(value, masks):
        return lax.ppermute(
            value,
            "ctx",
            [(i, ((i // nq) ^ masks[i % nq]) * nq + i % nq) for i in range(ctx_size)],
        )

    moves = (over_heads, over_rows, over_fsdp, over_split)

    def exchange_heads(own, halves):
        one = over_heads(own, 1)
        two = over_heads(own, 2)
        first, second = halves
        low = over_heads(first(one), 2)
        high = over_heads(second(two), 1)
        return one, two, low, high

    def local(
        tokens,
        cotangent,
        lengths,
        dealing,
        qkv_weight,
        out_weight,
        in_weight,
        back_weight,
        norm_gains,
        shifts,
        ffn_gain,
        ffn_shifts,
    ):
        ctx = lax.axis_index("ctx")
        fs = lax.axis_index("fsdp")
        hg = ctx // nq
        qs = ctx % nq
        rows = tokens.shape[1]
        shard = qkv_weight.shape[0]
        deal_row = dealing[0]
        group_count = deal_row.shape[0]
        per = rows // GROUP
        bounds = jnp.cumsum(lengths[0])
        members = [
            [((hg ^ m) * nq + (qs + s) % nq) * per + j for m in range(TP) for j in range(per)]
            for s in range(nq)
        ]
        stored = jnp.stack([g for part in members for g in part]).astype(jnp.int32)
        onehot = (stored[:, None] == jnp.arange(group_count, dtype=jnp.int32)[None, :]).astype(
            jnp.int32
        )
        dealt = jnp.sum(onehot * deal_row[None, :], axis=1)
        mine = tokens[0]
        half = rows // 2
        one, two, low, high = exchange_heads(mine, (lambda a: a[:half], lambda a: a[half:]))
        chunks = (mine, one, two, low, high)

        def own_columns(weight):
            def take(at, size):
                value = weight[:, at : at + size]
                for g in range(1, TP):
                    other = weight[:, at + g * HC : at + g * HC + size]
                    value = jnp.where(hg == g, other, value)
                return value

            out = []
            for h in range(HPG):
                out += [take(D + h * DH, DH), take(2 * D + h * DH, DH)]
            return jnp.concatenate(out + [take(0, HC)], axis=1)

        feature = norm_gains.shape[1]
        narrow_rows = jnp.concatenate([norm_gains, shifts], axis=0)
        broad_rows = jnp.concatenate([ffn_gain[None], ffn_shifts], axis=0).reshape(12, feature)
        small = jnp.concatenate(
            [
                jnp.pad(narrow_rows, ((0, 6), (0, HC - feature))),
                jnp.pad(broad_rows, ((0, 4), (0, 2 * HC - feature))),
            ],
            axis=1,
        )
        span = shard // nq
        tail = small.shape[0] // nq
        columns_half = pick(own_columns(qkv_weight).reshape(nq, span, 3 * HC), qs)
        piece = jnp.concatenate([columns_half, pick(small.reshape(nq, tail, -1), qs)], axis=0)
        if fast:
            shards = (in_weight, back_weight, out_weight)
            own_piece = weight_piece(*shards, hg * 2 + qs)
            far_piece = weight_piece(*shards, (hg ^ 3) * 2 + qs)
            piece = tie(piece, own_piece, far_piece)
        came = [over_fsdp(piece, m) for m in range(1, fsdp_size)]
        parts = jnp.stack([piece] + came)
        if fast:
            foreign = gather_pieces(own_piece, came, moves)
            corner = gather_pieces(far_piece, foreign, moves)
            shared = [over_rows(tie(parts, one, two), 1)]
        else:
            shared = [over_rows(parts, s) for s in range(1, nq)]
        parts = jnp.stack([parts] + shared)
        if not fast:
            w_own = jnp.concatenate(
                [
                    pick(pick(parts, (h - qs) % nq), f ^ fs)[:span]
                    for f in range(fsdp_size)
                    for h in range(nq)
                ],
                axis=0,
            )
        tails = [
            jnp.concatenate(
                [pick(pick(parts, (h - qs) % nq), f ^ fs)[span:] for h in range(nq)], axis=0
            )
            for f in range(fsdp_size)
        ]
        narrow_all = jnp.concatenate([p[:10, :feature] for p in tails], axis=1).astype(F32)
        broad_all = jnp.concatenate(
            [p[:12, HC : HC + feature].reshape(3, -1) for p in tails], axis=1
        ).astype(F32)
        gains = narrow_all[:3]
        shift_rows = narrow_all[3:]
        ffn_scale = broad_all[0]
        ffn_shift_rows = broad_all[1:]

        if not fast:
            in_w = lax.all_gather(in_weight, "fsdp", axis=0, tiled=True)
            back_w = lax.all_gather(back_weight, "fsdp", axis=0, tiled=True)
            out_w = lax.all_gather(out_weight, "fsdp", axis=0, tiled=True)
            out_blocks = out_w.reshape(TP, HC, D)
            out_rel = jnp.concatenate([pick(out_blocks, hg ^ m) for m in range(TP)], axis=0)

        def own_heads(row):
            return pick(row.reshape(TP, HC), hg)

        value_bias = own_heads(shift_rows[2]).reshape(HPG, DH)
        bias = jnp.concatenate(
            [
                jnp.stack([jnp.zeros((HPG, DH), F32), value_bias], axis=1).reshape(-1),
                own_heads(shift_rows[1]),
            ]
        )[None]
        norm_rows = jnp.stack([gains[0], shift_rows[0]])
        norm_rows = jnp.pad(norm_rows, ((0, 6), (0, 0)))
        if fast:
            table = jnp.stack(
                [(f ^ fs) * nq + (qs + s) % nq for s in range(nq) for f in range(fsdp_size)]
            )
            *first, w_own = project(
                (mine, one, two), (table.astype(jnp.int32), parts[0], parts[1]), norm_rows, bias
            )
        else:
            first = project((mine, one, two), (w_own,), norm_rows, bias)
        if fast:
            gathered = gather_axis(tie(foreign, first[1]), (low, high), moves)
        projected = [first, project((low, high), (w_own,), norm_rows, bias)]
        normed = [p[0] for p in projected]
        queries = [p[1] for p in projected]
        pairs = [p[2] for p in projected]
        for s in range(1, nq):
            pairs = pairs + [over_rows(p[2], s) for p in projected]
        if fast:
            dealt = tie(dealt, gathered[0])

        *context_parts, context_t, log_total, q_turned, kv_rows, k_turned = attend_forward(
            dealt, bounds, queries, pairs
        )
        got = [context_parts[0]] + [over_heads(context_parts[m], m) for m in range(1, TP)]

        if fast:
            gathered = gather_rest(*gathered, corner, log_total, got, moves)

        def relative(row):
            blocks = row.reshape(TP, HC)
            return jnp.concatenate([pick(blocks, hg ^ m) for m in range(TP)])

        narrow = jnp.stack(
            [relative(gains[1]), relative(shift_rows[3]), shift_rows[4], gains[2], shift_rows[5]]
            + [shift_rows[6]] * 3
        )
        wide = jnp.pad(
            jnp.stack([ffn_shift_rows[0], ffn_scale, ffn_shift_rows[1]]), ((0, 5), (0, 0))
        )
        cot = cotangent[0]
        if fast:
            weights = (weight_places(hg, qs, fs), in_weight, out_weight, back_weight, *gathered)
        else:
            weights = (in_w, out_rel, back_w)
        (
            *sent,
            mixed_out,
            inner_low,
            normed_two_low,
            inner_two_low,
            hidden_low,
            branch_low,
            grad_middle,
            narrow_sums,
            broad_sums,
        ) = middle(got, mine, cot, narrow, wide, weights)
        grad_gain_one, grad_shift_three, grad_gain_two, grad_shift_five = narrow_sums[:4]
        grad_out_bias, grad_back_bias = narrow_sums[4:6]
        grad_ffn_gain, grad_in_bias, grad_ffn_shift = broad_sums[:3]

        grad_rows = [sent[0]] + [over_heads(sent[m], m) for m in range(1, TP)]
        set_rows = TP * rows
        place = jnp.stack([hg, qs, fs]).astype(jnp.int32)
        if fast:
            keep, send = weight_grads(
                tie(place, grad_rows[1]), inner_low, branch_low, normed_two_low, hidden_low, inner_two_low, cot
            )
            stage = first_stage(keep, send, moves)

        def backward_of(base, count, table):
            return attend_backward(
                base,
                count,
                table,
                bounds,
                queries,
                q_turned,
                kv_rows,
                k_turned,
                context_t,
                log_total,
                grad_rows,
            )

        def exchange(other):
            return [
                over_rows(other[:, (s - 1) * set_rows : s * set_rows], nq - s)
                for s in range(1, nq)
            ]

        table = tie(dealt, keep) if fast else dealt
        first_head = backward_of(0, 1, table)
        table = tie(dealt, first_head, stage[0]) if fast else dealt
        other_heads = backward_of(1, HPG - 1, table)
        cames = [exchange(first_head[2]), exchange(other_heads[2])]
        if fast:
            second = second_stage(stage, keep, other_heads, moves)
            cames = tie(cames, second[0])
        came = [cames[i][s] for s in range(nq - 1) for i in range(2)]
        dqs = [first_head[0], other_heads[0]]
        owns = [first_head[1], other_heads[1]]
        if fast:
            kept, sent_columns, first_send, first_keep, second_send, second_keep = columns(
                place, dqs, owns, came, w_own, norm_rows, narrow_sums, broad_sums, normed
            )
        else:
            *grads, sums, first_send, first_keep, second_send, second_keep = finish(
                dqs, owns, came, w_own
            )

        def plus(mine, came):
            return mine.astype(F32) + came.astype(F32)

        first_came = over_heads(first_send, 1)
        second_came = over_heads(second_send, 2)
        if fast:
            last, *second = second
            last = [over_heads(last[0], 2), over_heads(last[1], 1)]
            total, column_came = reduce_columns(kept, tie(sent_columns, last), fs, moves)
            first_keep, second_keep = tie((first_keep, second_keep), column_came)
        first_last = over_heads(plus(first_keep[1], first_came[1]).astype(BF16), 2)
        second_last = over_heads(plus(second_keep[1], second_came[1]).astype(BF16), 1)
        if fast:
            sides = (first_keep, first_came, first_last, second_keep, second_came, second_last)
            input_grad = outward(mine, norm_rows, grad_middle, sides)
        else:
            grad_normed = jnp.concatenate(
                [
                    plus(first_keep[0], first_came[0]) + first_last.astype(F32),
                    plus(second_keep[0], second_came[0]) + second_last.astype(F32),
                ],
                axis=0,
            )
            inputs = mine.astype(F32)
            first_pull = jax.vjp(layer_norm, inputs, gains[0], shift_rows[0])[1]
            grad_inputs_part, grad_gain_zero, grad_shift_zero = first_pull(grad_normed)
            input_grad = grad_middle + grad_inputs_part

        def absolute(row):
            blocks = row.reshape(TP, HC)
            return jnp.concatenate([pick(blocks, hg ^ m) for m in range(TP)])

        order = ctx * fsdp_size + fs
        total_devices = ctx_size * fsdp_size
        if fast:
            later = later_stages(last, *second, column_came, fs, moves)
            total = tie(total_of(total, *column_came), input_grad)
            came = [over_heads(pick(total, hg ^ m), m) for m in (1, 2, 3)]
            qkv_out, *small_out = settle(place, total, came)
            small_out = (small_out[0], small_out[1], small_out[2].reshape(-1), small_out[3])
            back_out, in_out, out_out = weight_outputs(*later, [qkv_out])
        else:

            def placed(row):
                blank = jnp.zeros((TP, HC), F32)
                return lax.dynamic_update_slice(blank, row[None], (hg, 0)).reshape(-1)

            row = sums[0]
            value_sums = row[:WIDE].reshape(HPG, 2, DH)[:, 1].reshape(-1)
            small_terms = jnp.concatenate(
                [
                    grad_gain_zero,
                    absolute(grad_gain_one),
                    grad_gain_two,
                    grad_shift_zero,
                    placed(row[WIDE:]),
                    placed(value_sums),
                    absolute(grad_shift_three),
                    grad_out_bias,
                    grad_shift_five,
                    grad_back_bias,
                    grad_ffn_gain,
                    grad_in_bias,
                    grad_ffn_shift,
                ]
            )
            axes = ("ctx", "fsdp")
            small_terms = lax.psum(small_terms, axes)
            narrow = small_terms[: 10 * D].reshape(10, total_devices, D // total_devices)
            narrow = pick(narrow, order, 1)
            broad = small_terms[10 * D :].reshape(3, total_devices, FF // total_devices)
            broad = pick(broad, order, 1)
            small_out = (narrow[:3], narrow[3:], broad[0], broad[1:])
            blocks = outer_sum(inner_low, branch_low).reshape(TP, HC, D)
            grad_out_w = jnp.concatenate([pick(blocks, hg ^ m) for m in range(TP)], axis=0)
            grad_in_w = outer_sum(normed_two_low, hidden_low)
            grad_back_w = outer_sum(inner_two_low, cot)
            back_out, in_out, out_out = (
                lax.psum_scatter(g.astype(BF16), axes, scatter_dimension=0, tiled=True).astype(F32)
                for g in (grad_back_w, grad_in_w, grad_out_w)
            )
            grad_qkv_w = outer_sum(jnp.concatenate(normed, axis=0), jnp.concatenate(grads, axis=0))
            pairs_w = grad_qkv_w[:, :WIDE].reshape(D, HPG, 2, DH)
            three = jnp.stack(
                [
                    grad_qkv_w[:, WIDE:],
                    pairs_w[:, :, 0].reshape(D, HC),
                    pairs_w[:, :, 1].reshape(D, HC),
                ],
                axis=1,
            )
            blank = jnp.zeros((D, 3, TP, HC), BF16)
            whole = lax.dynamic_update_slice(
                blank, three.astype(BF16)[:, :, None], (0, 0, hg, 0)
            ).reshape(D, 3 * D)
            qkv_out = lax.psum_scatter(whole, axes, scatter_dimension=0, tiled=True).astype(F32)
        return (
            mixed_out[None],
            input_grad[None],
            qkv_out,
            out_out,
            in_out,
            back_out,
        ) + small_out

    return local


def weight_piece(in_weight, back_weight, out_weight, c):
    cut = lax.dynamic_slice(in_weight, (0, c * 384), (192, 384))
    out_cut = lax.dynamic_slice(out_weight, (c // 2 * 48, c % 2 * 384), (48, 384))
    return jnp.concatenate(
        [
            jnp.concatenate([cut[:96], cut[96:]], axis=1),
            pick(back_weight.reshape(8, 96, D), c),
            jnp.concatenate([out_cut[:24], out_cut[24:]], axis=1),
        ],
        axis=0,
    )


def gather_pieces(piece, first, moves):
    over_heads, over_rows, over_fsdp, over_split = moves
    piece = tie(piece, *first)
    return [over_fsdp(piece, m) for m in (1, 2, 3)]


def gather_axis(foreign, before, moves):
    over_heads, over_rows, over_fsdp, over_split = moves
    foreign = jnp.stack(foreign)
    near = jnp.stack([foreign, over_rows(foreign, 1)])
    return near, over_split(tie(near, *before), (1, 2))


def gather_rest(near, axis, corner, first, then, moves):
    over_heads, over_rows, over_fsdp, over_split = moves
    axis, corner = tie((axis, jnp.stack(corner)), first, then)
    return near, axis, over_rows(axis, 1), corner, over_rows(corner, 1)


def weight_places(hg, qs, fs):
    near_x = jnp.where(qs == 0, 1, 2)
    far_x = 3 - near_x
    return jnp.stack(
        [fs ^ m for m in range(4)]
        + [fs ^ m ^ hg for m in range(4)]
        + [hg * 2 + qs, hg * 2 + 1 - qs]
        + [(hg ^ near_x) * 2 + qs, (hg ^ near_x) * 2 + 1 - qs]
        + [(hg ^ far_x) * 2 + 1 - qs, (hg ^ far_x) * 2 + qs]
        + [(hg ^ 3) * 2 + qs, (hg ^ 3) * 2 + 1 - qs]
    ).astype(jnp.int32)


def total_of(*parts):
    return functools.reduce(jnp.add, [p.astype(F32) for p in parts])


def first_stage(keep, send, moves):
    over_heads, over_rows, over_fsdp, over_split = moves
    came = over_rows(send, 1)
    return [total_of(keep[i, 2:], came[i, 2:]).astype(BF16) for i in range(2)], came


def second_stage(stage, keep, before, moves):
    over_heads, over_rows, over_fsdp, over_split = moves
    (first_send, second_send), came = stage
    arrived = [over_heads(first_send, 1), over_heads(second_send, 2)]
    keep, came = tie((keep, came), before)
    last = [total_of(keep[i, 1], came[i, 1], arrived[i][1]).astype(BF16) for i in range(2)]
    return last, keep, came, arrived


def later_stages(last, keep, came, arrived, before, fs, moves):
    over_heads, over_rows, over_fsdp, over_split = moves
    last = tie(last, before)
    whole = jnp.concatenate(
        [total_of(keep[i, 0], came[i, 0], arrived[i][0], last[i]).astype(BF16) for i in range(2)],
        axis=0,
    )
    back = whole[:384].reshape(4, 96, D)
    inner = whole[384:768].reshape(4, 4, 24, D)
    out = whole[768:].reshape(4, 24, D)

    def piece(f):
        return jnp.concatenate(
            [pick(back, f), pick(inner, f, 1).reshape(96, D), pick(out, f)], axis=0
        )

    return piece(fs), [over_fsdp(piece(fs ^ m), m) for m in (1, 2, 3)]


def weight_outputs(own, came, before):
    total = total_of(own, *tie(came, *before))
    inner = jnp.concatenate([total[96 + 24 * j : 120 + 24 * j] for j in range(4)], axis=1)
    return total[:96], inner, total[192:216]


def reduce_columns(keep, send, fs, moves):
    over_heads, over_rows, over_fsdp, over_split = moves
    kept = keep + over_rows(send, 1)
    kept = kept.reshape(TP, 4, 24, 640)
    low = kept.astype(BF16)
    return pick(kept, fs, 1), [over_fsdp(pick(low, fs ^ m, 1), m) for m in (1, 2, 3)]


def solution(mesh):
    ctx_size = mesh.shape["ctx"]
    fsdp_size = mesh.shape["fsdp"]
    in_specs = (
        P("fsdp", "ctx", None),
        P("fsdp", "ctx", None),
        P("fsdp", None),
        P("fsdp", None),
        P("fsdp", None),
        P("fsdp", None),
        P("fsdp", None),
        P("fsdp", None),
        P(None, "fsdp"),
        P(None, "fsdp"),
        P("fsdp"),
        P(None, "fsdp"),
    )
    out_specs = (
        P("fsdp", "ctx", None),
        P("fsdp", "ctx", None),
        P(("ctx", "fsdp"), None),
        P(("ctx", "fsdp"), None),
        P(("ctx", "fsdp"), None),
        P(("ctx", "fsdp"), None),
        P(None, ("ctx", "fsdp")),
        P(None, ("ctx", "fsdp")),
        P(("ctx", "fsdp")),
        P(None, ("ctx", "fsdp")),
    )
    return jax.shard_map(
        make_local(ctx_size, fsdp_size),
        mesh=mesh,
        in_specs=in_specs,
        out_specs=out_specs,
        check_vma=False,
    )
```
